32 devices in a mesh: batch: 8 (over y, x, core), tensor: 4 (over z).
Axes of the slice: x: 2, y: 2, z: 4, core: 2. Of those that a mesh axis runs over, the one named last changes fastest.
Arguments:
- tokens: bfloat16 [65536, 1024], P('batch'), may hold values from -6 to 6
- lengths: int32 [32], P('batch'), may hold values from 256 to 2048, as said below
- routes: int32 [32, 256], P('batch'), may hold values from 0 to 2047, as said below
- w_query: float32 [1024, 1024], P('batch', 'tensor'), may hold values from -0.1875 to 0.1875
- w_key: float32 [1024, 1024], P('batch', 'tensor'), may hold values from -0.1875 to 0.1875
- w_value: float32 [1024, 1024], P('batch', 'tensor'), may hold values from -0.1875 to 0.1875
- w_out: float32 [1024, 1024], P('tensor', 'batch'), may hold values from -0.75 to 0.75
- w_up: float32 [1024, 4096], P('batch', 'tensor'), may hold values from -0.1875 to 0.1875
- w_down: float32 [4096, 1024], P('tensor', 'batch'), may hold values from -0.125 to 0.125
- gain_attn: float32 [1024], P('batch'), may hold values from 0.1 to 1.9
- gain_mlp: float32 [1024], P('batch'), may hold values from 0.1 to 1.9
- w_router: float32 [1024], P('batch'), may hold values from -0.1875 to 0.1875
- cotangent: bfloat16 [65536, 1024], P('batch'), may hold values from -6 to 6
Outputs:
- output: bfloat16 [65536, 1024], P('batch')
- grad_tokens: bfloat16 [65536, 1024], P('batch')
- grad_query: float32 [1024, 1024], P('batch', 'tensor')
- grad_key: float32 [1024, 1024], P('batch', 'tensor')
- grad_value: float32 [1024, 1024], P('batch', 'tensor')
- grad_out: float32 [1024, 1024], P('tensor', 'batch')
- grad_up: float32 [1024, 4096], P('batch', 'tensor')
- grad_down: float32 [4096, 1024], P('tensor', 'batch')
- grad_gain_attn: float32 [1024], P('batch')
- grad_gain_mlp: float32 [1024], P('batch')
- grad_router: float32 [1024], P('batch')
The draws below stay inside these ranges and needn't reach their ends.
Inputs may be any that keep to these rules, and one draw needn't show every extreme that they name: `lengths`: one sequence has exactly 2048 positions and one exactly 256. `routes`: for a sequence of length L, its first L // 8 entries are distinct positions below L in increasing order, L - 1 among them; its other entries are 0.
All inputs are finite; a program needn't handle non-finite values.
Results may differ from the reference program's by a relative error of at most 0.019.
Values may be sent and summed in bfloat16 or wider, within the bound.
No kernel may reach another device: no remote copies, remote signals or barrier semaphores. Data moves between devices by JAX's collectives and lax.ppermute only.
A program may use at most 320 MiB of HBM per device.

```python
import jax
import jax.numpy as jnp
from jax import lax

D = 1024
HEADS = 16
HEAD_DIM = 64
FF = 4096
SLOTS = 2048
SEQS = 32
CAP = 256
TOKENS = 65536


def routing_pair(key):
    base = jax.random.fold_in(key, 11)
    key_len, key_pick, key_score = jax.random.split(base, 3)
    lens = jax.random.randint(key_len, (SEQS,), SLOTS // 8, SLOTS + 1)
    chosen_seq = jax.random.permutation(key_pick, SEQS)
    seq_index = jnp.arange(SEQS)
    lens = jnp.where(seq_index == chosen_seq[0], SLOTS, lens)
    lens = jnp.where(seq_index == chosen_seq[1], SLOTS // 8, lens)
    slot_index = jnp.arange(SLOTS)[None, :]
    ranking = jax.random.randint(key_score, (SEQS, SLOTS), 0, 2 ** 19) * SLOTS + slot_index
    ranking = jnp.where(slot_index < lens[:, None], ranking, -1)
    ranking = jnp.where(slot_index == lens[:, None] - 1, 2 ** 30 + SLOTS, ranking)
    picked = lax.top_k(ranking, CAP)[1]
    routed_count = lens // 8
    column = jnp.arange(CAP)[None, :]
    picked = jnp.where(column < routed_count[:, None], picked, SLOTS)
    picked = jnp.sort(picked, axis=1)
    picked = jnp.where(picked == SLOTS, 0, picked)
    return (lens.astype(jnp.int32), picked.astype(jnp.int32))


def draw_lengths(key, part):
    return routing_pair(key)[0]


def draw_routes(key, part):
    return routing_pair(key)[1]


def block_levels(own_key, shape, cuts, least, top_value):
    def one(axis_at, blocks):
        heights = jax.random.uniform(jax.random.fold_in(jax.random.fold_in(own_key, 6), axis_at), (blocks,), jnp.float32, least / len(cuts), top_value / len(cuts))
        return jnp.repeat(jnp.exp(heights), shape[axis_at] // blocks).reshape((-1,) + (1,) * (len(shape) - axis_at - 1))

    loudness = one(*cuts[0])
    for cut in cuts[1:]:
        loudness = loudness * one(*cut)
    return loudness


def gaussian(rng, extent, width, most, cuts=(), kind=jnp.bfloat16):
    gain = block_levels(rng, extent, cuts, -0.22, 0.18) if cuts else 1.0
    drawn = jax.random.normal(rng, extent, jnp.float32) * width * gain
    return jnp.minimum(jnp.maximum(drawn, -most), most).astype(kind)


def setup_inputs(seed: int = 0) -> dict:
    keys = jax.random.split(jax.random.key(seed), 14)
    return {
        "tokens": gaussian(keys[0], (TOKENS, D), 1.0, 6.0, ((0, 8),)),
        "lengths": draw_lengths(jax.random.fold_in(keys[13], 71), 0),
        "routes": draw_routes(jax.random.fold_in(keys[13], 71), 0),
        "w_query": gaussian(keys[3], (D, D), D ** -0.5, 0.1875, ((0, 8), (1, 4)), jnp.float32),
        "w_key": gaussian(keys[4], (D, D), D ** -0.5, 0.1875, ((0, 8), (1, 4)), jnp.float32),
        "w_value": gaussian(keys[5], (D, D), D ** -0.5, 0.1875, ((0, 8), (1, 4)), jnp.float32),
        "w_out": gaussian(keys[6], (D, D), (D // 16) ** -0.5, 0.75, ((0, 4), (1, 8)), jnp.float32),
        "w_up": gaussian(keys[7], (D, FF), D ** -0.5, 0.1875, ((0, 8), (1, 4)), jnp.float32),
        "w_down": gaussian(keys[8], (FF, D), (FF // 2) ** -0.5, 0.125, ((0, 4), (1, 8)), jnp.float32),
        "gain_attn": jnp.clip(1.0 + 0.18 * jax.random.normal(keys[9], (D,), jnp.float32), 0.1, 1.9),
        "gain_mlp": jnp.clip(1.0 + 0.18 * jax.random.normal(keys[10], (D,), jnp.float32), 0.1, 1.9),
        "w_router": gaussian(keys[11], (D,), D ** -0.5, 0.1875, ((0, 8),), jnp.float32),
        "cotangent": gaussian(keys[12], (TOKENS, D), 1.0, 6.0, ((0, 8),)),
    }


EPSILON = 1e-06
highest = lax.Precision.HIGHEST

@jax.custom_vjp
def low(v):
    return lax.optimization_barrier(v.astype(jnp.bfloat16)).astype(jnp.float32)

@jax.custom_vjp
def low_back(v):
    return v

def low_keep(v):
    return (low(v), None)

def low_pass(kept, grad):
    return (grad,)

def back_keep(v):
    return (v, None)

def back_low(kept, grad):
    return (low(grad),)
low.defvjp(low_keep, low_pass)
low_back.defvjp(back_keep, back_low)

def gelu_tanh(values):
    return 0.5 * values * (1.0 + jnp.tanh(0.7978845608028654 * (values + 0.044715 * values * values * values)))

def rms_scale(values):
    return values * lax.rsqrt(lax.optimization_barrier(jnp.mean(values * values, axis=-1, keepdims=True)) + EPSILON)

def one_sequence(weights, seq_tokens, seq_routes, seq_length):
    low_query, low_key, low_value, low_out, low_up, low_down, gain_one, gain_two, low_router = weights
    scale_qk = HEAD_DIM ** (-0.5)
    routed = low_back(jnp.take(seq_tokens, seq_routes, axis=0))
    position = jnp.arange(CAP)
    live_count = seq_length // 8
    is_live = position < live_count
    router_score = jnp.dot(routed, low_router, precision=highest)
    gate_prob = 1.0 / (1.0 + jnp.exp(-router_score))
    attn_in = low(rms_scale(routed) * gain_one)
    queries = low_back(low(jnp.dot(attn_in, low_query, precision=highest))).reshape(CAP, HEADS, HEAD_DIM)
    keys_all = low_back(low(jnp.dot(attn_in, low_key, precision=highest))).reshape(CAP, HEADS, HEAD_DIM)
    vals_all = low_back(low(jnp.dot(attn_in, low_value, precision=highest))).reshape(CAP, HEADS, HEAD_DIM)
    raw_scores = low_back(jnp.einsum('qhd,khd->hqk', queries, keys_all, precision=highest) * scale_qk)
    allowed = (position[None, :] <= position[:, None]) & (position[None, :] < live_count)
    masked = jnp.where(allowed[None], raw_scores, -1e+30)
    row_max = lax.optimization_barrier(jnp.max(masked, axis=-1, keepdims=True))
    exp_scores = jnp.exp(masked - row_max)
    attn_probs = low(exp_scores / lax.optimization_barrier(jnp.sum(exp_scores, axis=-1, keepdims=True)))
    heads_out = low(low_back(jnp.einsum('hqk,khd->qhd', attn_probs, vals_all, precision=highest))).reshape(CAP, D)
    attn_out = low_back(jnp.dot(heads_out, low_out, precision=highest))
    middle = routed + attn_out
    mlp_in = low(rms_scale(middle) * gain_two)
    hidden_pre = low_back(jnp.dot(mlp_in, low_up, precision=highest))
    hidden = low(gelu_tanh(hidden_pre))
    mlp_out = low_back(jnp.dot(hidden, low_down, precision=highest))
    gate_live = jnp.where(is_live, gate_prob, jnp.zeros_like(gate_prob))
    update = low(gate_live[:, None] * (attn_out + mlp_out))
    return seq_tokens + jnp.zeros_like(seq_tokens).at[seq_routes].add(update)

def reference(tokens, lengths, routes, w_query, w_key, w_value, w_out, w_up, w_down, gain_attn, gain_mlp, w_router, cotangent):
    step_fn = jax.checkpoint(one_sequence)

    def forward(tokens_f, wq_master, wk_master, wv_master, wo_master, wu_master, wd_master, ga_master, gm_master, wr_master):
        lowered = (low(wq_master), low(wk_master), low(wv_master), low(wo_master), low(wu_master), low(wd_master), low(ga_master), low(gm_master), low(wr_master))

        def scan_body(state_in, inputs):
            seq_tokens, seq_routes, seq_length = inputs
            return (state_in, step_fn(lowered, seq_tokens, seq_routes, seq_length))
        _, outputs = lax.scan(scan_body, jnp.zeros((), jnp.float32), (tokens_f.reshape(SEQS, SLOTS, D), routes, lengths))
        return outputs.reshape(SEQS * SLOTS, D)
    tokens_f = tokens.astype(jnp.float32)
    result, pullback = jax.vjp(forward, tokens_f, w_query, w_key, w_value, w_out, w_up, w_down, gain_attn, gain_mlp, w_router)
    grads = pullback(cotangent.astype(jnp.float32))
    return (result.astype(jnp.bfloat16), grads[0].astype(jnp.bfloat16), grads[1], grads[2], grads[3], grads[4], grads[5], grads[6], grads[7], grads[8], grads[9])
```

```python
import functools

import jax
import jax.numpy as jnp
from jax import lax
from jax.experimental import pallas as pl
from jax.experimental.pallas import tpu as pltpu
from jax.sharding import PartitionSpec as P

HEAD_DIM = 64
SLOT_BLOCK = 512
EPSILON = 1e-06


def gelu_tanh(values):
    return (
        0.5
        * values
        * (1.0 + jnp.tanh(0.7978845608028654 * (values + 0.044715 * values * values * values)))
    )


def product(left, right):
    return jnp.dot(left, right, preferred_element_type=jnp.float32)


def contract_rows(left, right):
    return lax.dot_general(
        left, right, (((0,), (0,)), ((), ())), preferred_element_type=jnp.float32
    )


def times_transposed(left, right):
    return lax.dot_general(
        left, right, (((1,), (1,)), ((), ())), preferred_element_type=jnp.float32
    )


def norm_backward(d_normed_in, normed, inverse, gain_vec):
    d_scaled = d_normed_in * gain_vec
    d_input = inverse * (d_scaled - normed * jnp.mean(d_scaled * normed, axis=-1, keepdims=True))
    return (d_input, jnp.sum(d_normed_in * normed, axis=0))


def norm_forward(values):
    inverse = lax.rsqrt(jnp.mean(values * values, axis=-1, keepdims=True) + EPSILON)
    return (values * inverse, inverse)


def pick_kernel(order_ref, routes_ref, tokens_ref, cot_ref, routed_ref, cot_routed_ref):
    block = pl.program_id(1)
    capacity = routes_ref.shape[1]
    slots = tokens_ref.shape[1]
    column = lax.broadcasted_iota(jnp.int32, (capacity, slots), 1) + block * slots
    chooser = (routes_ref[0] == column).astype(jnp.bfloat16)
    part = product(chooser, tokens_ref[0])
    cot_part = product(chooser, cot_ref[0])

    @pl.when(block == 0)
    def _():
        routed_ref[0] = part
        cot_routed_ref[0] = cot_part

    @pl.when(block > 0)
    def _():
        routed_ref[0] += part
        cot_routed_ref[0] += cot_part


def pick_rows(tokens, cotangent, routes, order, count):
    seq_count, slots, features = tokens.shape
    capacity = routes.shape[1]
    per_block = min(SLOT_BLOCK, slots)
    table = pl.BlockSpec((1, per_block, features), lambda i, j, order: (order[i], j, 0))
    picked = pl.BlockSpec((1, capacity, features), lambda i, j, order: (i, 0, 0))
    shape = jax.ShapeDtypeStruct((count, capacity, features), jnp.float32)
    return pl.pallas_call(
        pick_kernel,
        out_shape=(shape, shape),
        grid_spec=pltpu.PrefetchScalarGridSpec(
            num_scalar_prefetch=1,
            grid=(count, slots // per_block),
            in_specs=[
                pl.BlockSpec((1, capacity, 1), lambda i, j, order: (order[i], 0, 0)),
                table,
                table,
            ],
            out_specs=[picked, picked],
        ),
        compiler_params=pltpu.CompilerParams(vmem_limit_bytes=32 << 20),
        name="pick_rows",
    )(order, routes[:, :, None], tokens, cotangent)


def place_kernel(order_ref, routes_ref, table_ref, values_ref, out_ref):
    block = pl.program_id(1)
    slots = table_ref.shape[1]
    capacity = routes_ref.shape[2]
    row = lax.broadcasted_iota(jnp.int32, (slots, capacity), 0) + block * slots
    chooser = (routes_ref[0] == row).astype(jnp.bfloat16)
    placed = product(chooser, values_ref[0])
    out_ref[0] = (table_ref[0].astype(jnp.float32) + placed).astype(jnp.bfloat16)


def place_rows(table, values, routes, order):
    seq_count, slots, features = table.shape
    capacity = routes.shape[1]
    per_block = min(SLOT_BLOCK, slots)
    tall = pl.BlockSpec((1, per_block, features), lambda i, j, order: (order[i], j, 0))
    return pl.pallas_call(
        place_kernel,
        out_shape=jax.ShapeDtypeStruct(table.shape, table.dtype),
        grid_spec=pltpu.PrefetchScalarGridSpec(
            num_scalar_prefetch=1,
            grid=(seq_count, slots // per_block),
            in_specs=[
                pl.BlockSpec((1, 1, capacity), lambda i, j, order: (order[i], 0, 0)),
                tall,
                pl.BlockSpec((1, capacity, features), lambda i, j, order: (i, 0, 0)),
            ],
            out_specs=tall,
        ),
        compiler_params=pltpu.CompilerParams(vmem_limit_bytes=32 << 20),
        name="place_rows",
    )(order, routes[:, None, :], table, values)


def causal_allowed(live_count, capacity):
    position = jnp.arange(capacity)
    allowed = position[None, :] <= position[:, None]
    allowed = allowed[None, None] & (
        position[None, None, None, :] < live_count[:, None, None, None]
    )
    return allowed


def attend_forward(queries, keys_all, vals_all, live_count, scale_qk):
    raw_scores = (
        jnp.einsum("sqhd,skhd->shqk", queries, keys_all, preferred_element_type=jnp.float32)
        * scale_qk
    )
    masked = jnp.where(causal_allowed(live_count, queries.shape[1]), raw_scores, -1e30)
    row_max = jnp.max(masked, axis=-1, keepdims=True)
    exp_scores = jnp.exp(masked - row_max)
    row_total = jnp.sum(exp_scores, axis=-1, keepdims=True)
    attn_probs = (exp_scores / row_total).astype(jnp.bfloat16)
    log_total = row_max + jnp.log(row_total)
    heads_out = jnp.einsum(
        "shqk,skhd->sqhd", attn_probs, vals_all, preferred_element_type=jnp.float32
    )
    return (heads_out.astype(jnp.bfloat16), log_total)


def attend_backward(queries, keys_all, vals_all, d_heads, log_total, live_count, scale_qk):
    raw_scores = (
        jnp.einsum("sqhd,skhd->shqk", queries, keys_all, preferred_element_type=jnp.float32)
        * scale_qk
    )
    masked = jnp.where(causal_allowed(live_count, queries.shape[1]), raw_scores, -1e30)
    attn_probs = jnp.exp(masked - log_total)
    d_vals = jnp.einsum(
        "shqk,sqhd->skhd",
        attn_probs.astype(jnp.bfloat16),
        d_heads,
        preferred_element_type=jnp.float32,
    ).astype(jnp.bfloat16)
    d_probs = jnp.einsum("sqhd,skhd->shqk", d_heads, vals_all, preferred_element_type=jnp.float32)
    d_scores = (
        attn_probs * (d_probs - jnp.sum(d_probs * attn_probs, axis=-1, keepdims=True))
    ).astype(jnp.bfloat16)
    d_queries = (
        jnp.einsum("shqk,skhd->sqhd", d_scores, keys_all, preferred_element_type=jnp.float32)
        * scale_qk
    ).astype(jnp.bfloat16)
    d_keys = (
        jnp.einsum("shqk,sqhd->skhd", d_scores, queries, preferred_element_type=jnp.float32)
        * scale_qk
    ).astype(jnp.bfloat16)
    return (d_queries, d_keys, d_vals)


class Exchange:
    def __init__(self, mesh):
        self.batch = mesh.shape["batch"]
        self.tensor = mesh.shape["tensor"]
        bits = []
        bit = self.batch // 2
        while bit:
            bits.append(bit)
            bit //= 2
        self.core = bits[-1]
        self.chips = bits[:-1]

    def swap(self, array, bit):
        return lax.ppermute(array, "batch", [(i, i ^ bit) for i in range(self.batch)])

    def shift(self, array, step):
        size = self.tensor
        return lax.ppermute(array, "tensor", [(i, (i + step) % size) for i in range(size)])

    def block_order(self):
        order = [0]
        for bit in reversed([self.core] + self.chips):
            order = order + [place ^ bit for place in order]
        return order

    def gather_rows(self, array, flip):
        rows, width = array.shape
        places = len(self.chips)
        total = array.reshape((1,) * places + array.shape)
        sequence = range(places)
        for place in sequence if flip else reversed(sequence):
            other = self.swap(total, self.chips[place])
            total = jnp.concatenate([total, other], axis=place)
        half = total.reshape(rows * self.batch // 2, width)
        return half, self.swap(half, self.core)

    def gather_tensor(self, array):
        pieces = [array]
        for _ in range(self.tensor - 1):
            pieces.append(self.shift(pieces[-1], 1))
        return pieces

    def scatter_rows(self, kept, sent, flip):
        places = len(self.chips)
        total = add_rounded(kept, self.swap(sent, self.core))
        rows = total.shape[0] // (self.batch // 2)
        total = total.reshape((2,) * places + (rows, total.shape[1]))
        sequence = range(places)
        for place in reversed(sequence) if flip else sequence:
            own = lax.slice_in_dim(total, 0, 1, axis=place)
            other = lax.slice_in_dim(total, 1, 2, axis=place)
            total = add_rounded(own, self.swap(other, self.chips[place]))
        return total.reshape(rows, total.shape[-1])

    def scatter_tensor(self, pieces):
        total = pieces[-1]
        for piece in reversed(pieces[:-1]):
            total = add_rounded(piece, self.shift(total, -1))
        return total


def add_rounded(left, right):
    return (left.astype(jnp.float32) + right.astype(jnp.float32)).astype(jnp.bfloat16)


def swap_blocks(values, device, bits, blocks):
    shape = values.shape
    spread = values.reshape(shape[:-1] + (2,) * len(bits) + (shape[-1] // blocks,))
    first = len(shape) - 1
    for place, bit in enumerate(bits):
        spread = jnp.where((device & bit) != 0, jnp.flip(spread, axis=first + place), spread)
    return spread.reshape(shape)


def shards(
    mesh,
    tokens,
    lengths,
    routes,
    w_query,
    w_key,
    w_value,
    w_out,
    w_up,
    w_down,
    gain_attn,
    gain_mlp,
    w_router,
    cotangent,
):
    low = jnp.bfloat16
    moves = Exchange(mesh)
    device = lax.axis_index("batch")
    column = lax.axis_index("tensor")
    seq_count, capacity = routes.shape
    feature_count = tokens.shape[1]
    slot_count = tokens.shape[0] // seq_count
    tokens = tokens.reshape(seq_count, slot_count, feature_count)
    cotangent = cotangent.reshape(seq_count, slot_count, feature_count)
    bits = moves.chips + [moves.core]
    ways = len(bits)

    repeats = max(1, moves.tensor // seq_count)
    local_count = max(1, seq_count // moves.tensor)
    first = column // repeats if repeats > 1 else column * local_count
    order = (first + jnp.arange(local_count)).astype(jnp.int32)
    counts_once = (column % repeats) == 0

    def once(values):
        return jnp.where(counts_once, values, 0.0) if repeats > 1 else values

    def relative(values):
        swapped = swap_blocks(values, device, bits, moves.batch)
        shape = values.shape
        spread = swapped.reshape(shape[:-1] + (2,) * ways + (shape[-1] // moves.batch,))
        lead = len(shape) - 1
        axes = tuple(range(lead)) + (lead + ways - 1,) + tuple(range(lead, lead + ways - 1))
        return spread.transpose(axes + (lead + ways,)).reshape(shape)

    def absolute(values):
        shape = values.shape
        spread = values.reshape(shape[:-1] + (2,) * ways + (shape[-1] // moves.batch,))
        lead = len(shape) - 1
        axes = tuple(range(lead)) + tuple(range(lead + 1, lead + ways)) + (lead,)
        spread = spread.transpose(axes + (lead + ways,)).reshape(shape)
        return swap_blocks(spread, device, bits, moves.batch)

    wide = w_query.shape[1]
    wide_up = w_up.shape[1] // 2

    def fetch(parts, flip):
        pieces = moves.gather_tensor(jnp.concatenate([p.astype(low) for p in parts], axis=1))
        width = parts[0].shape[1]
        ordered = [
            piece[:, i * width : (i + 1) * width] for i in range(len(parts)) for piece in pieces
        ]
        return moves.gather_rows(jnp.concatenate(ordered, axis=1), flip)

    down_turned = w_down.astype(low).T
    query_key = fetch((w_query, w_key), False)
    value_out = fetch((w_value, w_out.astype(low).T), True)
    up_one = fetch((w_up[:, :wide_up],), False)
    up_two = fetch((w_up[:, wide_up:],), True)
    down_one = fetch((down_turned[:, :wide_up],), False)
    down_two = fetch((down_turned[:, wide_up:],), True)
    small = jnp.concatenate([gain_attn, gain_mlp, w_router]).astype(low)
    small = lax.all_gather(small, "batch", axis=0)
    small = small.reshape(moves.batch, 3, -1).transpose(1, 0, 2).reshape(3, feature_count)
    small = relative(small.astype(jnp.float32))
    gain_one, gain_two, router_vec = small[0], small[1], small[2]

    half = feature_count // 2
    heads_wide = wide * moves.tensor

    def forward_product(left, pair):
        return product(left[:, :half], pair[0]) + product(left[:, half:], pair[1])

    def backward_product(lefts, pairs):
        halves = []
        for side in range(2):
            total = times_transposed(lefts[0], pairs[0][side])
            for left, pair in zip(lefts[1:], pairs[1:]):
                total = total + times_transposed(left, pair[side])
            halves.append(total)
        return jnp.concatenate(halves, axis=1)

    routed, cot_routed = pick_rows(tokens, cotangent, routes, order, local_count)
    rows_total = local_count * capacity
    routed = relative(routed.reshape(rows_total, feature_count))
    cot_routed = relative(cot_routed.reshape(rows_total, feature_count))
    live_count = lax.dynamic_slice_in_dim(lengths, first, local_count) // 8
    position = jnp.arange(capacity)
    is_live = (position[None, :] < live_count[:, None]).reshape(rows_total)
    router_score = jnp.sum(routed * router_vec, axis=-1)
    gate_prob = 1.0 / (1.0 + jnp.exp(-router_score))
    gate_live = jnp.where(is_live, gate_prob, 0.0)
    scale_qk = HEAD_DIM ** (-0.5)
    head_shape = (local_count, capacity, heads_wide // HEAD_DIM, HEAD_DIM)
    value_pair = tuple(side[:, :heads_wide] for side in value_out)
    out_pair = tuple(side[:, heads_wide:] for side in value_out)

    normed_one, inverse_one = norm_forward(routed)
    attn_in = (normed_one * gain_one).astype(low)
    both = forward_product(attn_in, query_key).astype(low)
    queries = both[:, :heads_wide].reshape(head_shape)
    keys_all = both[:, heads_wide:].reshape(head_shape)
    vals_all = forward_product(attn_in, value_pair).astype(low).reshape(head_shape)
    heads_four, log_total = attend_forward(queries, keys_all, vals_all, live_count, scale_qk)
    heads_out = heads_four.reshape(rows_total, heads_wide)
    attn_out = backward_product([heads_out], [out_pair])
    middle = routed + attn_out
    normed_two, inverse_two = norm_forward(middle)
    mlp_in = (normed_two * gain_two).astype(low)
    ups = (up_one, up_two)
    downs = (down_one, down_two)
    pre = [forward_product(mlp_in, pair) for pair in ups]
    hidden = [gelu_tanh(values).astype(low) for values in pre]
    mlp_out = backward_product(hidden, downs)
    branch = attn_out + mlp_out
    update = (gate_live[:, None] * branch).astype(low)
    d_branch = gate_live[:, None] * cot_routed
    d_mlp_out = d_branch.astype(low)
    d_score = gate_live * (1.0 - gate_prob) * jnp.sum(cot_routed * branch, axis=-1)

    def spread_out(rows, table):
        pieces = moves.gather_tensor(absolute(rows))
        kept = pieces[::repeats] if repeats > 1 else pieces
        values = jnp.concatenate(
            [piece.reshape(local_count, capacity, feature_count) for piece in kept], axis=0
        )
        steps = jnp.arange(0, moves.tensor, repeats)
        owners = ((column - steps) % moves.tensor).astype(jnp.int32)
        if repeats > 1:
            places = owners // repeats
        else:
            places = (owners[:, None] * local_count + jnp.arange(local_count)).reshape(-1)
        return place_rows(table, values, routes, places.astype(jnp.int32)).reshape(
            -1, feature_count
        )

    output = spread_out(update, tokens)

    def reduce(grad_of, parts, flip):
        kept = once(grad_of(0, half)).astype(low)
        sent = once(grad_of(half, feature_count)).astype(low)
        total = moves.scatter_rows(kept, sent, flip)
        width = total.shape[1] // parts // moves.tensor
        pieces = [
            jnp.concatenate(
                [
                    total[:, (i * moves.tensor + k) * width : (i * moves.tensor + k + 1) * width]
                    for i in range(parts)
                ],
                axis=1,
            )
            for k in range(moves.tensor)
        ]
        return moves.scatter_tensor(pieces)

    def reduce_product(left, right, parts, flip):
        return reduce(lambda a, b: contract_rows(left[:, a:b], right), parts, flip)

    grad_down = [
        reduce_product(d_mlp_out, values, 1, flip) for values, flip in zip(hidden, (False, True))
    ]
    d_hidden = [forward_product(d_mlp_out, pair) for pair in downs]
    d_pre = [
        jax.vjp(gelu_tanh, values)[1](grad)[0].astype(low) for values, grad in zip(pre, d_hidden)
    ]
    grad_up = [
        reduce_product(mlp_in, values, 1, flip) for values, flip in zip(d_pre, (False, True))
    ]
    d_mlp_in = backward_product(d_pre, ups)
    d_middle, grad_gain_mlp = norm_backward(d_mlp_in, normed_two, inverse_two, gain_two)
    d_attn_out = (d_middle + d_branch).astype(low)
    d_heads = forward_product(d_attn_out, out_pair).astype(low).reshape(head_shape)
    d_queries, d_keys, d_vals = attend_backward(
        queries, keys_all, vals_all, d_heads, log_total, live_count, scale_qk
    )
    flat_shape = (rows_total, heads_wide)
    d_both = jnp.concatenate([d_queries.reshape(flat_shape), d_keys.reshape(flat_shape)], axis=1)
    d_vals = d_vals.reshape(flat_shape)
    grad_query_key = reduce_product(attn_in, d_both, 2, False)
    grad_value_out = reduce(
        lambda a, b: jnp.concatenate(
            [
                contract_rows(attn_in[:, a:b], d_vals),
                contract_rows(d_attn_out[:, a:b], heads_out),
            ],
            axis=1,
        ),
        2,
        True,
    )
    d_attn_in = backward_product([d_both, d_vals], [query_key, value_pair])
    d_from_norm, grad_gain_attn = norm_backward(d_attn_in, normed_one, inverse_one, gain_one)
    grad_router = jnp.sum(routed * d_score[:, None], axis=0)
    d_routed = (d_middle + d_from_norm + d_score[:, None] * router_vec).astype(low)
    grad_tokens = spread_out(d_routed, cotangent)

    small_grads = absolute(jnp.stack([grad_gain_attn, grad_gain_mlp, grad_router]))
    small_grads = lax.psum(once(small_grads), ("batch", "tensor"))
    own = feature_count // moves.batch
    small_grads = lax.dynamic_slice_in_dim(small_grads, device * own, own, axis=1)

    full = jnp.float32
    return (
        output,
        grad_tokens,
        grad_query_key[:, :wide].astype(full),
        grad_query_key[:, wide:].astype(full),
        grad_value_out[:, :wide].astype(full),
        grad_value_out[:, wide:].T.astype(full),
        jnp.concatenate(grad_up, axis=1).astype(full),
        jnp.concatenate(grad_down, axis=1).T.astype(full),
        small_grads[0],
        small_grads[1],
        small_grads[2],
    )


def solution(mesh):
    in_specs = (
        P("batch", None),
        P("batch"),
        P("batch", None),
        P("batch", "tensor"),
        P("batch", "tensor"),
        P("batch", "tensor"),
        P("tensor", "batch"),
        P("batch", "tensor"),
        P("tensor", "batch"),
        P("batch"),
        P("batch"),
        P("batch"),
        P("batch", None),
    )
    out_specs = (
        P("batch", None),
        P("batch", None),
        P("batch", "tensor"),
        P("batch", "tensor"),
        P("batch", "tensor"),
        P("tensor", "batch"),
        P("batch", "tensor"),
        P("tensor", "batch"),
        P("batch"),
        P("batch"),
        P("batch"),
    )
    return jax.shard_map(
        functools.partial(shards, mesh),
        mesh=mesh,
        in_specs=in_specs,
        out_specs=out_specs,
        check_vma=False,
    )
```

```python
import functools

import jax
import jax.numpy as jnp
from jax import lax
from jax.experimental import pallas as pl
from jax.experimental.pallas import tpu as pltpu
from jax.sharding import PartitionSpec as P

HEAD_DIM = 64
SLOT_BLOCK = 512
EPSILON = 1e-06


CURVE = 0.7978845608028654
CUBIC = 0.044715


def gelu_tanh(values):
    return 0.5 * values * (1.0 + jnp.tanh(CURVE * (values + CUBIC * values * values * values)))


def gelu_slope(values):
    square = values * values
    bend = jnp.tanh(CURVE * (values + CUBIC * values * square))
    inner = CURVE * (1.0 + 3.0 * CUBIC * square)
    return 0.5 * (1.0 + bend) + 0.5 * values * (1.0 - bend * bend) * inner


def product(left, right):
    return jnp.dot(left, right, preferred_element_type=jnp.float32)


def contract_rows(left, right):
    return lax.dot_general(
        left, right, (((0,), (0,)), ((), ())), preferred_element_type=jnp.float32
    )


def times_transposed(left, right):
    return lax.dot_general(
        left, right, (((1,), (1,)), ((), ())), preferred_element_type=jnp.float32
    )


def norm_backward(d_normed_in, normed, inverse, gain_vec):
    d_scaled = d_normed_in * gain_vec
    d_input = inverse * (d_scaled - normed * jnp.mean(d_scaled * normed, axis=-1, keepdims=True))
    return (d_input, jnp.sum(d_normed_in * normed, axis=0, keepdims=True))


def norm_forward(values):
    inverse = lax.rsqrt(jnp.mean(values * values, axis=-1, keepdims=True) + EPSILON)
    return (values * inverse, inverse)


LOW = jnp.bfloat16
FULL = jnp.float32


def pick_kernel(order_ref, routes_ref, turn_ref, tokens_ref, cot_ref, routed_ref, cot_routed_ref, total, cot_total):
    block = pl.program_id(1)
    capacity = routes_ref.shape[1]
    slots = tokens_ref.shape[1]
    column = lax.broadcasted_iota(jnp.int32, (capacity, slots), 1) + block * slots
    chooser = (routes_ref[0] == column).astype(LOW)
    part = product(chooser, tokens_ref[0])
    cot_part = product(chooser, cot_ref[0])

    @pl.when(block == 0)
    def _():
        total[...] = part
        cot_total[...] = cot_part

    @pl.when(block > 0)
    def _():
        total[...] += part
        cot_total[...] += cot_part

    @pl.when(block == pl.num_programs(1) - 1)
    def _():
        routed_ref[0] = product(total[...].astype(LOW), turn_ref[...]).astype(LOW)
        cot_routed_ref[0] = product(cot_total[...].astype(LOW), turn_ref[...]).astype(LOW)


def pick_rows(tokens, cotangent, routes, order, count, turn):
    seq_count, slots, features = tokens.shape
    capacity = routes.shape[1]
    per_block = min(SLOT_BLOCK, slots)
    table = pl.BlockSpec((1, per_block, features), lambda i, j, order: (order[i], j, 0))
    picked = pl.BlockSpec((1, capacity, features), lambda i, j, order: (i, 0, 0))
    shape = jax.ShapeDtypeStruct((count, capacity, features), LOW)
    return pl.pallas_call(
        pick_kernel,
        out_shape=(shape, shape),
        grid_spec=pltpu.PrefetchScalarGridSpec(
            num_scalar_prefetch=1,
            grid=(count, slots // per_block),
            in_specs=[
                pl.BlockSpec((1, capacity, 1), lambda i, j, order: (order[i], 0, 0)),
                pl.BlockSpec((features, features), lambda i, j, order: (0, 0)),
                table,
                table,
            ],
            out_specs=[picked, picked],
            scratch_shapes=[pltpu.VMEM((capacity, features), FULL)] * 2,
        ),
        compiler_params=pltpu.CompilerParams(vmem_limit_bytes=48 << 20),
        cost_estimate=pl.CostEstimate(
            flops=4 * count * capacity * slots * features,
            bytes_accessed=4 * count * slots * features,
            transcendentals=0,
        ),
        name="pick_rows",
    )(order, routes[:, :, None], turn, tokens, cotangent)


def place_kernel(order_ref, routes_ref, table_ref, values_ref, out_ref):
    block = pl.program_id(1)
    slots = table_ref.shape[1]
    capacity = routes_ref.shape[2]
    row = lax.broadcasted_iota(jnp.int32, (slots, capacity), 0) + block * slots
    chooser = (routes_ref[0] == row).astype(LOW)
    placed = product(chooser, values_ref[0])
    out_ref[0] = (table_ref[0].astype(FULL) + placed).astype(LOW)


def place_rows(table, values, routes, order):
    seq_count, slots, features = table.shape
    capacity = routes.shape[1]
    per_block = min(SLOT_BLOCK, slots)
    tall = pl.BlockSpec((1, per_block, features), lambda i, j, order: (order[i], j, 0))
    return pl.pallas_call(
        place_kernel,
        out_shape=jax.ShapeDtypeStruct(table.shape, table.dtype),
        grid_spec=pltpu.PrefetchScalarGridSpec(
            num_scalar_prefetch=1,
            grid=(seq_count, slots // per_block),
            in_specs=[
                pl.BlockSpec((1, 1, capacity), lambda i, j, order: (order[i], 0, 0)),
                tall,
                pl.BlockSpec((1, capacity, features), lambda i, j, order: (i, 0, 0)),
            ],
            out_specs=tall,
        ),
        compiler_params=pltpu.CompilerParams(vmem_limit_bytes=48 << 20),
        cost_estimate=pl.CostEstimate(
            flops=2 * seq_count * capacity * slots * features,
            bytes_accessed=4 * seq_count * slots * features,
            transcendentals=0,
        ),
        name="place_rows",
    )(order, routes[:, None, :], table, values)


def gates(routed, router_vec, live_ref, capacity):
    rows = routed.shape[0]
    score = jnp.sum(routed * router_vec, axis=-1, keepdims=True)
    gate_prob = 1.0 / (1.0 + jnp.exp(-score))
    live = [
        lax.broadcasted_iota(jnp.int32, (capacity, 1), 0) < live_ref[seq]
        for seq in range(rows // capacity)
    ]
    live = live[0] if len(live) == 1 else jnp.concatenate(live, axis=0)
    return gate_prob, jnp.where(live, gate_prob, 0.0)


def probabilities(queries, keys_all, live_count, scale_qk):
    scores = times_transposed(queries, keys_all) * scale_qk
    row = lax.broadcasted_iota(jnp.int32, scores.shape, 0)
    column = lax.broadcasted_iota(jnp.int32, scores.shape, 1)
    masked = jnp.where((column <= row) & (column < live_count), scores, -1e30)
    exp_scores = jnp.exp(masked - jnp.max(masked, axis=-1, keepdims=True))
    return exp_scores / jnp.sum(exp_scores, axis=-1, keepdims=True)


def split_heads(pair):
    owner = lax.broadcasted_iota(jnp.int32, pair.shape, 1) // HEAD_DIM
    return [jnp.where(owner == i, pair, jnp.zeros_like(pair)) for i in range(pair.shape[1] // HEAD_DIM)]


def attend_kernel(
    capacity, live_ref, routed_ref, cot_ref, small_ref, qk_own, qk_other, vo_own, vo_other,
    attn_in_ref, qkv_ref, heads_ref, attn_out_ref, mlp_in_ref, d_mlp_out_ref,
):
    routed = routed_ref[...].astype(FULL)
    rows, features = routed.shape
    half = features // 2
    wide = qkv_ref.shape[1] // 3
    _, gate_live = gates(routed, small_ref[2:3], live_ref, capacity)
    d_mlp_out_ref[...] = (gate_live * cot_ref[...].astype(FULL)).astype(LOW)
    normed, _ = norm_forward(routed)
    attn_in = (normed * small_ref[0:1]).astype(LOW)
    attn_in_ref[...] = attn_in
    left, right = attn_in[:, :half], attn_in[:, half:]
    qkv_ref[:, : 2 * wide] = (product(left, qk_own[...]) + product(right, qk_other[...])).astype(LOW)
    qkv_ref[:, 2 * wide :] = (
        product(left, vo_own[:, :wide]) + product(right, vo_other[:, :wide])
    ).astype(LOW)
    tile = 2 * HEAD_DIM
    for seq in range(rows // capacity):
        at = slice(seq * capacity, (seq + 1) * capacity)
        for start in range(0, wide, tile):
            keys_all = qkv_ref[at, wide + start : wide + start + tile]
            queries = split_heads(qkv_ref[at, start : start + tile])
            vals = split_heads(qkv_ref[at, 2 * wide + start : 2 * wide + start + tile])
            total = None
            for query, val in zip(queries, vals):
                probs = probabilities(query, keys_all, live_ref[seq], HEAD_DIM ** (-0.5))
                part = product(probs.astype(LOW), val)
                total = part if total is None else total + part
            heads_ref[at, start : start + tile] = total.astype(LOW)
    heads_out = heads_ref[...]
    attn_out_ref[:, :half] = times_transposed(heads_out, vo_own[:, wide:])
    attn_out_ref[:, half:] = times_transposed(heads_out, vo_other[:, wide:])
    normed_two, _ = norm_forward(routed + attn_out_ref[...])
    mlp_in_ref[...] = (normed_two * small_ref[1:2]).astype(LOW)


def whole_specs(count):
    return [pl.BlockSpec(memory_space=pltpu.VMEM)] * count


def attend(live_count, routed, cot_routed, small, query_key, value_out, capacity):
    rows, features = routed.shape
    wide = query_key[0].shape[1] // 2
    return pl.pallas_call(
        functools.partial(attend_kernel, capacity),
        out_shape=(
            jax.ShapeDtypeStruct((rows, features), LOW),
            jax.ShapeDtypeStruct((rows, 3 * wide), LOW),
            jax.ShapeDtypeStruct((rows, wide), LOW),
            jax.ShapeDtypeStruct((rows, features), FULL),
            jax.ShapeDtypeStruct((rows, features), LOW),
            jax.ShapeDtypeStruct((rows, features), LOW),
        ),
        in_specs=[pl.BlockSpec(memory_space=pltpu.SMEM)] + whole_specs(7),
        out_specs=tuple(whole_specs(6)),
        compiler_params=pltpu.CompilerParams(vmem_limit_bytes=56 << 20),
        cost_estimate=pl.CostEstimate(
            flops=8 * rows * features * wide + 4 * rows * capacity * wide,
            bytes_accessed=8 * features * wide + 14 * rows * features,
            transcendentals=rows * capacity * wide // HEAD_DIM,
        ),
        name="attend",
    )(live_count, routed, cot_routed, small, *query_key, *value_out)


def up_kernel(mlp_in_ref, d_mlp_out_ref, *refs):
    weights, outs = refs[:4], refs[4:]
    mlp_in = mlp_in_ref[...]
    d_mlp_out = d_mlp_out_ref[...]
    half = mlp_in.shape[1] // 2
    for stream in range(2):
        own, other = weights[2 * stream : 2 * stream + 2]
        pre_ref, hidden_ref, kept_ref, sent_ref = outs[4 * stream : 4 * stream + 4]
        pre = product(mlp_in[:, :half], own[...]) + product(mlp_in[:, half:], other[...])
        hidden = gelu_tanh(pre).astype(LOW)
        pre_ref[...] = pre
        hidden_ref[...] = hidden
        sent_ref[...] = contract_rows(d_mlp_out[:, half:], hidden).astype(LOW)
        kept_ref[...] = contract_rows(d_mlp_out[:, :half], hidden).astype(LOW)


TILE = 512


def up_layer(mlp_in, d_mlp_out, ups):
    rows, features = mlp_in.shape
    half = features // 2
    width = ups[0][0].shape[1]
    tile = min(TILE, width)
    whole = pl.BlockSpec((rows, features), lambda i: (0, 0))
    weight = pl.BlockSpec((half, tile), lambda i: (0, i))
    tall = pl.BlockSpec((rows, tile), lambda i: (0, i))
    outs = [
        jax.ShapeDtypeStruct((rows, width), FULL),
        jax.ShapeDtypeStruct((rows, width), LOW),
        jax.ShapeDtypeStruct((half, width), LOW),
        jax.ShapeDtypeStruct((half, width), LOW),
    ]
    got = pl.pallas_call(
        up_kernel,
        grid=(width // tile,),
        out_shape=tuple(outs * 2),
        in_specs=[whole, whole] + [weight] * 4,
        out_specs=tuple([tall, tall, weight, weight] * 2),
        compiler_params=pltpu.CompilerParams(vmem_limit_bytes=56 << 20),
        cost_estimate=pl.CostEstimate(
            flops=8 * rows * features * width,
            bytes_accessed=8 * features * width + 12 * rows * width,
            transcendentals=2 * rows * width,
        ),
        name="up_layer",
    )(mlp_in, d_mlp_out, *ups[0], *ups[1])
    return got[:4], got[4:]


def down_kernel(
    capacity, live_ref, routed_ref, cot_ref, small_ref, turn_ref, attn_out_ref, mlp_in_ref, d_mlp_out_ref, *refs
):
    weights, middle, outs = refs[:8], refs[8:12], refs[12:]
    update_ref, d_mlp_in_ref, dot_ref = outs[:3]
    grads, mlp_out = outs[3:7], outs[7]
    mlp_in = mlp_in_ref[...]
    d_mlp_out = d_mlp_out_ref[...]
    half = mlp_in.shape[1] // 2

    @pl.when(pl.program_id(0) == 0)
    def _():
        mlp_out[...] = jnp.zeros_like(mlp_out)
        d_mlp_in_ref[...] = jnp.zeros_like(d_mlp_in_ref)

    for stream in range(2):
        up_own, up_other, down_own, down_other = weights[4 * stream : 4 * stream + 4]
        pre_ref, hidden_ref = middle[2 * stream : 2 * stream + 2]
        kept_ref, sent_ref = grads[2 * stream : 2 * stream + 2]
        d_hidden = product(d_mlp_out[:, :half], down_own[...]) + product(
            d_mlp_out[:, half:], down_other[...]
        )
        d_pre = (d_hidden * gelu_slope(pre_ref[...])).astype(LOW)
        sent_ref[...] = contract_rows(mlp_in[:, half:], d_pre).astype(LOW)
        kept_ref[...] = contract_rows(mlp_in[:, :half], d_pre).astype(LOW)
        d_mlp_in_ref[:, :half] += times_transposed(d_pre, up_own[...])
        d_mlp_in_ref[:, half:] += times_transposed(d_pre, up_other[...])
        hidden = hidden_ref[...]
        mlp_out[:, :half] += times_transposed(hidden, down_own[...])
        mlp_out[:, half:] += times_transposed(hidden, down_other[...])

    @pl.when(pl.program_id(0) == pl.num_programs(0) - 1)
    def _():
        _, gate_live = gates(routed_ref[...].astype(FULL), small_ref[2:3], live_ref, capacity)
        branch = attn_out_ref[...] + mlp_out[...]
        update = (gate_live * branch).astype(LOW)
        update_ref[...] = times_transposed(update, turn_ref[...]).astype(LOW)
        dot_ref[...] = jnp.sum(cot_ref[...].astype(FULL) * branch, axis=-1, keepdims=True)


def down_layer(live_count, routed, cot_routed, small, turn, attn_out, mlp_in, d_mlp_out, ups, downs, kept, capacity):
    rows, features = mlp_in.shape
    half = features // 2
    width = ups[0][0].shape[1]
    tile = min(TILE, width)
    whole = pl.BlockSpec((rows, features), lambda i: (0, 0))
    weight = pl.BlockSpec((half, tile), lambda i: (0, i))
    tall = pl.BlockSpec((rows, tile), lambda i: (0, i))
    outs = (
        jax.ShapeDtypeStruct((rows, features), LOW),
        jax.ShapeDtypeStruct((rows, features), FULL),
        jax.ShapeDtypeStruct((rows, 1), FULL),
    ) + (jax.ShapeDtypeStruct((half, width), LOW),) * 4
    got = pl.pallas_call(
        functools.partial(down_kernel, capacity),
        grid=(width // tile,),
        out_shape=outs,
        in_specs=[
            pl.BlockSpec(memory_space=pltpu.SMEM),
            whole,
            whole,
            pl.BlockSpec(small.shape, lambda i: (0, 0)),
            pl.BlockSpec(turn.shape, lambda i: (0, 0)),
            whole,
            whole,
            whole,
        ]
        + [weight] * 8
        + [tall] * 4,
        out_specs=(whole, whole, pl.BlockSpec((rows, 1), lambda i: (0, 0))) + (weight,) * 4,
        scratch_shapes=[pltpu.VMEM((rows, features), FULL)],
        compiler_params=pltpu.CompilerParams(vmem_limit_bytes=56 << 20),
        cost_estimate=pl.CostEstimate(
            flops=16 * rows * features * width,
            bytes_accessed=12 * features * width + 12 * rows * width,
            transcendentals=2 * rows * width,
        ),
        name="down_layer",
    )(
        live_count, routed, cot_routed, small, turn, attn_out, mlp_in, d_mlp_out,
        *ups[0], *downs[0], *ups[1], *downs[1],
        *[array for stream in kept for array in stream[:2]],
    )
    return got[0], got[1], got[2], got[3:5], got[5:7]


def attend_back_kernel(
    capacity, live_ref, routed_ref, cot_ref, small_ref, turn_ref, attn_out_ref, d_mlp_in_ref, dot_ref, qkv_ref,
    qk_own, qk_other, vo_own, vo_other, d_routed_ref, d_attn_out_ref, d_qkv_ref, small_grads_ref, d_heads_ref,
):
    routed = routed_ref[...].astype(FULL)
    rows, features = routed.shape
    half = features // 2
    wide = qkv_ref.shape[1] // 3
    scale_qk = HEAD_DIM ** (-0.5)
    gate_prob, gate_live = gates(routed, small_ref[2:3], live_ref, capacity)
    normed_two, inverse_two = norm_forward(routed + attn_out_ref[...])
    d_middle, small_grads_ref[1:2] = norm_backward(
        d_mlp_in_ref[...], normed_two, inverse_two, small_ref[1:2]
    )
    d_attn_out = (d_middle + gate_live * cot_ref[...].astype(FULL)).astype(LOW)
    d_attn_out_ref[...] = d_attn_out
    d_heads_ref[...] = (
        product(d_attn_out[:, :half], vo_own[:, wide:]) + product(d_attn_out[:, half:], vo_other[:, wide:])
    ).astype(LOW)
    tile = 2 * HEAD_DIM
    for seq in range(rows // capacity):
        at = slice(seq * capacity, (seq + 1) * capacity)
        for start in range(0, wide, tile):
            query_pair = qkv_ref[at, start : start + tile]
            key_pair = qkv_ref[at, wide + start : wide + start + tile]
            val_pair = qkv_ref[at, 2 * wide + start : 2 * wide + start + tile]
            d_query, d_key, d_val = 0.0, 0.0, 0.0
            for query, key, d_head in zip(
                split_heads(query_pair), split_heads(key_pair), split_heads(d_heads_ref[at, start : start + tile])
            ):
                probs = probabilities(query, key_pair, live_ref[seq], scale_qk)
                d_val = d_val + contract_rows(probs.astype(LOW), d_head)
                d_probs = times_transposed(d_head, val_pair)
                d_scores = (
                    probs * (d_probs - jnp.sum(d_probs * probs, axis=-1, keepdims=True))
                ).astype(LOW)
                d_query = d_query + product(d_scores, key)
                d_key = d_key + contract_rows(d_scores, query)
            d_qkv_ref[at, start : start + tile] = (d_query * scale_qk).astype(LOW)
            d_qkv_ref[at, wide + start : wide + start + tile] = (d_key * scale_qk).astype(LOW)
            d_qkv_ref[at, 2 * wide + start : 2 * wide + start + tile] = d_val.astype(LOW)
    d_both = d_qkv_ref[:, : 2 * wide]
    d_vals = d_qkv_ref[:, 2 * wide :]
    d_attn_in = jnp.concatenate(
        [
            times_transposed(d_both, qk[...]) + times_transposed(d_vals, vo[:, :wide])
            for qk, vo in ((qk_own, vo_own), (qk_other, vo_other))
        ],
        axis=1,
    )
    normed_one, inverse_one = norm_forward(routed)
    d_from_norm, small_grads_ref[0:1] = norm_backward(d_attn_in, normed_one, inverse_one, small_ref[0:1])
    d_score = gate_live * (1.0 - gate_prob) * dot_ref[...]
    small_grads_ref[2:3] = jnp.sum(routed * d_score, axis=0, keepdims=True)
    d_routed = (d_middle + d_from_norm + d_score * small_ref[2:3]).astype(LOW)
    d_routed_ref[...] = times_transposed(d_routed, turn_ref[...]).astype(LOW)


def attend_back(live_count, routed, cot_routed, small, turn, attn_out, d_mlp_in, dot, qkv, query_key, value_out, capacity):
    rows, features = routed.shape
    wide = query_key[0].shape[1] // 2
    return pl.pallas_call(
        functools.partial(attend_back_kernel, capacity),
        out_shape=(
            jax.ShapeDtypeStruct((rows, features), LOW),
            jax.ShapeDtypeStruct((rows, features), LOW),
            jax.ShapeDtypeStruct((rows, 3 * wide), LOW),
            jax.ShapeDtypeStruct((3, features), FULL),
        ),
        in_specs=[pl.BlockSpec(memory_space=pltpu.SMEM)] + whole_specs(12),
        out_specs=tuple(whole_specs(4)),
        scratch_shapes=[pltpu.VMEM((rows, wide), LOW)],
        compiler_params=pltpu.CompilerParams(vmem_limit_bytes=56 << 20),
        cost_estimate=pl.CostEstimate(
            flops=8 * rows * features * wide + 10 * rows * capacity * wide,
            bytes_accessed=8 * features * wide + 14 * rows * features,
            transcendentals=rows * capacity * wide // HEAD_DIM,
        ),
        name="attend_back",
    )(live_count, routed, cot_routed, small, turn, attn_out, d_mlp_in, dot, qkv, *query_key, *value_out)


def grads_kernel(attn_in_ref, d_attn_out_ref, heads_ref, d_qkv_ref, qk_kept, qk_sent, vo_kept, vo_sent):
    half = attn_in_ref.shape[1] // 2
    wide = heads_ref.shape[1]
    for at, qk_ref, vo_ref in (
        (slice(half, 2 * half), qk_sent, vo_sent),
        (slice(0, half), qk_kept, vo_kept),
    ):
        attn_in = attn_in_ref[:, at]
        qk_ref[...] = contract_rows(attn_in, d_qkv_ref[:, : 2 * wide]).astype(LOW)
        vo_ref[:, :wide] = contract_rows(attn_in, d_qkv_ref[:, 2 * wide :]).astype(LOW)
        vo_ref[:, wide:] = contract_rows(d_attn_out_ref[:, at], heads_ref[...]).astype(LOW)


def attend_grads(attn_in, d_attn_out, heads_out, d_qkv):
    rows, features = attn_in.shape
    wide = heads_out.shape[1]
    got = pl.pallas_call(
        grads_kernel,
        out_shape=(jax.ShapeDtypeStruct((features // 2, 2 * wide), LOW),) * 4,
        in_specs=whole_specs(4),
        out_specs=tuple(whole_specs(4)),
        compiler_params=pltpu.CompilerParams(vmem_limit_bytes=56 << 20),
        cost_estimate=pl.CostEstimate(
            flops=8 * rows * features * wide,
            bytes_accessed=8 * features * wide + 8 * rows * features,
            transcendentals=0,
        ),
        name="attend_grads",
    )(attn_in, d_attn_out, heads_out, d_qkv)
    return got[:2], got[2:]


class Exchange:
    def __init__(self, mesh):
        self.batch = mesh.shape["batch"]
        self.tensor = mesh.shape["tensor"]
        bits = []
        bit = self.batch // 2
        while bit:
            bits.append(bit)
            bit //= 2
        self.core = bits[-1]
        self.chips = bits[:-1]

    def swap(self, array, bit):
        return lax.ppermute(array, "batch", [(i, i ^ bit) for i in range(self.batch)])

    def shift(self, array, step):
        size = self.tensor
        return lax.ppermute(array, "tensor", [(i, (i + step) % size) for i in range(size)])

    def block_order(self):
        order = [0]
        for bit in reversed([self.core] + self.chips):
            order = order + [place ^ bit for place in order]
        return order

    def gather_rows(self, array, flip):
        rows, width = array.shape
        places = len(self.chips)
        total = array.reshape((1,) * places + array.shape)
        sequence = range(places)
        for place in sequence if flip else reversed(sequence):
            other = self.swap(total, self.chips[place])
            total = jnp.concatenate([total, other], axis=place)
        half = total.reshape(rows * self.batch // 2, width)
        return half, self.swap(half, self.core)

    def gather_tensor(self, array):
        pieces = [array]
        for _ in range(self.tensor - 1):
            pieces.append(self.shift(pieces[-1], 1))
        return pieces

    def gather_small(self, array):
        total = array[None]
        for bit in reversed([self.core] + self.chips):
            total = jnp.concatenate([total, self.swap(total, bit)], axis=0)
        return total.transpose(1, 0, 2).reshape(array.shape[0], -1)

    def sum_all(self, array):
        for bit in self.chips + [self.core]:
            array = array + self.swap(array, bit)
        total = array
        for step in range(1, self.tensor):
            total = total + self.shift(array, step)
        return total

    def scatter_rows(self, kept, sent, flip):
        places = len(self.chips)
        total = add_rounded(kept, self.swap(sent, self.core))
        rows = total.shape[0] // (self.batch // 2)
        total = total.reshape((2,) * places + (rows, total.shape[1]))
        sequence = range(places)
        for place in reversed(sequence) if flip else sequence:
            own = lax.slice_in_dim(total, 0, 1, axis=place)
            other = lax.slice_in_dim(total, 1, 2, axis=place)
            total = add_rounded(own, self.swap(other, self.chips[place]))
        return total.reshape(rows, total.shape[-1])

    def scatter_tensor(self, pieces):
        total = pieces[-1]
        for piece in reversed(pieces[:-1]):
            total = add_rounded(piece, self.shift(total, -1))
        return total


def add_rounded(left, right):
    return (left.astype(FULL) + right.astype(FULL)).astype(LOW)


def shards(
    mesh,
    tokens,
    lengths,
    routes,
    w_query,
    w_key,
    w_value,
    w_out,
    w_up,
    w_down,
    gain_attn,
    gain_mlp,
    w_router,
    cotangent,
):
    moves = Exchange(mesh)
    device = lax.axis_index("batch")
    column = lax.axis_index("tensor")
    seq_count, capacity = routes.shape
    features = tokens.shape[1]
    tokens = tokens.reshape(seq_count, -1, features)
    cotangent = cotangent.reshape(tokens.shape)

    repeats = max(1, moves.tensor // seq_count)
    local_count = max(1, seq_count // moves.tensor)
    first = column // repeats if repeats > 1 else column * local_count
    order = (first + jnp.arange(local_count)).astype(jnp.int32)
    counts_once = (column % repeats) == 0

    def once(values):
        return jnp.where(counts_once, values, jnp.zeros_like(values)) if repeats > 1 else values

    own = features // moves.batch
    place_block = jnp.asarray(moves.block_order(), jnp.int32)
    source = ((place_block ^ device)[:, None] * own + jnp.arange(own, dtype=jnp.int32)).reshape(-1)
    turn = (jnp.arange(features, dtype=jnp.int32)[:, None] == source[None, :]).astype(LOW)

    wide = w_query.shape[1]
    wide_up = w_up.shape[1] // 2

    def fetch(parts, flip):
        pieces = moves.gather_tensor(jnp.concatenate([p.astype(LOW) for p in parts], axis=1))
        width = parts[0].shape[1]
        ordered = [
            piece[:, i * width : (i + 1) * width] for i in range(len(parts)) for piece in pieces
        ]
        return moves.gather_rows(jnp.concatenate(ordered, axis=1), flip)

    down_turned = w_down.astype(LOW).T
    query_key = fetch((w_query, w_key), False)
    value_out = fetch((w_value, w_out.astype(LOW).T), True)
    ups = (fetch((w_up[:, :wide_up],), False), fetch((w_up[:, wide_up:],), True))
    downs = (fetch((down_turned[:, :wide_up],), False), fetch((down_turned[:, wide_up:],), True))
    small = jnp.stack([gain_attn, gain_mlp, w_router]).astype(LOW)
    small = moves.gather_small(small).astype(FULL)

    rows_total = local_count * capacity
    routed, cot_routed = pick_rows(tokens, cotangent, routes, order, local_count, turn)
    routed = routed.reshape(rows_total, features)
    cot_routed = cot_routed.reshape(rows_total, features)
    live_count = lax.dynamic_slice_in_dim(lengths, first, local_count) // 8
    attn_in, qkv, heads_out, attn_out, mlp_in, d_mlp_out = attend(
        live_count, routed, cot_routed, small, query_key, value_out, capacity
    )

    def reduce(kept, sent, parts, flip):
        total = moves.scatter_rows(once(kept), once(sent), flip)
        width = total.shape[1] // parts // moves.tensor
        pieces = [
            jnp.concatenate(
                [
                    total[:, (i * moves.tensor + k) * width : (i * moves.tensor + k + 1) * width]
                    for i in range(parts)
                ],
                axis=1,
            )
            for k in range(moves.tensor)
        ]
        return moves.scatter_tensor(pieces)

    kept = up_layer(mlp_in, d_mlp_out, ups)
    grad_down = [reduce(*stream[2:], 1, flip) for stream, flip in zip(kept, (False, True))]
    update, d_mlp_in, dot, *up_grads = down_layer(
        live_count, routed, cot_routed, small, turn, attn_out, mlp_in, d_mlp_out, ups, downs, kept, capacity
    )
    grad_up = [reduce(*stream, 1, flip) for stream, flip in zip(up_grads, (False, True))]

    def spread_out(rows, table):
        pieces = moves.gather_tensor(rows)
        kept = pieces[::repeats] if repeats > 1 else pieces
        values = jnp.concatenate(
            [piece.reshape(local_count, capacity, features) for piece in kept], axis=0
        )
        steps = jnp.arange(0, moves.tensor, repeats)
        owners = ((column - steps) % moves.tensor).astype(jnp.int32)
        if repeats > 1:
            places = owners // repeats
        else:
            places = (owners[:, None] * local_count + jnp.arange(local_count)).reshape(-1)
        return place_rows(table, values, routes, places.astype(jnp.int32)).reshape(-1, features)

    output = spread_out(update, tokens)
    d_routed, d_attn_out, d_qkv, small_grads = attend_back(
        live_count, routed, cot_routed, small, turn, attn_out, d_mlp_in, dot, qkv, query_key, value_out, capacity
    )
    grad_tokens = spread_out(d_routed, cotangent)
    qk_grads, vo_grads = attend_grads(attn_in, d_attn_out, heads_out, d_qkv)
    grad_query_key = reduce(*qk_grads, 2, False)
    grad_value_out = reduce(*vo_grads, 2, True)

    small_grads = lax.dot_general(
        small_grads, turn.astype(FULL), (((1,), (1,)), ((), ())), precision=lax.Precision.HIGHEST
    )
    small_grads = moves.sum_all(once(small_grads))
    small_grads = lax.dynamic_slice_in_dim(small_grads, device * own, own, axis=1)

    return (
        output,
        grad_tokens,
        grad_query_key[:, :wide].astype(FULL),
        grad_query_key[:, wide:].astype(FULL),
        grad_value_out[:, :wide].astype(FULL),
        grad_value_out[:, wide:].T.astype(FULL),
        jnp.concatenate(grad_up, axis=1).astype(FULL),
        jnp.concatenate(grad_down, axis=1).T.astype(FULL),
        small_grads[0],
        small_grads[1],
        small_grads[2],
    )


def solution(mesh):
    in_specs = (
        P("batch", None),
        P("batch"),
        P("batch", None),
        P("batch", "tensor"),
        P("batch", "tensor"),
        P("batch", "tensor"),
        P("tensor", "batch"),
        P("batch", "tensor"),
        P("tensor", "batch"),
        P("batch"),
        P("batch"),
        P("batch"),
        P("batch", None),
    )
    out_specs = (
        P("batch", None),
        P("batch", None),
        P("batch", "tensor"),
        P("batch", "tensor"),
        P("batch", "tensor"),
        P("tensor", "batch"),
        P("batch", "tensor"),
        P("tensor", "batch"),
        P("batch"),
        P("batch"),
        P("batch"),
    )
    return jax.shard_map(
        functools.partial(shards, mesh),
        mesh=mesh,
        in_specs=in_specs,
        out_specs=out_specs,
        check_vma=False,
    )
```

```python
import functools

import jax
import jax.numpy as jnp
from jax import lax
from jax.experimental import pallas as pl
from jax.experimental.pallas import tpu as pltpu
from jax.sharding import PartitionSpec as P

HEAD_DIM = 64
SLOT_BLOCK = 512
EPSILON = 1e-06


CURVE = 0.7978845608028654
CUBIC = 0.044715


def gelu_tanh(values):
    return 0.5 * values * (1.0 + jnp.tanh(CURVE * (values + CUBIC * values * values * values)))


def gelu_slope(values):
    square = values * values
    bend = jnp.tanh(CURVE * (values + CUBIC * values * square))
    inner = CURVE * (1.0 + 3.0 * CUBIC * square)
    return 0.5 * (1.0 + bend) + 0.5 * values * (1.0 - bend * bend) * inner


def product(left, right):
    return jnp.dot(left, right, preferred_element_type=jnp.float32)


def contract_rows(left, right):
    return lax.dot_general(
        left, right, (((0,), (0,)), ((), ())), preferred_element_type=jnp.float32
    )


def times_transposed(left, right):
    return lax.dot_general(
        left, right, (((1,), (1,)), ((), ())), preferred_element_type=jnp.float32
    )


def norm_backward(d_normed_in, normed, inverse, gain_vec):
    d_scaled = d_normed_in * gain_vec
    d_input = inverse * (d_scaled - normed * jnp.mean(d_scaled * normed, axis=-1, keepdims=True))
    return (d_input, jnp.sum(d_normed_in * normed, axis=0, keepdims=True))


def norm_forward(values):
    inverse = lax.rsqrt(jnp.mean(values * values, axis=-1, keepdims=True) + EPSILON)
    return (values * inverse, inverse)


LOW = jnp.bfloat16
FULL = jnp.float32


def pick_kernel(order_ref, routes_ref, turn_ref, tokens_ref, cot_ref, routed_ref, cot_routed_ref, total, cot_total):
    block = pl.program_id(1)
    capacity = routes_ref.shape[1]
    slots = tokens_ref.shape[1]
    column = lax.broadcasted_iota(jnp.int32, (capacity, slots), 1) + block * slots
    chooser = (routes_ref[0] == column).astype(LOW)
    part = product(chooser, tokens_ref[0])
    cot_part = product(chooser, cot_ref[0])

    @pl.when(block == 0)
    def _():
        total[...] = part
        cot_total[...] = cot_part

    @pl.when(block > 0)
    def _():
        total[...] += part
        cot_total[...] += cot_part

    @pl.when(block == pl.num_programs(1) - 1)
    def _():
        routed_ref[0] = product(total[...].astype(LOW), turn_ref[...]).astype(LOW)
        cot_routed_ref[0] = product(cot_total[...].astype(LOW), turn_ref[...]).astype(LOW)


def pick_rows(tokens, cotangent, routes, order, count, turn):
    seq_count, slots, features = tokens.shape
    capacity = routes.shape[1]
    per_block = min(SLOT_BLOCK, slots)
    table = pl.BlockSpec((1, per_block, features), lambda i, j, order: (order[i], j, 0))
    picked = pl.BlockSpec((1, capacity, features), lambda i, j, order: (i, 0, 0))
    shape = jax.ShapeDtypeStruct((count, capacity, features), LOW)
    return pl.pallas_call(
        pick_kernel,
        out_shape=(shape, shape),
        grid_spec=pltpu.PrefetchScalarGridSpec(
            num_scalar_prefetch=1,
            grid=(count, slots // per_block),
            in_specs=[
                pl.BlockSpec((1, capacity, 1), lambda i, j, order: (order[i], 0, 0)),
                pl.BlockSpec((features, features), lambda i, j, order: (0, 0)),
                table,
                table,
            ],
            out_specs=[picked, picked],
            scratch_shapes=[pltpu.VMEM((capacity, features), FULL)] * 2,
        ),
        compiler_params=pltpu.CompilerParams(vmem_limit_bytes=48 << 20),
        cost_estimate=pl.CostEstimate(
            flops=4 * count * capacity * slots * features,
            bytes_accessed=4 * count * slots * features,
            transcendentals=0,
        ),
        name="pick_rows",
    )(order, routes[:, :, None], turn, tokens, cotangent)


def place_kernel(order_ref, routes_ref, table_ref, values_ref, out_ref):
    block = pl.program_id(1)
    slots = table_ref.shape[1]
    capacity = routes_ref.shape[2]
    row = lax.broadcasted_iota(jnp.int32, (slots, capacity), 0) + block * slots
    chooser = (routes_ref[0] == row).astype(LOW)
    placed = product(chooser, values_ref[0])
    out_ref[0] = (table_ref[0].astype(FULL) + placed).astype(LOW)


def place_rows(table, values, routes, order):
    seq_count, slots, features = table.shape
    capacity = routes.shape[1]
    per_block = min(SLOT_BLOCK, slots)
    tall = pl.BlockSpec((1, per_block, features), lambda i, j, order: (order[i], j, 0))
    return pl.pallas_call(
        place_kernel,
        out_shape=jax.ShapeDtypeStruct(table.shape, table.dtype),
        grid_spec=pltpu.PrefetchScalarGridSpec(
            num_scalar_prefetch=1,
            grid=(seq_count, slots // per_block),
            in_specs=[
                pl.BlockSpec((1, 1, capacity), lambda i, j, order: (order[i], 0, 0)),
                tall,
                pl.BlockSpec((1, capacity, features), lambda i, j, order: (i, 0, 0)),
            ],
            out_specs=tall,
        ),
        compiler_params=pltpu.CompilerParams(vmem_limit_bytes=48 << 20),
        cost_estimate=pl.CostEstimate(
            flops=2 * seq_count * capacity * slots * features,
            bytes_accessed=4 * seq_count * slots * features,
            transcendentals=0,
        ),
        name="place_rows",
    )(order, routes[:, None, :], table, values)


def gates(routed, router_vec, live_ref, capacity):
    rows = routed.shape[0]
    score = jnp.sum(routed * router_vec, axis=-1, keepdims=True)
    gate_prob = 1.0 / (1.0 + jnp.exp(-score))
    live = [
        lax.broadcasted_iota(jnp.int32, (capacity, 1), 0) < live_ref[seq]
        for seq in range(rows // capacity)
    ]
    live = live[0] if len(live) == 1 else jnp.concatenate(live, axis=0)
    return gate_prob, jnp.where(live, gate_prob, 0.0)


def probabilities(queries, keys_all, live_count, scale_qk):
    scores = times_transposed(queries, keys_all) * scale_qk
    row = lax.broadcasted_iota(jnp.int32, scores.shape, 0)
    column = lax.broadcasted_iota(jnp.int32, scores.shape, 1)
    masked = jnp.where((column <= row) & (column < live_count), scores, -1e30)
    exp_scores = jnp.exp(masked - jnp.max(masked, axis=-1, keepdims=True))
    return exp_scores / jnp.sum(exp_scores, axis=-1, keepdims=True)


def split_heads(pair):
    owner = lax.broadcasted_iota(jnp.int32, pair.shape, 1) // HEAD_DIM
    return [jnp.where(owner == i, pair, jnp.zeros_like(pair)) for i in range(pair.shape[1] // HEAD_DIM)]


def attend_kernel(
    capacity, live_ref, routed_ref, cot_ref, small_ref, own, other,
    attn_in_ref, qkv_ref, heads_ref, attn_out_ref, mlp_in_ref, d_mlp_out_ref,
):
    routed = routed_ref[...].astype(FULL)
    rows, features = routed.shape
    half = features // 2
    wide = qkv_ref.shape[1] // 3
    _, gate_live = gates(routed, small_ref[2:3], live_ref, capacity)
    d_mlp_out_ref[...] = (gate_live * cot_ref[...].astype(FULL)).astype(LOW)
    normed, _ = norm_forward(routed)
    attn_in = (normed * small_ref[0:1]).astype(LOW)
    attn_in_ref[...] = attn_in
    left, right = attn_in[:, :half], attn_in[:, half:]
    qkv_ref[:, : 2 * wide] = (product(left, own[0]) + product(right, other[0])).astype(LOW)
    qkv_ref[:, 2 * wide :] = (
        product(left, own[1, :, :wide]) + product(right, other[1, :, :wide])
    ).astype(LOW)
    tile = 2 * HEAD_DIM
    for seq in range(rows // capacity):
        at = slice(seq * capacity, (seq + 1) * capacity)
        for start in range(0, wide, tile):
            keys_all = qkv_ref[at, wide + start : wide + start + tile]
            queries = split_heads(qkv_ref[at, start : start + tile])
            vals = split_heads(qkv_ref[at, 2 * wide + start : 2 * wide + start + tile])
            total = None
            for query, val in zip(queries, vals):
                probs = probabilities(query, keys_all, live_ref[seq], HEAD_DIM ** (-0.5))
                part = product(probs.astype(LOW), val)
                total = part if total is None else total + part
            heads_ref[at, start : start + tile] = total.astype(LOW)
    heads_out = heads_ref[...]
    attn_out_ref[:, :half] = times_transposed(heads_out, own[1, :, wide:])
    attn_out_ref[:, half:] = times_transposed(heads_out, other[1, :, wide:])
    normed_two, _ = norm_forward(routed + attn_out_ref[...])
    mlp_in_ref[...] = (normed_two * small_ref[1:2]).astype(LOW)


def whole_specs(count):
    return [pl.BlockSpec(memory_space=pltpu.VMEM)] * count


def attend(live_count, routed, cot_routed, small, weights, capacity):
    rows, features = routed.shape
    wide = weights[0].shape[2] // 2
    return pl.pallas_call(
        functools.partial(attend_kernel, capacity),
        out_shape=(
            jax.ShapeDtypeStruct((rows, features), LOW),
            jax.ShapeDtypeStruct((rows, 3 * wide), LOW),
            jax.ShapeDtypeStruct((rows, wide), LOW),
            jax.ShapeDtypeStruct((rows, features), FULL),
            jax.ShapeDtypeStruct((rows, features), LOW),
            jax.ShapeDtypeStruct((rows, features), LOW),
        ),
        in_specs=[pl.BlockSpec(memory_space=pltpu.SMEM)] + whole_specs(5),
        out_specs=tuple(whole_specs(6)),
        compiler_params=pltpu.CompilerParams(vmem_limit_bytes=56 << 20),
        cost_estimate=pl.CostEstimate(
            flops=8 * rows * features * wide + 4 * rows * capacity * wide,
            bytes_accessed=8 * features * wide + 14 * rows * features,
            transcendentals=rows * capacity * wide // HEAD_DIM,
        ),
        name="attend",
    )(live_count, routed, cot_routed, small, *weights)


def send(sent_refs, stream, left, right):
    half = left.shape[1] // 2
    part = half // 2
    for i in range(2):
        rows = left[:, half + i * part : half + (i + 1) * part]
        sent_refs[2 * stream + i][...] = contract_rows(rows, right).astype(LOW)


def up_kernel(mlp_in_ref, d_mlp_out_ref, own, other, pre_ref, hidden_ref, kept_ref, *sent_refs):
    mlp_in = mlp_in_ref[...]
    d_mlp_out = d_mlp_out_ref[...]
    half = mlp_in.shape[1] // 2
    for stream in range(2):
        pre = product(mlp_in[:, :half], own[stream]) + product(mlp_in[:, half:], other[stream])
        hidden = gelu_tanh(pre).astype(LOW)
        pre_ref[stream] = pre
        hidden_ref[stream] = hidden
        send(sent_refs, stream, d_mlp_out, hidden)
        kept_ref[stream] = contract_rows(d_mlp_out[:, :half], hidden).astype(LOW)


TILE = 512


def up_layer(mlp_in, d_mlp_out, ups):
    rows, features = mlp_in.shape
    streams, half, width = ups[0].shape
    tile = min(TILE, width)
    whole = pl.BlockSpec((rows, features), lambda i: (0, 0))
    weight = pl.BlockSpec((streams, half, tile), lambda i: (0, 0, i))
    tall = pl.BlockSpec((streams, rows, tile), lambda i: (0, 0, i))
    return pl.pallas_call(
        up_kernel,
        grid=(width // tile,),
        out_shape=(
            jax.ShapeDtypeStruct((streams, rows, width), FULL),
            jax.ShapeDtypeStruct((streams, rows, width), LOW),
            jax.ShapeDtypeStruct(ups[0].shape, LOW),
        )
        + (jax.ShapeDtypeStruct((half // 2, width), LOW),) * 4,
        in_specs=[whole, whole, weight, weight],
        out_specs=(tall, tall, weight) + (pl.BlockSpec((half // 2, tile), lambda i: (0, i)),) * 4,
        compiler_params=pltpu.CompilerParams(vmem_limit_bytes=56 << 20),
        cost_estimate=pl.CostEstimate(
            flops=8 * rows * features * width,
            bytes_accessed=8 * features * width + 12 * rows * width,
            transcendentals=2 * rows * width,
        ),
        name="up_layer",
    )(mlp_in, d_mlp_out, *ups)


def down_kernel(
    capacity, live_ref, routed_ref, cot_ref, small_ref, turn_ref, attn_out_ref, mlp_in_ref, d_mlp_out_ref,
    up_own, up_other, down_own, down_other, pre_ref, hidden_ref,
    update_ref, d_mlp_in_ref, dot_ref, kept_ref, sent_one, sent_two, sent_three, sent_four, mlp_out,
):
    sent_refs = (sent_one, sent_two, sent_three, sent_four)
    mlp_in = mlp_in_ref[...]
    d_mlp_out = d_mlp_out_ref[...]
    half = mlp_in.shape[1] // 2

    @pl.when(pl.program_id(0) == 0)
    def _():
        mlp_out[...] = jnp.zeros_like(mlp_out)
        d_mlp_in_ref[...] = jnp.zeros_like(d_mlp_in_ref)

    for stream in range(2):
        d_hidden = product(d_mlp_out[:, :half], down_own[stream]) + product(
            d_mlp_out[:, half:], down_other[stream]
        )
        d_pre = (d_hidden * gelu_slope(pre_ref[stream])).astype(LOW)
        send(sent_refs, stream, mlp_in, d_pre)
        kept_ref[stream] = contract_rows(mlp_in[:, :half], d_pre).astype(LOW)
        d_mlp_in_ref[:, :half] += times_transposed(d_pre, up_own[stream])
        d_mlp_in_ref[:, half:] += times_transposed(d_pre, up_other[stream])
        hidden = hidden_ref[stream]
        mlp_out[:, :half] += times_transposed(hidden, down_own[stream])
        mlp_out[:, half:] += times_transposed(hidden, down_other[stream])

    @pl.when(pl.program_id(0) == pl.num_programs(0) - 1)
    def _():
        _, gate_live = gates(routed_ref[...].astype(FULL), small_ref[2:3], live_ref, capacity)
        branch = attn_out_ref[...] + mlp_out[...]
        update = (gate_live * branch).astype(LOW)
        update_ref[...] = times_transposed(update, turn_ref[...]).astype(LOW)
        dot_ref[...] = jnp.sum(cot_ref[...].astype(FULL) * branch, axis=-1, keepdims=True)


def down_layer(live_count, routed, cot_routed, small, turn, attn_out, mlp_in, d_mlp_out, ups, downs, pre, hidden, capacity):
    rows, features = mlp_in.shape
    streams, half, width = ups[0].shape
    tile = min(TILE, width)
    whole = pl.BlockSpec((rows, features), lambda i: (0, 0))
    weight = pl.BlockSpec((streams, half, tile), lambda i: (0, 0, i))
    tall = pl.BlockSpec((streams, rows, tile), lambda i: (0, 0, i))
    return pl.pallas_call(
        functools.partial(down_kernel, capacity),
        grid=(width // tile,),
        out_shape=(
            jax.ShapeDtypeStruct((rows, features), LOW),
            jax.ShapeDtypeStruct((rows, features), FULL),
            jax.ShapeDtypeStruct((rows, 1), FULL),
            jax.ShapeDtypeStruct(ups[0].shape, LOW),
        )
        + (jax.ShapeDtypeStruct((half // 2, width), LOW),) * 4,
        in_specs=[
            pl.BlockSpec(memory_space=pltpu.SMEM),
            whole,
            whole,
            pl.BlockSpec(small.shape, lambda i: (0, 0)),
            pl.BlockSpec(turn.shape, lambda i: (0, 0)),
            whole,
            whole,
            whole,
        ]
        + [weight] * 4
        + [tall] * 2,
        out_specs=(whole, whole, pl.BlockSpec((rows, 1), lambda i: (0, 0)), weight)
        + (pl.BlockSpec((half // 2, tile), lambda i: (0, i)),) * 4,
        scratch_shapes=[pltpu.VMEM((rows, features), FULL)],
        compiler_params=pltpu.CompilerParams(vmem_limit_bytes=56 << 20),
        cost_estimate=pl.CostEstimate(
            flops=16 * rows * features * width,
            bytes_accessed=12 * features * width + 12 * rows * width,
            transcendentals=2 * rows * width,
        ),
        name="down_layer",
    )(live_count, routed, cot_routed, small, turn, attn_out, mlp_in, d_mlp_out, *ups, *downs, pre, hidden)


def attend_back_kernel(
    capacity, live_ref, routed_ref, cot_ref, small_ref, turn_ref, attn_out_ref, d_mlp_in_ref, dot_ref, qkv_ref,
    own, other, d_routed_ref, d_attn_out_ref, d_qkv_ref, small_grads_ref, d_heads_ref,
):
    routed = routed_ref[...].astype(FULL)
    rows, features = routed.shape
    half = features // 2
    wide = qkv_ref.shape[1] // 3
    scale_qk = HEAD_DIM ** (-0.5)
    gate_prob, gate_live = gates(routed, small_ref[2:3], live_ref, capacity)
    normed_two, inverse_two = norm_forward(routed + attn_out_ref[...])
    d_middle, small_grads_ref[1:2] = norm_backward(
        d_mlp_in_ref[...], normed_two, inverse_two, small_ref[1:2]
    )
    d_attn_out = (d_middle + gate_live * cot_ref[...].astype(FULL)).astype(LOW)
    d_attn_out_ref[...] = d_attn_out
    d_heads_ref[...] = (
        product(d_attn_out[:, :half], own[1, :, wide:]) + product(d_attn_out[:, half:], other[1, :, wide:])
    ).astype(LOW)
    tile = 2 * HEAD_DIM
    for seq in range(rows // capacity):
        at = slice(seq * capacity, (seq + 1) * capacity)
        for start in range(0, wide, tile):
            query_pair = qkv_ref[at, start : start + tile]
            key_pair = qkv_ref[at, wide + start : wide + start + tile]
            val_pair = qkv_ref[at, 2 * wide + start : 2 * wide + start + tile]
            d_query, d_key, d_val = 0.0, 0.0, 0.0
            for query, key, d_head in zip(
                split_heads(query_pair), split_heads(key_pair), split_heads(d_heads_ref[at, start : start + tile])
            ):
                probs = probabilities(query, key_pair, live_ref[seq], scale_qk)
                d_val = d_val + contract_rows(probs.astype(LOW), d_head)
                d_probs = times_transposed(d_head, val_pair)
                d_scores = (
                    probs * (d_probs - jnp.sum(d_probs * probs, axis=-1, keepdims=True))
                ).astype(LOW)
                d_query = d_query + product(d_scores, key)
                d_key = d_key + contract_rows(d_scores, query)
            d_qkv_ref[at, start : start + tile] = (d_query * scale_qk).astype(LOW)
            d_qkv_ref[at, wide + start : wide + start + tile] = (d_key * scale_qk).astype(LOW)
            d_qkv_ref[at, 2 * wide + start : 2 * wide + start + tile] = d_val.astype(LOW)
    d_both = d_qkv_ref[:, : 2 * wide]
    d_vals = d_qkv_ref[:, 2 * wide :]
    d_attn_in = jnp.concatenate(
        [
            times_transposed(d_both, side[0]) + times_transposed(d_vals, side[1, :, :wide])
            for side in (own, other)
        ],
        axis=1,
    )
    normed_one, inverse_one = norm_forward(routed)
    d_from_norm, small_grads_ref[0:1] = norm_backward(d_attn_in, normed_one, inverse_one, small_ref[0:1])
    d_score = gate_live * (1.0 - gate_prob) * dot_ref[...]
    small_grads_ref[2:3] = jnp.sum(routed * d_score, axis=0, keepdims=True)
    d_routed = (d_middle + d_from_norm + d_score * small_ref[2:3]).astype(LOW)
    d_routed_ref[...] = times_transposed(d_routed, turn_ref[...]).astype(LOW)


def attend_back(live_count, routed, cot_routed, small, turn, attn_out, d_mlp_in, dot, qkv, weights, capacity):
    rows, features = routed.shape
    wide = weights[0].shape[2] // 2
    return pl.pallas_call(
        functools.partial(attend_back_kernel, capacity),
        out_shape=(
            jax.ShapeDtypeStruct((rows, features), LOW),
            jax.ShapeDtypeStruct((rows, features), LOW),
            jax.ShapeDtypeStruct((rows, 3 * wide), LOW),
            jax.ShapeDtypeStruct((3, features), FULL),
        ),
        in_specs=[pl.BlockSpec(memory_space=pltpu.SMEM)] + whole_specs(10),
        out_specs=tuple(whole_specs(4)),
        scratch_shapes=[pltpu.VMEM((rows, wide), LOW)],
        compiler_params=pltpu.CompilerParams(vmem_limit_bytes=56 << 20),
        cost_estimate=pl.CostEstimate(
            flops=8 * rows * features * wide + 10 * rows * capacity * wide,
            bytes_accessed=8 * features * wide + 14 * rows * features,
            transcendentals=rows * capacity * wide // HEAD_DIM,
        ),
        name="attend_back",
    )(live_count, routed, cot_routed, small, turn, attn_out, d_mlp_in, dot, qkv, *weights)


def grads_kernel(attn_in_ref, d_attn_out_ref, heads_ref, d_qkv_ref, kept_ref, *sent_refs):
    half = attn_in_ref.shape[1] // 2
    wide = heads_ref.shape[1]
    part = half // 2
    targets = [
        (half + i * part, half + (i + 1) * part, (sent_refs[i], sent_refs[2 + i])) for i in range(2)
    ] + [(0, half, (kept_ref.at[0], kept_ref.at[1]))]
    for low, high, (qk_ref, vo_ref) in targets:
        attn_in = attn_in_ref[:, low:high]
        qk_ref[...] = contract_rows(attn_in, d_qkv_ref[:, : 2 * wide]).astype(LOW)
        vo_ref[:, :wide] = contract_rows(attn_in, d_qkv_ref[:, 2 * wide :]).astype(LOW)
        vo_ref[:, wide:] = contract_rows(d_attn_out_ref[:, low:high], heads_ref[...]).astype(LOW)


def attend_grads(attn_in, d_attn_out, heads_out, d_qkv):
    rows, features = attn_in.shape
    wide = heads_out.shape[1]
    return pl.pallas_call(
        grads_kernel,
        out_shape=(jax.ShapeDtypeStruct((2, features // 2, 2 * wide), LOW),)
        + (jax.ShapeDtypeStruct((features // 4, 2 * wide), LOW),) * 4,
        in_specs=whole_specs(4),
        out_specs=tuple(whole_specs(5)),
        compiler_params=pltpu.CompilerParams(vmem_limit_bytes=56 << 20),
        cost_estimate=pl.CostEstimate(
            flops=8 * rows * features * wide,
            bytes_accessed=8 * features * wide + 8 * rows * features,
            transcendentals=0,
        ),
        name="attend_grads",
    )(attn_in, d_attn_out, heads_out, d_qkv)


class Exchange:
    def __init__(self, mesh):
        self.batch = mesh.shape["batch"]
        self.tensor = mesh.shape["tensor"]
        bits = []
        bit = self.batch // 2
        while bit:
            bits.append(bit)
            bit //= 2
        self.core = bits[-1]
        self.chips = bits[:-1]

    def swap(self, array, bit):
        with jax.named_scope(f"swap{bit}"):
            return lax.ppermute(array, "batch", [(i, i ^ bit) for i in range(self.batch)])

    def shift(self, array, step):
        size = self.tensor
        with jax.named_scope(f"shift{step}"):
            return lax.ppermute(array, "tensor", [(i, (i + step) % size) for i in range(size)])

    def block_order(self):
        order = [0]
        for bit in reversed([self.core] + self.chips):
            order = order + [place ^ bit for place in order]
        return order

    def gather_small(self, array):
        total = array[None]
        for bit in reversed([self.core] + self.chips):
            total = jnp.concatenate([total, self.swap(total, bit)], axis=0)
        return total.transpose(1, 0, 2).reshape(array.shape[0], -1)

    def sum_all(self, array):
        for bit in self.chips + [self.core]:
            array = array + self.swap(array, bit)
        total = array
        for step in range(1, self.tensor):
            total = total + self.shift(array, step)
        return total

    def axis(self, stream, step):
        return step if stream else len(self.chips) - 1 - step

    def swap_step(self, pair, step):
        return [self.swap(array, self.chips[self.axis(i, step)]) for i, array in enumerate(pair)]


def small_kernel(kernel, out_shape, *arrays, name):
    return pl.pallas_call(
        kernel,
        out_shape=out_shape,
        in_specs=whole_specs(len(arrays)),
        out_specs=tuple(whole_specs(len(out_shape))),
        compiler_params=pltpu.CompilerParams(vmem_limit_bytes=40 << 20),
        cost_estimate=pl.CostEstimate(
            flops=0, bytes_accessed=4 * sum(a.size for a in arrays), transcendentals=0
        ),
        name=name,
    )(*arrays)


def streams_kernel(parts, *refs):
    pieces, outs = refs[:-2], refs[-2:]
    count = len(pieces)
    width = pieces[0].shape[1] // (2 * parts)
    for stream, out_ref in enumerate(outs):
        lead = (0,) * (len(out_ref.shape) - 2)
        for i in range(parts):
            source = (stream * parts + i) * width
            for k, piece in enumerate(pieces):
                target = (i * count + k) * width
                out_ref[lead + (slice(None), slice(target, target + width))] = piece[
                    :, source : source + width
                ]


def to_streams(pieces, parts, places):
    rows, columns = pieces[0].shape
    shape = (1,) * places + (rows, columns * len(pieces) // 2)
    out = jax.ShapeDtypeStruct(shape, pieces[0].dtype)
    return small_kernel(functools.partial(streams_kernel, parts), (out, out), *pieces, name="streams")


def join_kernel(axes, stacked, *refs):
    ins, outs = refs[:4], refs[4:]
    for stream in range(2):
        for side in range(2):
            source = ins[2 * stream + side]
            at = [slice(None)] * len(source.shape)
            size = source.shape[axes[stream]]
            at[axes[stream]] = slice(side * size, (side + 1) * size)
            if stacked:
                outs[0][(stream,) + tuple(at)] = source[...]
            else:
                outs[stream][tuple(at)] = source[...]


def join(pair, arrived, axes, stacked):
    columns = pair[0].shape[-1]
    tile = min(TILE, columns)
    shapes = []
    for array, axis in zip(pair, axes):
        shape = list(array.shape)
        shape[axis] *= 2
        shapes.append(tuple(shape))
    if stacked:
        shapes = [(2,) + shapes[0]]

    def tiled(shape):
        return pl.BlockSpec(tuple(shape[:-1]) + (tile,), column_block(len(shape)))

    got = pl.pallas_call(
        functools.partial(join_kernel, axes, stacked),
        grid=(columns // tile,),
        out_shape=tuple(jax.ShapeDtypeStruct(shape, LOW) for shape in shapes),
        in_specs=[tiled(pair[i // 2].shape) for i in range(4)],
        out_specs=tuple(tiled(shape) for shape in shapes),
        compiler_params=pltpu.CompilerParams(vmem_limit_bytes=40 << 20),
        cost_estimate=pl.CostEstimate(
            flops=0, bytes_accessed=8 * sum(a.size for a in pair), transcendentals=0
        ),
        name="join",
    )(pair[0], arrived[0], pair[1], arrived[1])
    return got[0] if stacked else got


def added(refs, at):
    total = refs[0][at].astype(FULL)
    for ref in refs[1:]:
        total = total + ref[at].astype(FULL)
    return total.astype(LOW)


def split_kernel(axes, first, *refs):
    ins, (kept_one, kept_two, sent_one, sent_two) = refs[:-4], refs[-4:]
    for stream, (kept_ref, sent_ref) in enumerate(((kept_one, sent_one), (kept_two, sent_two))):
        axis = axes[stream]
        for side, out_ref in ((1, sent_ref), (0, kept_ref)):
            at = [slice(None)] * len(out_ref.shape)
            at[axis] = slice(side, side + 1)
            if not first:
                out_ref[...] = added(ins[stream::2], tuple(at))
                continue
            for part in range(2):
                if axis == 0 and part != side:
                    continue
                arrived = ins[1 + 2 * stream + part]
                lead = slice(part, part + 1)
                inner = tuple(at[1:])
                total = ins[0][(stream, lead) + inner].astype(FULL)
                total = total + arrived[(slice(None),) + inner].astype(FULL)
                out_ref[(slice(0, 1) if axis == 0 else lead,)] = total.astype(LOW)


def split(arrays, axes, first):
    columns = arrays[0].shape[-1]
    tile = min(TILE, columns)
    outs, specs = [], []
    for stream in range(2):
        shape = list(arrays[0].shape[1:] if first else arrays[stream].shape)
        shape[axes[stream]] = 1
        outs.append(jax.ShapeDtypeStruct(tuple(shape), LOW))
        specs.append(pl.BlockSpec(tuple(shape[:-1]) + (tile,), column_block(len(shape))))
    got = pl.pallas_call(
        functools.partial(split_kernel, axes, first),
        grid=(columns // tile,),
        out_shape=tuple(outs * 2),
        in_specs=[
            pl.BlockSpec(array.shape[:-1] + (tile,), column_block(array.ndim)) for array in arrays
        ],
        out_specs=tuple(specs * 2),
        compiler_params=pltpu.CompilerParams(vmem_limit_bytes=40 << 20),
        cost_estimate=pl.CostEstimate(
            flops=0, bytes_accessed=3 * sum(a.size for a in arrays), transcendentals=0
        ),
        name="split",
    )(*arrays)
    return got[:2], got[2:]


def column_block(rank):
    return lambda i: (0,) * (rank - 1) + (i,)


def pieces_kernel(parts, *refs):
    ins, outs = refs[:4], refs[4:]
    count = len(outs)
    width = outs[0].shape[1] // (2 * parts)
    lead = (0,) * (len(ins[0].shape) - 2)
    for k in reversed(range(count)):
        for stream in range(2):
            for i in range(parts):
                source = (i * count + k) * width
                target = (stream * parts + i) * width
                outs[k][:, target : target + width] = added(
                    ins[stream::2], lead + (slice(None), slice(source, source + width))
                )


def to_pieces(kept, arrived, parts, count):
    rows, columns = kept[0].shape[-2:]
    out = jax.ShapeDtypeStruct((rows, 2 * columns // count), LOW)
    return small_kernel(
        functools.partial(pieces_kernel, parts), (out,) * count, *kept, *arrived, name="pieces"
    )


def total_of(addends):
    total = addends[0].astype(FULL)
    for array in addends[1:]:
        total = total + array.astype(FULL)
    return total.astype(LOW)


def after(values, *others):
    return lax.optimization_barrier((values, others))[0]


class Line:
    def __init__(self):
        self.last = None

    def wait(self, *arrays):
        self.last = (self.last, arrays)

    def __call__(self, kernel, *arrays, **rest):
        if self.last is not None:
            arrays = after(arrays, self.last)
        out = kernel(*arrays, **rest)
        leaves = jax.tree.leaves(out)
        self.last = min(leaves, key=lambda leaf: leaf.size)
        return out


def shards(
    mesh,
    tokens,
    lengths,
    routes,
    w_query,
    w_key,
    w_value,
    w_out,
    w_up,
    w_down,
    gain_attn,
    gain_mlp,
    w_router,
    cotangent,
):
    moves = Exchange(mesh)
    device = lax.axis_index("batch")
    column = lax.axis_index("tensor")
    seq_count, capacity = routes.shape
    features = tokens.shape[1]
    tokens = tokens.reshape(seq_count, -1, features)
    cotangent = cotangent.reshape(tokens.shape)

    repeats = max(1, moves.tensor // seq_count)
    local_count = max(1, seq_count // moves.tensor)
    first = column // repeats if repeats > 1 else column * local_count
    order = (first + jnp.arange(local_count)).astype(jnp.int32)
    counts_once = (column % repeats) == 0

    def once(values):
        return jnp.where(counts_once, values, jnp.zeros_like(values)) if repeats > 1 else values

    own = features // moves.batch
    place_block = jnp.asarray(moves.block_order(), jnp.int32)
    source = ((place_block ^ device)[:, None] * own + jnp.arange(own, dtype=jnp.int32)).reshape(-1)
    turn = (jnp.arange(features, dtype=jnp.int32)[:, None] == source[None, :]).astype(LOW)

    wide = w_query.shape[1]
    steps = len(moves.chips)
    shard_q = jnp.concatenate(
        [w_query.astype(LOW), w_key.astype(LOW), w_value.astype(LOW), w_out.astype(LOW).T], axis=1
    )
    shard_u = w_up.astype(LOW)
    shard_d = w_down.astype(LOW).T

    def ring(array, hops):
        pieces = [array]
        for _ in range(hops):
            pieces.append(moves.shift(pieces[-1], 1))
        return pieces

    hops = moves.tensor - 1
    line = Line()
    rows_total = local_count * capacity
    live_count = lax.dynamic_slice_in_dim(lengths, first, local_count) // 8

    def flat(array):
        return array.reshape(rows_total, features)

    def named(name, function, *arrays):
        with jax.named_scope(name):
            return function(*arrays)

    def axes_of(step):
        return tuple(moves.axis(stream, step) for stream in range(2))

    def gather(name, pair, step):
        arrived = named(name, moves.swap_step, pair, step)
        last = step == steps - 1
        return lambda: line(lambda *a: join(a[:2], a[2:], axes_of(step), last), *pair, *arrived)

    def whole(name, stacked):
        own_side = stacked.reshape(2, features // 2, stacked.shape[-1])
        return own_side, named(name, moves.swap, own_side, moves.core)

    def first_step(name, shard):
        half = shard.shape[1] // 2
        arrived = named(name, moves.swap_step, [shard[:, :half], shard[:, half:]], 0)
        return jnp.concatenate([shard, jnp.concatenate(arrived, axis=1)], axis=0)

    def doubled(pieces, parts):
        got = line(lambda *a: to_streams(a, parts, steps), *pieces)
        pair = []
        for stream, array in enumerate(got):
            lead = [1] * steps
            lead[moves.axis(stream, 0)] = 2
            pair.append(array.reshape(tuple(lead) + (array.shape[-2] // 2, array.shape[-1])))
        return pair

    def scatter(name, kept, *sent):
        shape = (2,) * steps + (own, kept.shape[-1])
        with jax.named_scope("core_" + name):
            arrays = [moves.swap(once(part), moves.core) for part in sent]
        arrays = [part.reshape((1,) + shape[1:]) for part in arrays]
        arrays, is_first = (once(kept).reshape((2,) + shape), *arrays), True
        for step in reversed(range(steps)):
            kept_pair, sent_pair = line(lambda *a: split(a, axes_of(step), is_first), *arrays)
            arrived = named(f"back{step}_" + name, moves.swap_step, sent_pair, step)
            arrays, is_first = (*kept_pair, *arrived), False
            yield None
        yield arrays

    def finish(name, arrays, parts):
        pieces = line(lambda *a: to_pieces(a[:2], a[2:], parts, moves.tensor), *arrays)
        total = pieces[-1]
        with jax.named_scope("z_" + name):
            for piece in reversed(pieces[:-1]):
                total = total_of([piece, moves.shift(total, -1)])
        return total

    def place_all(pieces, table):
        kept = pieces[::repeats] if repeats > 1 else pieces
        values = jnp.concatenate(
            [piece.reshape(local_count, capacity, features) for piece in kept], axis=0
        )
        owners = ((column - jnp.arange(0, moves.tensor, repeats)) % moves.tensor).astype(jnp.int32)
        if repeats > 1:
            places = owners // repeats
        else:
            places = (owners[:, None] * local_count + jnp.arange(local_count)).reshape(-1)
        return line(
            lambda v, t: place_rows(t, v, routes, places.astype(jnp.int32)), values, table
        ).reshape(-1, features)

    pieces_q = named("z_q", ring, shard_q, hops)
    wide_u = first_step("out0_u", shard_u)
    wide_d = first_step("out0_d", shard_d)
    small = jnp.stack([gain_attn, gain_mlp, w_router]).astype(LOW)
    small = named("small", moves.gather_small, small).astype(FULL)
    routed, cot_routed = pick_rows(tokens, cotangent, routes, order, local_count, turn)
    line.last = cot_routed
    routed, cot_routed = flat(routed), flat(cot_routed)
    pieces_q = after(pieces_q, small, wide_u, wide_d)
    pair_q = line(lambda *a: to_streams(a, 2, steps), *pieces_q)
    pieces_u = named("z_u", ring, after(wide_u, pieces_q[-1]), hops)
    for step in range(steps - 1):
        pair_q = gather(f"out{step}_q", pair_q, step)()
    joined_q = gather("last_q", pair_q, steps - 1)
    pair_u = doubled(pieces_u, 1)
    pieces_d = named("z_d", ring, after(wide_d, pieces_u[-1]), hops)
    for step in range(1, steps - 1):
        pair_u = gather(f"out{step}_u", pair_u, step)()
    joined_u = gather("last_u", pair_u, steps - 1)
    attn_weights = whole("core_q", joined_q())
    line.wait(pieces_d[1])
    attn_in, qkv, heads_out, attn_out, mlp_in, d_mlp_out = line(
        lambda *a: attend(*a[:4], a[4:], capacity), live_count, routed, cot_routed, small, *attn_weights
    )
    pair_d = doubled(pieces_d, 1)
    for step in range(1, steps - 1):
        pair_d = gather(f"out{step}_d", pair_d, step)()
    joined_d = gather("last_d", pair_d, steps - 1)
    ups = whole("core_u", joined_u())
    pre, hidden, *down_parts = line(
        lambda *a: up_layer(*a[:2], a[2:]), mlp_in, d_mlp_out, *ups
    )
    joined_d = joined_d()
    down_scatter = scatter("dn", *after(down_parts, joined_d))
    downs = whole("core_d", joined_d)
    next(down_scatter)
    update, d_mlp_in, dot, *up_parts = line(
        lambda *a: down_layer(*a[:8], a[8:10], a[10:12], a[12], a[13], capacity),
        live_count, routed, cot_routed, small, turn, attn_out, mlp_in, d_mlp_out, *ups, *downs, pre, hidden,
    )
    updates = named("z_update", ring, update, hops)
    for _ in range(steps - 1):
        next(down_scatter)
    up_scatter = scatter("up", *up_parts)
    next(up_scatter)
    d_routed, d_attn_out, d_qkv, small_grads = line(
        lambda *a: attend_back(*a[:9], a[9:], capacity),
        live_count, routed, cot_routed, small, turn, attn_out, d_mlp_in, dot, qkv, *attn_weights,
    )
    small_grads = lax.dot_general(
        small_grads, turn.astype(FULL), (((1,), (1,)), ((), ())), precision=lax.Precision.HIGHEST
    )
    small_grads = named("small", moves.sum_all, once(small_grads))
    small_grads = lax.dynamic_slice_in_dim(small_grads, device * own, own, axis=1)
    d_routeds = named("z_routed", ring, after(d_routed, updates[-1]), hops)
    line.wait(updates[1])
    attn_parts = line(attend_grads, attn_in, d_attn_out, heads_out, d_qkv)
    for _ in range(steps - 1):
        next(up_scatter)
    line.wait(updates[min(2, hops)])
    grad_d = finish("dn", next(down_scatter), 1)
    attn_scatter = scatter("qkvo", *attn_parts)
    next(attn_scatter)
    line.wait(d_routeds[1])
    output = place_all(updates, tokens)
    for _ in range(steps - 1):
        next(attn_scatter)
    line.wait(small_grads)
    grad_u = finish("up", next(up_scatter), 1)
    line.wait(grad_d)
    grad_tokens = place_all(d_routeds, cotangent)
    grad_q = finish("qkvo", next(attn_scatter), 2)

    return (
        output,
        grad_tokens,
        grad_q[:, :wide].astype(FULL),
        grad_q[:, wide : 2 * wide].astype(FULL),
        grad_q[:, 2 * wide : 3 * wide].astype(FULL),
        grad_q[:, 3 * wide :].T.astype(FULL),
        grad_u.astype(FULL),
        grad_d.T.astype(FULL),
        small_grads[0],
        small_grads[1],
        small_grads[2],
    )


def solution(mesh):
    in_specs = (
        P("batch", None),
        P("batch"),
        P("batch", None),
        P("batch", "tensor"),
        P("batch", "tensor"),
        P("batch", "tensor"),
        P("tensor", "batch"),
        P("batch", "tensor"),
        P("tensor", "batch"),
        P("batch"),
        P("batch"),
        P("batch"),
        P("batch", None),
    )
    out_specs = (
        P("batch", None),
        P("batch", None),
        P("batch", "tensor"),
        P("batch", "tensor"),
        P("batch", "tensor"),
        P("tensor", "batch"),
        P("batch", "tensor"),
        P("tensor", "batch"),
        P("batch"),
        P("batch"),
        P("batch"),
    )
    return jax.shard_map(
        functools.partial(shards, mesh),
        mesh=mesh,
        in_specs=in_specs,
        out_specs=out_specs,
        check_vma=False,
    )
```

```python
import functools

import jax
import jax.numpy as jnp
from jax import lax
from jax.experimental import pallas as pl
from jax.experimental.pallas import tpu as pltpu
from jax.sharding import PartitionSpec as P

HEAD_DIM = 64
SLOT_BLOCK = 512
PLACE_BLOCK = 2048
EPSILON = 1e-06


CURVE = 0.7978845608028654
CUBIC = 0.044715


def gelu_tanh(values):
    return 0.5 * values * (1.0 + jnp.tanh(CURVE * (values + CUBIC * values * values * values)))


def gelu_slope(values):
    square = values * values
    bend = jnp.tanh(CURVE * (values + CUBIC * values * square))
    inner = CURVE * (1.0 + 3.0 * CUBIC * square)
    return 0.5 * (1.0 + bend) + 0.5 * values * (1.0 - bend * bend) * inner


def product(left, right):
    return jnp.dot(left, right, preferred_element_type=jnp.float32)


def contract_rows(left, right):
    return lax.dot_general(
        left, right, (((0,), (0,)), ((), ())), preferred_element_type=jnp.float32
    )


def times_transposed(left, right):
    return lax.dot_general(
        left, right, (((1,), (1,)), ((), ())), preferred_element_type=jnp.float32
    )


def norm_backward(d_normed_in, normed, inverse, gain_vec):
    d_scaled = d_normed_in * gain_vec
    d_input = inverse * (d_scaled - normed * jnp.mean(d_scaled * normed, axis=-1, keepdims=True))
    return (d_input, jnp.sum(d_normed_in * normed, axis=0, keepdims=True))


def norm_forward(values):
    inverse = lax.rsqrt(jnp.mean(values * values, axis=-1, keepdims=True) + EPSILON)
    return (values * inverse, inverse)


LOW = jnp.bfloat16
FULL = jnp.float32


def pick_kernel(order_ref, routes_ref, turn_ref, tokens_ref, cot_ref, routed_ref, cot_routed_ref, total, cot_total):
    block = pl.program_id(1)
    capacity = routes_ref.shape[1]
    slots = tokens_ref.shape[1]
    column = lax.broadcasted_iota(jnp.int32, (capacity, slots), 1) + block * slots
    chooser = (routes_ref[0] == column).astype(LOW)
    part = product(chooser, tokens_ref[0])
    cot_part = product(chooser, cot_ref[0])

    @pl.when(block == 0)
    def _():
        total[...] = part
        cot_total[...] = cot_part

    @pl.when(block > 0)
    def _():
        total[...] += part
        cot_total[...] += cot_part

    @pl.when(block == pl.num_programs(1) - 1)
    def _():
        routed_ref[0] = product(total[...].astype(LOW), turn_ref[...]).astype(LOW)
        cot_routed_ref[0] = product(cot_total[...].astype(LOW), turn_ref[...]).astype(LOW)


def pick_rows(tokens, cotangent, routes, order, count, turn):
    seq_count, slots, features = tokens.shape
    capacity = routes.shape[1]
    per_block = min(SLOT_BLOCK, slots)
    table = pl.BlockSpec((1, per_block, features), lambda i, j, order: (order[i], j, 0))
    picked = pl.BlockSpec((1, capacity, features), lambda i, j, order: (i, 0, 0))
    shape = jax.ShapeDtypeStruct((count, capacity, features), LOW)
    return pl.pallas_call(
        pick_kernel,
        out_shape=(shape, shape),
        grid_spec=pltpu.PrefetchScalarGridSpec(
            num_scalar_prefetch=1,
            grid=(count, slots // per_block),
            in_specs=[
                pl.BlockSpec((1, capacity, 1), lambda i, j, order: (order[i], 0, 0)),
                pl.BlockSpec((features, features), lambda i, j, order: (0, 0)),
                table,
                table,
            ],
            out_specs=[picked, picked],
            scratch_shapes=[pltpu.VMEM((capacity, features), FULL)] * 2,
        ),
        compiler_params=pltpu.CompilerParams(vmem_limit_bytes=48 << 20),
        cost_estimate=pl.CostEstimate(
            flops=4 * count * capacity * slots * features,
            bytes_accessed=4 * count * slots * features,
            transcendentals=0,
        ),
        name="pick_rows",
    )(order, routes[:, :, None], turn, tokens, cotangent)


def place_kernel(order_ref, routes_ref, table_ref, values_ref, out_ref):
    block = pl.program_id(1)
    slots = table_ref.shape[1]
    capacity = routes_ref.shape[2]
    row = lax.broadcasted_iota(jnp.int32, (slots, capacity), 0) + block * slots
    chooser = (routes_ref[0] == row).astype(LOW)
    placed = product(chooser, values_ref[0])
    out_ref[0] = (table_ref[0].astype(FULL) + placed).astype(LOW)


def place_rows(table, values, routes, order):
    seq_count, slots, features = table.shape
    capacity = routes.shape[1]
    per_block = min(PLACE_BLOCK, slots)
    tall = pl.BlockSpec((1, per_block, features), lambda i, j, order: (order[i], j, 0))
    return pl.pallas_call(
        place_kernel,
        out_shape=jax.ShapeDtypeStruct(table.shape, table.dtype),
        grid_spec=pltpu.PrefetchScalarGridSpec(
            num_scalar_prefetch=1,
            grid=(seq_count, slots // per_block),
            in_specs=[
                pl.BlockSpec((1, 1, capacity), lambda i, j, order: (order[i], 0, 0)),
                tall,
                pl.BlockSpec((1, capacity, features), lambda i, j, order: (i, 0, 0)),
            ],
            out_specs=tall,
        ),
        compiler_params=pltpu.CompilerParams(vmem_limit_bytes=56 << 20),
        cost_estimate=pl.CostEstimate(
            flops=2 * seq_count * capacity * slots * features,
            bytes_accessed=4 * seq_count * slots * features,
            transcendentals=0,
        ),
        name="place_rows",
    )(order, routes[:, None, :], table, values)


def gates(routed, router_vec, live_ref, capacity):
    rows = routed.shape[0]
    score = jnp.sum(routed * router_vec, axis=-1, keepdims=True)
    gate_prob = 1.0 / (1.0 + jnp.exp(-score))
    live = [
        lax.broadcasted_iota(jnp.int32, (capacity, 1), 0) < live_ref[seq]
        for seq in range(rows // capacity)
    ]
    live = live[0] if len(live) == 1 else jnp.concatenate(live, axis=0)
    return gate_prob, jnp.where(live, gate_prob, 0.0)


def probabilities(queries, keys_all, live_count, scale_qk):
    scores = times_transposed(queries, keys_all) * scale_qk
    row = lax.broadcasted_iota(jnp.int32, scores.shape, 0)
    column = lax.broadcasted_iota(jnp.int32, scores.shape, 1)
    masked = jnp.where((column <= row) & (column < live_count), scores, -1e30)
    exp_scores = jnp.exp(masked - jnp.max(masked, axis=-1, keepdims=True))
    return exp_scores / jnp.sum(exp_scores, axis=-1, keepdims=True)


def split_heads(pair):
    owner = lax.broadcasted_iota(jnp.int32, pair.shape, 1) // HEAD_DIM
    return [jnp.where(owner == i, pair, jnp.zeros_like(pair)) for i in range(pair.shape[1] // HEAD_DIM)]


def attend_kernel(
    capacity, live_ref, routed_ref, cot_ref, small_ref, own, other,
    attn_in_ref, qkv_ref, heads_ref, attn_out_ref, mlp_in_ref, d_mlp_out_ref,
):
    routed = routed_ref[...].astype(FULL)
    rows, features = routed.shape
    half = features // 2
    wide = qkv_ref.shape[1] // 3
    _, gate_live = gates(routed, small_ref[2:3], live_ref, capacity)
    d_mlp_out_ref[...] = (gate_live * cot_ref[...].astype(FULL)).astype(LOW)
    normed, _ = norm_forward(routed)
    attn_in = (normed * small_ref[0:1]).astype(LOW)
    attn_in_ref[...] = attn_in
    left, right = attn_in[:, :half], attn_in[:, half:]
    qkv_ref[:, : 2 * wide] = (product(left, own[0]) + product(right, other[0])).astype(LOW)
    qkv_ref[:, 2 * wide :] = (
        product(left, own[1, :, :wide]) + product(right, other[1, :, :wide])
    ).astype(LOW)
    tile = 2 * HEAD_DIM
    for seq in range(rows // capacity):
        at = slice(seq * capacity, (seq + 1) * capacity)
        for start in range(0, wide, tile):
            keys_all = qkv_ref[at, wide + start : wide + start + tile]
            queries = split_heads(qkv_ref[at, start : start + tile])
            vals = split_heads(qkv_ref[at, 2 * wide + start : 2 * wide + start + tile])
            total = None
            for query, val in zip(queries, vals):
                probs = probabilities(query, keys_all, live_ref[seq], HEAD_DIM ** (-0.5))
                part = product(probs.astype(LOW), val)
                total = part if total is None else total + part
            heads_ref[at, start : start + tile] = total.astype(LOW)
    heads_out = heads_ref[...]
    attn_out_ref[:, :half] = times_transposed(heads_out, own[1, :, wide:])
    attn_out_ref[:, half:] = times_transposed(heads_out, other[1, :, wide:])
    normed_two, _ = norm_forward(routed + attn_out_ref[...])
    mlp_in_ref[...] = (normed_two * small_ref[1:2]).astype(LOW)


def whole_specs(count):
    return [pl.BlockSpec(memory_space=pltpu.VMEM)] * count


def attend(live_count, routed, cot_routed, small, weights, capacity):
    rows, features = routed.shape
    wide = weights[0].shape[2] // 2
    return pl.pallas_call(
        functools.partial(attend_kernel, capacity),
        out_shape=(
            jax.ShapeDtypeStruct((rows, features), LOW),
            jax.ShapeDtypeStruct((rows, 3 * wide), LOW),
            jax.ShapeDtypeStruct((rows, wide), LOW),
            jax.ShapeDtypeStruct((rows, features), FULL),
            jax.ShapeDtypeStruct((rows, features), LOW),
            jax.ShapeDtypeStruct((rows, features), LOW),
        ),
        in_specs=[pl.BlockSpec(memory_space=pltpu.SMEM)] + whole_specs(5),
        out_specs=tuple(whole_specs(6)),
        compiler_params=pltpu.CompilerParams(vmem_limit_bytes=56 << 20),
        cost_estimate=pl.CostEstimate(
            flops=8 * rows * features * wide + 4 * rows * capacity * wide,
            bytes_accessed=8 * features * wide + 14 * rows * features,
            transcendentals=rows * capacity * wide // HEAD_DIM,
        ),
        name="attend",
    )(live_count, routed, cot_routed, small, *weights)


def up_kernel(mlp_in_ref, d_mlp_out_ref, own, other, pre_ref, hidden_ref, kept_ref, sent_ref):
    mlp_in = mlp_in_ref[...]
    d_mlp_out = d_mlp_out_ref[...]
    half = mlp_in.shape[1] // 2
    for stream in range(2):
        pre = product(mlp_in[:, :half], own[stream]) + product(mlp_in[:, half:], other[stream])
        hidden = gelu_tanh(pre).astype(LOW)
        pre_ref[stream] = pre
        hidden_ref[stream] = hidden
        sent_ref[stream] = contract_rows(d_mlp_out[:, half:], hidden).astype(LOW)
        kept_ref[stream] = contract_rows(d_mlp_out[:, :half], hidden).astype(LOW)


TILE = 512


def up_layer(mlp_in, d_mlp_out, ups):
    rows, features = mlp_in.shape
    streams, half, width = ups[0].shape
    tile = min(TILE, width)
    whole = pl.BlockSpec((rows, features), lambda i: (0, 0))
    weight = pl.BlockSpec((streams, half, tile), lambda i: (0, 0, i))
    tall = pl.BlockSpec((streams, rows, tile), lambda i: (0, 0, i))
    return pl.pallas_call(
        up_kernel,
        grid=(width // tile,),
        out_shape=(
            jax.ShapeDtypeStruct((streams, rows, width), FULL),
            jax.ShapeDtypeStruct((streams, rows, width), LOW),
            jax.ShapeDtypeStruct(ups[0].shape, LOW),
            jax.ShapeDtypeStruct(ups[0].shape, LOW),
        ),
        in_specs=[whole, whole, weight, weight],
        out_specs=(tall, tall, weight, weight),
        compiler_params=pltpu.CompilerParams(vmem_limit_bytes=56 << 20),
        cost_estimate=pl.CostEstimate(
            flops=8 * rows * features * width,
            bytes_accessed=8 * features * width + 12 * rows * width,
            transcendentals=2 * rows * width,
        ),
        name="up_layer",
    )(mlp_in, d_mlp_out, *ups)


def down_kernel(
    capacity, live_ref, routed_ref, cot_ref, small_ref, turn_ref, attn_out_ref, mlp_in_ref, d_mlp_out_ref,
    up_own, up_other, down_own, down_other, pre_ref, hidden_ref,
    update_ref, d_mlp_in_ref, dot_ref, kept_ref, sent_ref, mlp_out,
):
    mlp_in = mlp_in_ref[...]
    d_mlp_out = d_mlp_out_ref[...]
    half = mlp_in.shape[1] // 2

    @pl.when(pl.program_id(0) == 0)
    def _():
        mlp_out[...] = jnp.zeros_like(mlp_out)
        d_mlp_in_ref[...] = jnp.zeros_like(d_mlp_in_ref)

    for stream in range(2):
        d_hidden = product(d_mlp_out[:, :half], down_own[stream]) + product(
            d_mlp_out[:, half:], down_other[stream]
        )
        d_pre = (d_hidden * gelu_slope(pre_ref[stream])).astype(LOW)
        sent_ref[stream] = contract_rows(mlp_in[:, half:], d_pre).astype(LOW)
        kept_ref[stream] = contract_rows(mlp_in[:, :half], d_pre).astype(LOW)
        d_mlp_in_ref[:, :half] += times_transposed(d_pre, up_own[stream])
        d_mlp_in_ref[:, half:] += times_transposed(d_pre, up_other[stream])
        hidden = hidden_ref[stream]
        mlp_out[:, :half] += times_transposed(hidden, down_own[stream])
        mlp_out[:, half:] += times_transposed(hidden, down_other[stream])

    @pl.when(pl.program_id(0) == pl.num_programs(0) - 1)
    def _():
        _, gate_live = gates(routed_ref[...].astype(FULL), small_ref[2:3], live_ref, capacity)
        branch = attn_out_ref[...] + mlp_out[...]
        update = (gate_live * branch).astype(LOW)
        update_ref[...] = times_transposed(update, turn_ref[...]).astype(LOW)
        dot_ref[...] = jnp.sum(cot_ref[...].astype(FULL) * branch, axis=-1, keepdims=True)


def down_layer(live_count, routed, cot_routed, small, turn, attn_out, mlp_in, d_mlp_out, ups, downs, pre, hidden, capacity):
    rows, features = mlp_in.shape
    streams, half, width = ups[0].shape
    tile = min(TILE, width)
    whole = pl.BlockSpec((rows, features), lambda i: (0, 0))
    weight = pl.BlockSpec((streams, half, tile), lambda i: (0, 0, i))
    tall = pl.BlockSpec((streams, rows, tile), lambda i: (0, 0, i))
    return pl.pallas_call(
        functools.partial(down_kernel, capacity),
        grid=(width // tile,),
        out_shape=(
            jax.ShapeDtypeStruct((rows, features), LOW),
            jax.ShapeDtypeStruct((rows, features), FULL),
            jax.ShapeDtypeStruct((rows, 1), FULL),
            jax.ShapeDtypeStruct(ups[0].shape, LOW),
            jax.ShapeDtypeStruct(ups[0].shape, LOW),
        ),
        in_specs=[
            pl.BlockSpec(memory_space=pltpu.SMEM),
            whole,
            whole,
            pl.BlockSpec(small.shape, lambda i: (0, 0)),
            pl.BlockSpec(turn.shape, lambda i: (0, 0)),
            whole,
            whole,
            whole,
        ]
        + [weight] * 4
        + [tall] * 2,
        out_specs=(whole, whole, pl.BlockSpec((rows, 1), lambda i: (0, 0)), weight, weight),
        scratch_shapes=[pltpu.VMEM((rows, features), FULL)],
        compiler_params=pltpu.CompilerParams(vmem_limit_bytes=56 << 20),
        cost_estimate=pl.CostEstimate(
            flops=16 * rows * features * width,
            bytes_accessed=12 * features * width + 12 * rows * width,
            transcendentals=2 * rows * width,
        ),
        name="down_layer",
    )(live_count, routed, cot_routed, small, turn, attn_out, mlp_in, d_mlp_out, *ups, *downs, pre, hidden)


def attend_back_kernel(
    capacity, live_ref, routed_ref, cot_ref, small_ref, turn_ref, attn_out_ref, d_mlp_in_ref, dot_ref, qkv_ref,
    own, other, d_routed_ref, d_attn_out_ref, d_qkv_ref, small_grads_ref, d_heads_ref,
):
    routed = routed_ref[...].astype(FULL)
    rows, features = routed.shape
    half = features // 2
    wide = qkv_ref.shape[1] // 3
    scale_qk = HEAD_DIM ** (-0.5)
    gate_prob, gate_live = gates(routed, small_ref[2:3], live_ref, capacity)
    normed_two, inverse_two = norm_forward(routed + attn_out_ref[...])
    d_middle, small_grads_ref[1:2] = norm_backward(
        d_mlp_in_ref[...], normed_two, inverse_two, small_ref[1:2]
    )
    d_attn_out = (d_middle + gate_live * cot_ref[...].astype(FULL)).astype(LOW)
    d_attn_out_ref[...] = d_attn_out
    d_heads_ref[...] = (
        product(d_attn_out[:, :half], own[1, :, wide:]) + product(d_attn_out[:, half:], other[1, :, wide:])
    ).astype(LOW)
    tile = 2 * HEAD_DIM
    for seq in range(rows // capacity):
        at = slice(seq * capacity, (seq + 1) * capacity)
        for start in range(0, wide, tile):
            query_pair = qkv_ref[at, start : start + tile]
            key_pair = qkv_ref[at, wide + start : wide + start + tile]
            val_pair = qkv_ref[at, 2 * wide + start : 2 * wide + start + tile]
            d_query, d_key, d_val = 0.0, 0.0, 0.0
            for query, key, d_head in zip(
                split_heads(query_pair), split_heads(key_pair), split_heads(d_heads_ref[at, start : start + tile])
            ):
                probs = probabilities(query, key_pair, live_ref[seq], scale_qk)
                d_val = d_val + contract_rows(probs.astype(LOW), d_head)
                d_probs = times_transposed(d_head, val_pair)
                d_scores = (
                    probs * (d_probs - jnp.sum(d_probs * probs, axis=-1, keepdims=True))
                ).astype(LOW)
                d_query = d_query + product(d_scores, key)
                d_key = d_key + contract_rows(d_scores, query)
            d_qkv_ref[at, start : start + tile] = (d_query * scale_qk).astype(LOW)
            d_qkv_ref[at, wide + start : wide + start + tile] = (d_key * scale_qk).astype(LOW)
            d_qkv_ref[at, 2 * wide + start : 2 * wide + start + tile] = d_val.astype(LOW)
    d_both = d_qkv_ref[:, : 2 * wide]
    d_vals = d_qkv_ref[:, 2 * wide :]
    d_attn_in = jnp.concatenate(
        [
            times_transposed(d_both, side[0]) + times_transposed(d_vals, side[1, :, :wide])
            for side in (own, other)
        ],
        axis=1,
    )
    normed_one, inverse_one = norm_forward(routed)
    d_from_norm, small_grads_ref[0:1] = norm_backward(d_attn_in, normed_one, inverse_one, small_ref[0:1])
    d_score = gate_live * (1.0 - gate_prob) * dot_ref[...]
    small_grads_ref[2:3] = jnp.sum(routed * d_score, axis=0, keepdims=True)
    d_routed = (d_middle + d_from_norm + d_score * small_ref[2:3]).astype(LOW)
    d_routed_ref[...] = times_transposed(d_routed, turn_ref[...]).astype(LOW)


def attend_back(live_count, routed, cot_routed, small, turn, attn_out, d_mlp_in, dot, qkv, weights, capacity):
    rows, features = routed.shape
    wide = weights[0].shape[2] // 2
    return pl.pallas_call(
        functools.partial(attend_back_kernel, capacity),
        out_shape=(
            jax.ShapeDtypeStruct((rows, features), LOW),
            jax.ShapeDtypeStruct((rows, features), LOW),
            jax.ShapeDtypeStruct((rows, 3 * wide), LOW),
            jax.ShapeDtypeStruct((3, features), FULL),
        ),
        in_specs=[pl.BlockSpec(memory_space=pltpu.SMEM)] + whole_specs(10),
        out_specs=tuple(whole_specs(4)),
        scratch_shapes=[pltpu.VMEM((rows, wide), LOW)],
        compiler_params=pltpu.CompilerParams(vmem_limit_bytes=56 << 20),
        cost_estimate=pl.CostEstimate(
            flops=8 * rows * features * wide + 10 * rows * capacity * wide,
            bytes_accessed=8 * features * wide + 14 * rows * features,
            transcendentals=rows * capacity * wide // HEAD_DIM,
        ),
        name="attend_back",
    )(live_count, routed, cot_routed, small, turn, attn_out, d_mlp_in, dot, qkv, *weights)


def grads_kernel(attn_in_ref, d_attn_out_ref, heads_ref, d_qkv_ref, kept_ref, sent_ref):
    half = attn_in_ref.shape[1] // 2
    wide = heads_ref.shape[1]
    for at, out_ref in ((slice(half, 2 * half), sent_ref), (slice(0, half), kept_ref)):
        attn_in = attn_in_ref[:, at]
        out_ref[0] = contract_rows(attn_in, d_qkv_ref[:, : 2 * wide]).astype(LOW)
        out_ref[1, :, :wide] = contract_rows(attn_in, d_qkv_ref[:, 2 * wide :]).astype(LOW)
        out_ref[1, :, wide:] = contract_rows(d_attn_out_ref[:, at], heads_ref[...]).astype(LOW)


def attend_grads(attn_in, d_attn_out, heads_out, d_qkv):
    rows, features = attn_in.shape
    wide = heads_out.shape[1]
    return pl.pallas_call(
        grads_kernel,
        out_shape=(jax.ShapeDtypeStruct((2, features // 2, 2 * wide), LOW),) * 2,
        in_specs=whole_specs(4),
        out_specs=tuple(whole_specs(2)),
        compiler_params=pltpu.CompilerParams(vmem_limit_bytes=56 << 20),
        cost_estimate=pl.CostEstimate(
            flops=8 * rows * features * wide,
            bytes_accessed=8 * features * wide + 8 * rows * features,
            transcendentals=0,
        ),
        name="attend_grads",
    )(attn_in, d_attn_out, heads_out, d_qkv)


class Exchange:
    def __init__(self, mesh):
        self.batch = mesh.shape["batch"]
        self.tensor = mesh.shape["tensor"]
        bits = []
        bit = self.batch // 2
        while bit:
            bits.append(bit)
            bit //= 2
        self.core = bits[-1]
        self.chips = bits[:-1]

    def swap(self, array, bit):
        with jax.named_scope(f"swap{bit}"):
            return lax.ppermute(array, "batch", [(i, i ^ bit) for i in range(self.batch)])

    def shift(self, array, step):
        size = self.tensor
        with jax.named_scope(f"shift{step}"):
            return lax.ppermute(array, "tensor", [(i, (i + step) % size) for i in range(size)])

    def block_order(self):
        order = [0]
        for bit in reversed([self.core] + self.chips):
            order = order + [place ^ bit for place in order]
        return order

    def gather_small(self, array):
        total = array[None]
        for bit in reversed([self.core] + self.chips):
            total = jnp.concatenate([total, self.swap(total, bit)], axis=0)
        return total.transpose(1, 0, 2).reshape(array.shape[0], -1)

    def axis(self, stream, step):
        return step if stream else len(self.chips) - 1 - step

    def swap_step(self, pair, step):
        return [self.swap(array, self.chips[self.axis(i, step)]) for i, array in enumerate(pair)]


def small_kernel(kernel, out_shape, *arrays, name):
    return pl.pallas_call(
        kernel,
        out_shape=out_shape,
        in_specs=whole_specs(len(arrays)),
        out_specs=tuple(whole_specs(len(out_shape))),
        compiler_params=pltpu.CompilerParams(vmem_limit_bytes=40 << 20),
        cost_estimate=pl.CostEstimate(
            flops=0, bytes_accessed=4 * sum(a.size for a in arrays), transcendentals=0
        ),
        name=name,
    )(*arrays)


def streams_kernel(parts, *refs):
    pieces, outs = refs[:-2], refs[-2:]
    count = len(pieces)
    width = pieces[0].shape[1] // (2 * parts)
    for stream, out_ref in enumerate(outs):
        lead = (0,) * (len(out_ref.shape) - 2)
        for i in range(parts):
            source = (stream * parts + i) * width
            for k, piece in enumerate(pieces):
                target = (i * count + k) * width
                out_ref[lead + (slice(None), slice(target, target + width))] = piece[
                    :, source : source + width
                ]


def to_streams(pieces, parts, places):
    rows, columns = pieces[0].shape
    shape = (1,) * places + (rows, columns * len(pieces) // 2)
    out = jax.ShapeDtypeStruct(shape, pieces[0].dtype)
    return small_kernel(functools.partial(streams_kernel, parts), (out, out), *pieces, name="streams")


def join_kernel(axes, stacked, *refs):
    ins, outs = refs[:4], refs[4:]
    for stream in range(2):
        for side in range(2):
            source = ins[2 * stream + side]
            at = [slice(None)] * len(source.shape)
            size = source.shape[axes[stream]]
            at[axes[stream]] = slice(side * size, (side + 1) * size)
            if stacked:
                outs[0][(stream,) + tuple(at)] = source[...]
            else:
                outs[stream][tuple(at)] = source[...]


def join(pair, arrived, axes, stacked):
    columns = pair[0].shape[-1]
    tile = min(TILE, columns)
    shapes = []
    for array, axis in zip(pair, axes):
        shape = list(array.shape)
        shape[axis] *= 2
        shapes.append(tuple(shape))
    if stacked:
        shapes = [(2,) + shapes[0]]

    def tiled(shape):
        return pl.BlockSpec(tuple(shape[:-1]) + (tile,), column_block(len(shape)))

    got = pl.pallas_call(
        functools.partial(join_kernel, axes, stacked),
        grid=(columns // tile,),
        out_shape=tuple(jax.ShapeDtypeStruct(shape, LOW) for shape in shapes),
        in_specs=[tiled(pair[i // 2].shape) for i in range(4)],
        out_specs=tuple(tiled(shape) for shape in shapes),
        compiler_params=pltpu.CompilerParams(vmem_limit_bytes=40 << 20),
        cost_estimate=pl.CostEstimate(
            flops=0, bytes_accessed=8 * sum(a.size for a in pair), transcendentals=0
        ),
        name="join",
    )(pair[0], arrived[0], pair[1], arrived[1])
    return got[0] if stacked else got


def added(refs, at):
    total = refs[0][at].astype(FULL)
    for ref in refs[1:]:
        total = total + ref[at].astype(FULL)
    return total.astype(LOW)


def split_kernel(axes, stacked, *refs):
    ins, (kept_one, kept_two, sent_one, sent_two) = refs[:-4], refs[-4:]
    for stream, (kept_ref, sent_ref) in enumerate(((kept_one, sent_one), (kept_two, sent_two))):
        sources = ins if stacked else ins[stream::2]
        for side, out_ref in ((1, sent_ref), (0, kept_ref)):
            at = [slice(None)] * len(out_ref.shape)
            at[axes[stream]] = slice(side, side + 1)
            at = ((stream,) if stacked else ()) + tuple(at)
            out_ref[...] = added(sources, at)


def split(arrays, axes, stacked):
    full = arrays[0].shape[1:] if stacked else arrays[0].shape
    columns = full[-1]
    tile = min(TILE, columns)
    outs, specs = [], []
    for stream in range(2):
        shape = list(full if stacked else arrays[stream].shape)
        shape[axes[stream]] = 1
        outs.append(jax.ShapeDtypeStruct(tuple(shape), LOW))
        specs.append(pl.BlockSpec(tuple(shape[:-1]) + (tile,), column_block(len(shape))))
    got = pl.pallas_call(
        functools.partial(split_kernel, axes, stacked),
        grid=(columns // tile,),
        out_shape=tuple(outs * 2),
        in_specs=[
            pl.BlockSpec(array.shape[:-1] + (tile,), column_block(array.ndim)) for array in arrays
        ],
        out_specs=tuple(specs * 2),
        compiler_params=pltpu.CompilerParams(vmem_limit_bytes=40 << 20),
        cost_estimate=pl.CostEstimate(
            flops=0, bytes_accessed=3 * sum(a.size for a in arrays), transcendentals=0
        ),
        name="split",
    )(*arrays)
    return got[:2], got[2:]


def column_block(rank):
    return lambda i: (0,) * (rank - 1) + (i,)


def pieces_kernel(parts, *refs):
    ins, outs = refs[:4], refs[4:]
    count = len(outs)
    width = outs[0].shape[1] // (2 * parts)
    lead = (0,) * (len(ins[0].shape) - 2)
    for k in reversed(range(count)):
        for stream in range(2):
            for i in range(parts):
                source = (i * count + k) * width
                target = (stream * parts + i) * width
                outs[k][:, target : target + width] = added(
                    ins[stream::2], lead + (slice(None), slice(source, source + width))
                )


def to_pieces(kept, arrived, parts, count):
    rows, columns = kept[0].shape[-2:]
    out = jax.ShapeDtypeStruct((rows, 2 * columns // count), LOW)
    return small_kernel(
        functools.partial(pieces_kernel, parts), (out,) * count, *kept, *arrived, name="pieces"
    )


def total_of(addends):
    total = addends[0].astype(FULL)
    for array in addends[1:]:
        total = total + array.astype(FULL)
    return total.astype(LOW)


def after(values, *others):
    return lax.optimization_barrier((values, others))[0]


class Line:
    def __init__(self):
        self.last = None

    def wait(self, *arrays):
        self.last = (self.last, arrays)

    def __call__(self, kernel, *arrays, **rest):
        if self.last is not None:
            arrays = after(arrays, self.last)
        out = kernel(*arrays, **rest)
        leaves = jax.tree.leaves(out)
        self.last = min(leaves, key=lambda leaf: leaf.size)
        return out


def shards(
    mesh,
    tokens,
    lengths,
    routes,
    w_query,
    w_key,
    w_value,
    w_out,
    w_up,
    w_down,
    gain_attn,
    gain_mlp,
    w_router,
    cotangent,
):
    moves = Exchange(mesh)
    device = lax.axis_index("batch")
    column = lax.axis_index("tensor")
    seq_count, capacity = routes.shape
    features = tokens.shape[1]
    tokens = tokens.reshape(seq_count, -1, features)
    cotangent = cotangent.reshape(tokens.shape)

    repeats = max(1, moves.tensor // seq_count)
    local_count = max(1, seq_count // moves.tensor)
    first = column // repeats if repeats > 1 else column * local_count
    order = (first + jnp.arange(local_count)).astype(jnp.int32)
    counts_once = (column % repeats) == 0

    def once(values):
        return jnp.where(counts_once, values, jnp.zeros_like(values)) if repeats > 1 else values

    own = features // moves.batch
    place_block = jnp.asarray(moves.block_order(), jnp.int32)
    source = ((place_block ^ device)[:, None] * own + jnp.arange(own, dtype=jnp.int32)).reshape(-1)
    turn = (jnp.arange(features, dtype=jnp.int32)[:, None] == source[None, :]).astype(LOW)

    wide = w_query.shape[1]
    steps = len(moves.chips)
    shard_q = jnp.concatenate(
        [w_query.astype(LOW), w_key.astype(LOW), w_value.astype(LOW), w_out.astype(LOW).T], axis=1
    )
    shard_u = w_up.astype(LOW)
    shard_d = w_down.astype(LOW).T

    def ring(array, hops):
        pieces = [array]
        for _ in range(hops):
            pieces.append(moves.shift(pieces[-1], 1))
        return pieces

    hops = moves.tensor - 1
    line = Line()
    rows_total = local_count * capacity
    live_count = lax.dynamic_slice_in_dim(lengths, first, local_count) // 8

    def flat(array):
        return array.reshape(rows_total, features)

    def named(name, function, *arrays):
        with jax.named_scope(name):
            return function(*arrays)

    def axes_of(step):
        return tuple(moves.axis(stream, step) for stream in range(2))

    def gather(name, pair, step):
        arrived = named(name, moves.swap_step, pair, step)
        last = step == steps - 1
        return lambda: line(lambda *a: join(a[:2], a[2:], axes_of(step), last), *pair, *arrived)

    def whole(name, stacked):
        own_side = stacked.reshape(2, features // 2, stacked.shape[-1])
        return own_side, named(name, moves.swap, own_side, moves.core)

    def first_step(name, shard):
        half = shard.shape[1] // 2
        arrived = named(name, moves.swap_step, [shard[:, :half], shard[:, half:]], 0)
        return jnp.concatenate([shard, jnp.concatenate(arrived, axis=1)], axis=0)

    def doubled(pieces, parts):
        got = line(lambda *a: to_streams(a, parts, steps), *pieces)
        pair = []
        for stream, array in enumerate(got):
            lead = [1] * steps
            lead[moves.axis(stream, 0)] = 2
            pair.append(array.reshape(tuple(lead) + (array.shape[-2] // 2, array.shape[-1])))
        return pair

    def wide_open(array):
        return once(array).reshape((2,) + (2,) * steps + (own, array.shape[-1]))

    def split_step(arrays, step, stacked):
        return split(arrays, axes_of(step), stacked)

    def together(*values):
        return lax.optimization_barrier(values)

    def place_all(pieces, table):
        kept = pieces[::repeats] if repeats > 1 else pieces
        values = jnp.concatenate(
            [piece.reshape(local_count, capacity, features) for piece in kept], axis=0
        )
        owners = ((column - jnp.arange(0, moves.tensor, repeats)) % moves.tensor).astype(jnp.int32)
        if repeats > 1:
            places = owners // repeats
        else:
            places = (owners[:, None] * local_count + jnp.arange(local_count)).reshape(-1)
        return place_rows(table, values, routes, places.astype(jnp.int32)).reshape(-1, features)

    ahead = moves.tensor // 2

    def out_both(name, array):
        with jax.named_scope("z_" + name):
            onward = [array, moves.shift(array, 1)]
            behind = [array]
            for _ in range(moves.tensor - 1 - ahead):
                behind.append(moves.shift(behind[-1], -1))
        return onward, behind[:0:-1]

    def out_on(name, onward, behind):
        onward = list(onward)
        with jax.named_scope("z_" + name):
            for _ in range(ahead - 1):
                onward.append(moves.shift(onward[-1], 1))
        return onward + list(behind)

    def sum_both(name, pieces):
        with jax.named_scope("z_" + name):
            fore = pieces[ahead + 1] if ahead + 1 < moves.tensor else jnp.zeros_like(pieces[0])
            for piece in pieces[ahead + 2 :]:
                fore = total_of([piece, moves.shift(fore, 1)])
            if ahead + 1 < moves.tensor:
                fore = moves.shift(fore, 1)
            back = None
            for piece in pieces[ahead:1:-1]:
                back = moves.shift(piece if back is None else total_of([piece, back]), -1)
        return fore, pieces[1] if back is None else total_of([pieces[1], back])

    def sum_on(name, back):
        with jax.named_scope("z_" + name):
            return moves.shift(back, -1)

    both_q = out_both("q", shard_q)
    routed, cot_routed = pick_rows(tokens, cotangent, routes, order, local_count, turn)
    line.last = cot_routed
    both_q = after(both_q, cot_routed)
    pieces_q = out_on("q", *both_q)
    routed, cot_routed = flat(routed), flat(cot_routed)
    wide_d = first_step("out0_d", after(shard_d, shard_q))
    small = after(jnp.stack([gain_attn, gain_mlp, w_router]).astype(LOW), both_q[0][1])
    small = named("small", moves.gather_small, small).astype(FULL)
    pieces_q = after(pieces_q, small, wide_d)
    pair_q = line(lambda *a: to_streams(a, 2, steps), *pieces_q)
    both_u = out_both("u", after(shard_u, pieces_q))
    pieces_u = out_on("u", *both_u)
    line.wait(both_u)
    for step in range(steps - 1):
        pair_q = gather(f"out{step}_q", pair_q, step)()
    joined_q = gather("last_q", pair_q, steps - 1)
    pair_u = line(lambda *a: to_streams(a, 1, steps), *pieces_u)
    joined_u = gather("out0_u", pair_u, 0)
    both_d = out_both("d", after(wide_d, pieces_u))
    pieces_d = out_on("d", *both_d)
    attn_weights = whole("core_q", joined_q())
    line.wait(both_d)
    for step in range(1, steps):
        joined_u = gather(f"out{step}_u", joined_u(), step)
    attn_in, qkv, heads_out, attn_out, mlp_in, d_mlp_out = line(
        lambda *a: attend(*a[:4], a[4:], capacity), live_count, routed, cot_routed, small, *attn_weights
    )
    pair_d = doubled(pieces_d, 1)
    for step in range(1, steps - 1):
        pair_d = gather(f"out{step}_d", pair_d, step)()
    joined_d = gather("last_d", pair_d, steps - 1)
    ups = whole("core_u", joined_u())
    pre, hidden, dn_kept, dn_sent = line(
        lambda *a: up_layer(*a[:2], a[2:]), mlp_in, d_mlp_out, *ups
    )
    joined_d = joined_d()

    joined_d, dn_kept, dn_sent = together(joined_d, dn_kept, dn_sent)
    dn_arrived = named("core_dn", moves.swap, once(dn_sent), moves.core)
    downs = whole("core_d", joined_d)
    dn = (wide_open(dn_kept), wide_open(dn_arrived))

    last = steps - 1
    dn_kept, dn_sent = split_step(dn, last, True)
    dn_sent, *rest = after((dn_sent, mlp_in, pre, hidden), downs)
    dn_sent, rest = together(dn_sent, rest)
    dn_arrived = named("back_dn", moves.swap_step, dn_sent, last)
    update, d_mlp_in, dot, up_kept, up_sent = down_layer(
        live_count, routed, cot_routed, small, turn, attn_out, rest[0], d_mlp_out, ups, downs, *rest[1:], capacity
    )
    dn = (*dn_kept, *dn_arrived)
    for step in reversed(range(1, last)):
        dn_kept, dn_sent = split_step(dn, step, False)
        dn = (*dn_kept, *named("back_dn", moves.swap_step, dn_sent, step))

    dn, update, d_mlp_in, dot, up_kept, up_sent = together(dn, update, d_mlp_in, dot, up_kept, up_sent)
    up_arrived = named("core_up", moves.swap, once(up_sent), moves.core)
    dn_kept, dn_sent = split_step(dn, 0, False)
    dn = (*dn_kept, *named("back0_dn", moves.swap_step, dn_sent, 0))
    with jax.named_scope("z_update"):
        next_update = moves.shift(update, 1)

    up_kept, up_arrived, dn, update, next_update, d_mlp_in, dot = together(
        up_kept, up_arrived, dn, update, next_update, d_mlp_in, dot
    )
    up_kept, up_sent = split_step((wide_open(up_kept), wide_open(up_arrived)), last, True)
    up = (*up_kept, *named("back1_up", moves.swap_step, up_sent, last))
    behind = [update]
    with jax.named_scope("z_update"):
        for _ in range(moves.tensor - 1 - ahead):
            behind.append(moves.shift(behind[-1], -1))
    updates = out_on("update", (update, next_update), behind[:0:-1])
    d_routed, d_attn_out, d_qkv, small_grads = attend_back(
        live_count, routed, cot_routed, small, turn, attn_out, d_mlp_in, dot, qkv, attn_weights, capacity
    )
    q_kept, q_sent = attend_grads(attn_in, d_attn_out, heads_out, d_qkv)
    for step in reversed(range(1, last)):
        up_kept, up_sent = split_step(up, step, False)
        up = (*up_kept, *named("back_up", moves.swap_step, up_sent, step))

    up, updates, dn, d_routed, small_grads, q_kept, q_sent = together(
        up, updates, dn, d_routed, small_grads, q_kept, q_sent
    )
    q_arrived = named("core_q", moves.swap, once(q_sent), moves.core)
    up_kept, up_sent = split_step(up, 0, False)
    up = (*up_kept, *named("back0_up", moves.swap_step, up_sent, 0))
    with jax.named_scope("z_routed"):
        next_routed = moves.shift(d_routed, 1)

    q_kept, q_arrived, up, updates, dn, d_routed, next_routed, small_grads = together(
        q_kept, q_arrived, up, updates, dn, d_routed, next_routed, small_grads
    )
    q_kept, q_sent = split_step((wide_open(q_kept), wide_open(q_arrived)), last, True)
    q = (*q_kept, *named("back1_q", moves.swap_step, q_sent, last))
    behind = [d_routed]
    with jax.named_scope("z_routed"):
        for _ in range(moves.tensor - 1 - ahead):
            behind.append(moves.shift(behind[-1], -1))
    d_routeds = out_on("routed", (d_routed, next_routed), behind[:0:-1])
    output = place_all(updates, tokens)
    dn_pieces = to_pieces(dn[:2], dn[2:], 1, moves.tensor)
    up_pieces = to_pieces(up[:2], up[2:], 1, moves.tensor)
    small_grads = lax.dot_general(
        small_grads, turn.astype(FULL), (((1,), (1,)), ((), ())), precision=lax.Precision.HIGHEST
    )
    small_grads = once(small_grads)
    for step in reversed(range(1, last)):
        q_kept, q_sent = split_step(q, step, False)
        q = (*q_kept, *named("back_q", moves.swap_step, q_sent, step))

    q, d_routeds, dn_pieces, up_pieces, output, small_grads = together(
        q, d_routeds, dn_pieces, up_pieces, output, small_grads
    )
    q_kept, q_sent = split_step(q, 0, False)
    q = (*q_kept, *named("back0_q", moves.swap_step, q_sent, 0))
    both_dn = sum_both("dn", dn_pieces)
    grad_tokens = place_all(d_routeds, cotangent)
    for bit in moves.chips[1:]:
        small_grads = small_grads + named("small", moves.swap, small_grads, bit)

    q, grad_tokens, both_dn, up_pieces, small_grads = together(
        q, grad_tokens, both_dn, up_pieces, small_grads
    )
    q_pieces = to_pieces(q[:2], q[2:], 2, moves.tensor)
    both_q = sum_both("q", q_pieces)
    last_dn = sum_on("dn", both_dn[1])
    both_up = sum_both("up", up_pieces)
    small_grads = small_grads + named("small", moves.swap, small_grads, moves.chips[0])

    both_q, last_dn, both_up, small_grads = together(both_q, last_dn, both_up, small_grads)
    last_q = sum_on("q", both_q[1])
    last_up = sum_on("up", both_up[1])
    grad_d = total_of([dn_pieces[0], both_dn[0], last_dn])
    small_grads = small_grads + named("small", moves.swap, small_grads, moves.core)
    with jax.named_scope("small"):
        small_grads = small_grads + sum(moves.shift(small_grads, step) for step in range(1, hops + 1))
    grad_q = total_of([q_pieces[0], both_q[0], last_q])
    grad_u = total_of([up_pieces[0], both_up[0], last_up])
    small_grads = lax.dynamic_slice_in_dim(small_grads, device * own, own, axis=1)

    return (
        output,
        grad_tokens,
        grad_q[:, :wide].astype(FULL),
        grad_q[:, wide : 2 * wide].astype(FULL),
        grad_q[:, 2 * wide : 3 * wide].astype(FULL),
        grad_q[:, 3 * wide :].T.astype(FULL),
        grad_u.astype(FULL),
        grad_d.T.astype(FULL),
        small_grads[0],
        small_grads[1],
        small_grads[2],
    )


def solution(mesh):
    in_specs = (
        P("batch", None),
        P("batch"),
        P("batch", None),
        P("batch", "tensor"),
        P("batch", "tensor"),
        P("batch", "tensor"),
        P("tensor", "batch"),
        P("batch", "tensor"),
        P("tensor", "batch"),
        P("batch"),
        P("batch"),
        P("batch"),
        P("batch", None),
    )
    out_specs = (
        P("batch", None),
        P("batch", None),
        P("batch", "tensor"),
        P("batch", "tensor"),
        P("batch", "tensor"),
        P("tensor", "batch"),
        P("batch", "tensor"),
        P("tensor", "batch"),
        P("batch"),
        P("batch"),
        P("batch"),
    )
    return jax.shard_map(
        functools.partial(shards, mesh),
        mesh=mesh,
        in_specs=in_specs,
        out_specs=out_specs,
        check_vma=False,
    )
```

```python
import functools

import jax
import jax.numpy as jnp
from jax import lax
from jax.experimental import pallas as pl
from jax.experimental.pallas import tpu as pltpu
from jax.sharding import PartitionSpec as P

HEAD_DIM = 64
SLOT_BLOCK = 512
PLACE_BLOCK = 2048
EPSILON = 1e-06


CURVE = 0.7978845608028654
CUBIC = 0.044715


def gelu_tanh(values):
    return 0.5 * values * (1.0 + jnp.tanh(CURVE * (values + CUBIC * values * values * values)))


def gelu_slope(values):
    square = values * values
    bend = jnp.tanh(CURVE * (values + CUBIC * values * square))
    inner = CURVE * (1.0 + 3.0 * CUBIC * square)
    return 0.5 * (1.0 + bend) + 0.5 * values * (1.0 - bend * bend) * inner


def product(left, right):
    return jnp.dot(left, right, preferred_element_type=jnp.float32)


def contract_rows(left, right):
    return lax.dot_general(
        left, right, (((0,), (0,)), ((), ())), preferred_element_type=jnp.float32
    )


def times_transposed(left, right):
    return lax.dot_general(
        left, right, (((1,), (1,)), ((), ())), preferred_element_type=jnp.float32
    )


def norm_backward(d_normed_in, normed, inverse, gain_vec):
    d_scaled = d_normed_in * gain_vec
    d_input = inverse * (d_scaled - normed * jnp.mean(d_scaled * normed, axis=-1, keepdims=True))
    return (d_input, jnp.sum(d_normed_in * normed, axis=0, keepdims=True))


def norm_forward(values):
    inverse = lax.rsqrt(jnp.mean(values * values, axis=-1, keepdims=True) + EPSILON)
    return (values * inverse, inverse)


LOW = jnp.bfloat16
FULL = jnp.float32


def pick_kernel(order_ref, routes_ref, turn_ref, tokens_ref, cot_ref, routed_ref, cot_routed_ref, total, cot_total):
    block = pl.program_id(1)
    capacity = routes_ref.shape[1]
    slots = tokens_ref.shape[1]
    column = lax.broadcasted_iota(jnp.int32, (capacity, slots), 1) + block * slots
    chooser = (routes_ref[0] == column).astype(LOW)
    part = product(chooser, tokens_ref[0])
    cot_part = product(chooser, cot_ref[0])

    @pl.when(block == 0)
    def _():
        total[...] = part
        cot_total[...] = cot_part

    @pl.when(block > 0)
    def _():
        total[...] += part
        cot_total[...] += cot_part

    @pl.when(block == pl.num_programs(1) - 1)
    def _():
        routed_ref[0] = product(total[...].astype(LOW), turn_ref[...]).astype(LOW)
        cot_routed_ref[0] = product(cot_total[...].astype(LOW), turn_ref[...]).astype(LOW)


def pick_rows(tokens, cotangent, routes, order, count, turn):
    seq_count, slots, features = tokens.shape
    capacity = routes.shape[1]
    per_block = min(SLOT_BLOCK, slots)
    table = pl.BlockSpec((1, per_block, features), lambda i, j, order: (order[i], j, 0))
    picked = pl.BlockSpec((1, capacity, features), lambda i, j, order: (i, 0, 0))
    shape = jax.ShapeDtypeStruct((count, capacity, features), LOW)
    return pl.pallas_call(
        pick_kernel,
        out_shape=(shape, shape),
        grid_spec=pltpu.PrefetchScalarGridSpec(
            num_scalar_prefetch=1,
            grid=(count, slots // per_block),
            in_specs=[
                pl.BlockSpec((1, capacity, 1), lambda i, j, order: (order[i], 0, 0)),
                pl.BlockSpec((features, features), lambda i, j, order: (0, 0)),
                table,
                table,
            ],
            out_specs=[picked, picked],
            scratch_shapes=[pltpu.VMEM((capacity, features), FULL)] * 2,
        ),
        compiler_params=pltpu.CompilerParams(vmem_limit_bytes=48 << 20),
        cost_estimate=pl.CostEstimate(
            flops=4 * count * capacity * slots * features,
            bytes_accessed=4 * count * slots * features,
            transcendentals=0,
        ),
        name="pick_rows",
    )(order, routes[:, :, None], turn, tokens, cotangent)


def place_kernel(order_ref, routes_ref, table_ref, values_ref, out_ref):
    block = pl.program_id(1)
    slots = table_ref.shape[1]
    capacity = routes_ref.shape[2]
    row = lax.broadcasted_iota(jnp.int32, (slots, capacity), 0) + block * slots
    chooser = (routes_ref[0] == row).astype(LOW)
    placed = product(chooser, values_ref[0])
    out_ref[0] = (table_ref[0].astype(FULL) + placed).astype(LOW)


def place_rows(table, values, routes, order):
    seq_count, slots, features = table.shape
    capacity = routes.shape[1]
    per_block = min(PLACE_BLOCK, slots)
    tall = pl.BlockSpec((1, per_block, features), lambda i, j, order: (order[i], j, 0))
    return pl.pallas_call(
        place_kernel,
        out_shape=jax.ShapeDtypeStruct(table.shape, table.dtype),
        grid_spec=pltpu.PrefetchScalarGridSpec(
            num_scalar_prefetch=1,
            grid=(seq_count, slots // per_block),
            in_specs=[
                pl.BlockSpec((1, 1, capacity), lambda i, j, order: (order[i], 0, 0)),
                tall,
                pl.BlockSpec((1, capacity, features), lambda i, j, order: (i, 0, 0)),
            ],
            out_specs=tall,
        ),
        compiler_params=pltpu.CompilerParams(vmem_limit_bytes=56 << 20),
        cost_estimate=pl.CostEstimate(
            flops=2 * seq_count * capacity * slots * features,
            bytes_accessed=4 * seq_count * slots * features,
            transcendentals=0,
        ),
        name="place_rows",
    )(order, routes[:, None, :], table, values)


def gates(routed, router_vec, live_ref, capacity):
    rows = routed.shape[0]
    score = jnp.sum(routed * router_vec, axis=-1, keepdims=True)
    gate_prob = 1.0 / (1.0 + jnp.exp(-score))
    live = [
        lax.broadcasted_iota(jnp.int32, (capacity, 1), 0) < live_ref[seq]
        for seq in range(rows // capacity)
    ]
    live = live[0] if len(live) == 1 else jnp.concatenate(live, axis=0)
    return gate_prob, jnp.where(live, gate_prob, 0.0)


def probabilities(queries, keys_all, live_count, scale_qk):
    scores = times_transposed(queries, keys_all) * scale_qk
    row = lax.broadcasted_iota(jnp.int32, scores.shape, 0)
    column = lax.broadcasted_iota(jnp.int32, scores.shape, 1)
    masked = jnp.where((column <= row) & (column < live_count), scores, -1e30)
    exp_scores = jnp.exp(masked - jnp.max(masked, axis=-1, keepdims=True))
    return exp_scores / jnp.sum(exp_scores, axis=-1, keepdims=True)


def split_heads(pair):
    owner = lax.broadcasted_iota(jnp.int32, pair.shape, 1) // HEAD_DIM
    return [jnp.where(owner == i, pair, jnp.zeros_like(pair)) for i in range(pair.shape[1] // HEAD_DIM)]


def attend_kernel(
    capacity, live_ref, routed_ref, cot_ref, small_ref, own, other,
    attn_in_ref, qkv_ref, heads_ref, attn_out_ref, mlp_in_ref, d_mlp_out_ref,
):
    routed = routed_ref[...].astype(FULL)
    rows, features = routed.shape
    half = features // 2
    wide = qkv_ref.shape[1] // 3
    _, gate_live = gates(routed, small_ref[2:3], live_ref, capacity)
    d_mlp_out_ref[...] = (gate_live * cot_ref[...].astype(FULL)).astype(LOW)
    normed, _ = norm_forward(routed)
    attn_in = (normed * small_ref[0:1]).astype(LOW)
    attn_in_ref[...] = attn_in
    left, right = attn_in[:, :half], attn_in[:, half:]
    qkv_ref[:, : 2 * wide] = (product(left, own[0]) + product(right, other[0])).astype(LOW)
    qkv_ref[:, 2 * wide :] = (
        product(left, own[1, :, :wide]) + product(right, other[1, :, :wide])
    ).astype(LOW)
    tile = 2 * HEAD_DIM
    for seq in range(rows // capacity):
        at = slice(seq * capacity, (seq + 1) * capacity)
        for start in range(0, wide, tile):
            keys_all = qkv_ref[at, wide + start : wide + start + tile]
            queries = split_heads(qkv_ref[at, start : start + tile])
            vals = split_heads(qkv_ref[at, 2 * wide + start : 2 * wide + start + tile])
            total = None
            for query, val in zip(queries, vals):
                probs = probabilities(query, keys_all, live_ref[seq], HEAD_DIM ** (-0.5))
                part = product(probs.astype(LOW), val)
                total = part if total is None else total + part
            heads_ref[at, start : start + tile] = total.astype(LOW)
    heads_out = heads_ref[...]
    attn_out_ref[:, :half] = times_transposed(heads_out, own[1, :, wide:])
    attn_out_ref[:, half:] = times_transposed(heads_out, other[1, :, wide:])
    normed_two, _ = norm_forward(routed + attn_out_ref[...])
    mlp_in_ref[...] = (normed_two * small_ref[1:2]).astype(LOW)


def whole_specs(count):
    return [pl.BlockSpec(memory_space=pltpu.VMEM)] * count


def attend(live_count, routed, cot_routed, small, weights, capacity):
    rows, features = routed.shape
    wide = weights[0].shape[2] // 2
    return pl.pallas_call(
        functools.partial(attend_kernel, capacity),
        out_shape=(
            jax.ShapeDtypeStruct((rows, features), LOW),
            jax.ShapeDtypeStruct((rows, 3 * wide), LOW),
            jax.ShapeDtypeStruct((rows, wide), LOW),
            jax.ShapeDtypeStruct((rows, features), FULL),
            jax.ShapeDtypeStruct((rows, features), LOW),
            jax.ShapeDtypeStruct((rows, features), LOW),
        ),
        in_specs=[pl.BlockSpec(memory_space=pltpu.SMEM)] + whole_specs(5),
        out_specs=tuple(whole_specs(6)),
        compiler_params=pltpu.CompilerParams(vmem_limit_bytes=56 << 20),
        cost_estimate=pl.CostEstimate(
            flops=8 * rows * features * wide + 4 * rows * capacity * wide,
            bytes_accessed=8 * features * wide + 14 * rows * features,
            transcendentals=rows * capacity * wide // HEAD_DIM,
        ),
        name="attend",
    )(live_count, routed, cot_routed, small, *weights)


def up_kernel(mlp_in_ref, d_mlp_out_ref, own, other, pre_ref, hidden_ref, kept_ref, sent_ref):
    mlp_in = mlp_in_ref[...]
    d_mlp_out = d_mlp_out_ref[...]
    half = mlp_in.shape[1] // 2
    for stream in range(2):
        pre = product(mlp_in[:, :half], own[stream]) + product(mlp_in[:, half:], other[stream])
        hidden = gelu_tanh(pre).astype(LOW)
        pre_ref[stream] = pre
        hidden_ref[stream] = hidden
        sent_ref[stream] = contract_rows(d_mlp_out[:, half:], hidden).astype(LOW)
        kept_ref[stream] = contract_rows(d_mlp_out[:, :half], hidden).astype(LOW)


TILE = 512


def up_layer(mlp_in, d_mlp_out, ups):
    rows, features = mlp_in.shape
    streams, half, width = ups[0].shape
    tile = min(TILE, width)
    whole = pl.BlockSpec((rows, features), lambda i: (0, 0))
    weight = pl.BlockSpec((streams, half, tile), lambda i: (0, 0, i))
    tall = pl.BlockSpec((streams, rows, tile), lambda i: (0, 0, i))
    return pl.pallas_call(
        up_kernel,
        grid=(width // tile,),
        out_shape=(
            jax.ShapeDtypeStruct((streams, rows, width), FULL),
            jax.ShapeDtypeStruct((streams, rows, width), LOW),
            jax.ShapeDtypeStruct(ups[0].shape, LOW),
            jax.ShapeDtypeStruct(ups[0].shape, LOW),
        ),
        in_specs=[whole, whole, weight, weight],
        out_specs=(tall, tall, weight, weight),
        compiler_params=pltpu.CompilerParams(vmem_limit_bytes=56 << 20),
        cost_estimate=pl.CostEstimate(
            flops=8 * rows * features * width,
            bytes_accessed=8 * features * width + 12 * rows * width,
            transcendentals=2 * rows * width,
        ),
        name="up_layer",
    )(mlp_in, d_mlp_out, *ups)


def down_kernel(
    capacity, live_ref, routed_ref, cot_ref, small_ref, turn_ref, attn_out_ref, mlp_in_ref, d_mlp_out_ref,
    up_own, up_other, down_own, down_other, pre_ref, hidden_ref,
    update_ref, d_mlp_in_ref, dot_ref, kept_ref, sent_ref, mlp_out,
):
    mlp_in = mlp_in_ref[...]
    d_mlp_out = d_mlp_out_ref[...]
    half = mlp_in.shape[1] // 2

    @pl.when(pl.program_id(0) == 0)
    def _():
        mlp_out[...] = jnp.zeros_like(mlp_out)
        d_mlp_in_ref[...] = jnp.zeros_like(d_mlp_in_ref)

    for stream in range(2):
        d_hidden = product(d_mlp_out[:, :half], down_own[stream]) + product(
            d_mlp_out[:, half:], down_other[stream]
        )
        d_pre = (d_hidden * gelu_slope(pre_ref[stream])).astype(LOW)
        sent_ref[stream] = contract_rows(mlp_in[:, half:], d_pre).astype(LOW)
        kept_ref[stream] = contract_rows(mlp_in[:, :half], d_pre).astype(LOW)
        d_mlp_in_ref[:, :half] += times_transposed(d_pre, up_own[stream])
        d_mlp_in_ref[:, half:] += times_transposed(d_pre, up_other[stream])
        hidden = hidden_ref[stream]
        mlp_out[:, :half] += times_transposed(hidden, down_own[stream])
        mlp_out[:, half:] += times_transposed(hidden, down_other[stream])

    @pl.when(pl.program_id(0) == pl.num_programs(0) - 1)
    def _():
        _, gate_live = gates(routed_ref[...].astype(FULL), small_ref[2:3], live_ref, capacity)
        branch = attn_out_ref[...] + mlp_out[...]
        update = (gate_live * branch).astype(LOW)
        update_ref[...] = times_transposed(update, turn_ref[...]).astype(LOW)
        dot_ref[...] = jnp.sum(cot_ref[...].astype(FULL) * branch, axis=-1, keepdims=True)


def down_layer(live_count, routed, cot_routed, small, turn, attn_out, mlp_in, d_mlp_out, ups, downs, pre, hidden, capacity):
    rows, features = mlp_in.shape
    streams, half, width = ups[0].shape
    tile = min(TILE, width)
    whole = pl.BlockSpec((rows, features), lambda i: (0, 0))
    weight = pl.BlockSpec((streams, half, tile), lambda i: (0, 0, i))
    tall = pl.BlockSpec((streams, rows, tile), lambda i: (0, 0, i))
    return pl.pallas_call(
        functools.partial(down_kernel, capacity),
        grid=(width // tile,),
        out_shape=(
            jax.ShapeDtypeStruct((rows, features), LOW),
            jax.ShapeDtypeStruct((rows, features), FULL),
            jax.ShapeDtypeStruct((rows, 1), FULL),
            jax.ShapeDtypeStruct(ups[0].shape, LOW),
            jax.ShapeDtypeStruct(ups[0].shape, LOW),
        ),
        in_specs=[
            pl.BlockSpec(memory_space=pltpu.SMEM),
            whole,
            whole,
            pl.BlockSpec(small.shape, lambda i: (0, 0)),
            pl.BlockSpec(turn.shape, lambda i: (0, 0)),
            whole,
            whole,
            whole,
        ]
        + [weight] * 4
        + [tall] * 2,
        out_specs=(whole, whole, pl.BlockSpec((rows, 1), lambda i: (0, 0)), weight, weight),
        scratch_shapes=[pltpu.VMEM((rows, features), FULL)],
        compiler_params=pltpu.CompilerParams(vmem_limit_bytes=56 << 20),
        cost_estimate=pl.CostEstimate(
            flops=16 * rows * features * width,
            bytes_accessed=12 * features * width + 12 * rows * width,
            transcendentals=2 * rows * width,
        ),
        name="down_layer",
    )(live_count, routed, cot_routed, small, turn, attn_out, mlp_in, d_mlp_out, *ups, *downs, pre, hidden)


def attend_back_kernel(
    capacity, live_ref, routed_ref, cot_ref, small_ref, turn_ref, attn_out_ref, d_mlp_in_ref, dot_ref, qkv_ref,
    own, other, d_routed_ref, d_attn_out_ref, d_qkv_ref, small_grads_ref, d_heads_ref,
):
    routed = routed_ref[...].astype(FULL)
    rows, features = routed.shape
    half = features // 2
    wide = qkv_ref.shape[1] // 3
    scale_qk = HEAD_DIM ** (-0.5)
    gate_prob, gate_live = gates(routed, small_ref[2:3], live_ref, capacity)
    normed_two, inverse_two = norm_forward(routed + attn_out_ref[...])
    d_middle, small_grads_ref[1:2] = norm_backward(
        d_mlp_in_ref[...], normed_two, inverse_two, small_ref[1:2]
    )
    d_attn_out = (d_middle + gate_live * cot_ref[...].astype(FULL)).astype(LOW)
    d_attn_out_ref[...] = d_attn_out
    d_heads_ref[...] = (
        product(d_attn_out[:, :half], own[1, :, wide:]) + product(d_attn_out[:, half:], other[1, :, wide:])
    ).astype(LOW)
    tile = 2 * HEAD_DIM
    for seq in range(rows // capacity):
        at = slice(seq * capacity, (seq + 1) * capacity)
        for start in range(0, wide, tile):
            query_pair = qkv_ref[at, start : start + tile]
            key_pair = qkv_ref[at, wide + start : wide + start + tile]
            val_pair = qkv_ref[at, 2 * wide + start : 2 * wide + start + tile]
            d_query, d_key, d_val = 0.0, 0.0, 0.0
            for query, key, d_head in zip(
                split_heads(query_pair), split_heads(key_pair), split_heads(d_heads_ref[at, start : start + tile])
            ):
                probs = probabilities(query, key_pair, live_ref[seq], scale_qk)
                d_val = d_val + contract_rows(probs.astype(LOW), d_head)
                d_probs = times_transposed(d_head, val_pair)
                d_scores = (
                    probs * (d_probs - jnp.sum(d_probs * probs, axis=-1, keepdims=True))
                ).astype(LOW)
                d_query = d_query + product(d_scores, key)
                d_key = d_key + contract_rows(d_scores, query)
            d_qkv_ref[at, start : start + tile] = (d_query * scale_qk).astype(LOW)
            d_qkv_ref[at, wide + start : wide + start + tile] = (d_key * scale_qk).astype(LOW)
            d_qkv_ref[at, 2 * wide + start : 2 * wide + start + tile] = d_val.astype(LOW)
    d_both = d_qkv_ref[:, : 2 * wide]
    d_vals = d_qkv_ref[:, 2 * wide :]
    d_attn_in = jnp.concatenate(
        [
            times_transposed(d_both, side[0]) + times_transposed(d_vals, side[1, :, :wide])
            for side in (own, other)
        ],
        axis=1,
    )
    normed_one, inverse_one = norm_forward(routed)
    d_from_norm, small_grads_ref[0:1] = norm_backward(d_attn_in, normed_one, inverse_one, small_ref[0:1])
    d_score = gate_live * (1.0 - gate_prob) * dot_ref[...]
    small_grads_ref[2:3] = jnp.sum(routed * d_score, axis=0, keepdims=True)
    d_routed = (d_middle + d_from_norm + d_score * small_ref[2:3]).astype(LOW)
    d_routed_ref[...] = times_transposed(d_routed, turn_ref[...]).astype(LOW)


def attend_back(live_count, routed, cot_routed, small, turn, attn_out, d_mlp_in, dot, qkv, weights, capacity):
    rows, features = routed.shape
    wide = weights[0].shape[2] // 2
    return pl.pallas_call(
        functools.partial(attend_back_kernel, capacity),
        out_shape=(
            jax.ShapeDtypeStruct((rows, features), LOW),
            jax.ShapeDtypeStruct((rows, features), LOW),
            jax.ShapeDtypeStruct((rows, 3 * wide), LOW),
            jax.ShapeDtypeStruct((3, features), FULL),
        ),
        in_specs=[pl.BlockSpec(memory_space=pltpu.SMEM)] + whole_specs(10),
        out_specs=tuple(whole_specs(4)),
        scratch_shapes=[pltpu.VMEM((rows, wide), LOW)],
        compiler_params=pltpu.CompilerParams(vmem_limit_bytes=56 << 20),
        cost_estimate=pl.CostEstimate(
            flops=8 * rows * features * wide + 10 * rows * capacity * wide,
            bytes_accessed=8 * features * wide + 14 * rows * features,
            transcendentals=rows * capacity * wide // HEAD_DIM,
        ),
        name="attend_back",
    )(live_count, routed, cot_routed, small, turn, attn_out, d_mlp_in, dot, qkv, *weights)


def grads_kernel(attn_in_ref, d_attn_out_ref, heads_ref, d_qkv_ref, kept_ref, sent_ref):
    half = attn_in_ref.shape[1] // 2
    wide = heads_ref.shape[1]
    for at, out_ref in ((slice(half, 2 * half), sent_ref), (slice(0, half), kept_ref)):
        attn_in = attn_in_ref[:, at]
        out_ref[0] = contract_rows(attn_in, d_qkv_ref[:, : 2 * wide]).astype(LOW)
        out_ref[1, :, :wide] = contract_rows(attn_in, d_qkv_ref[:, 2 * wide :]).astype(LOW)
        out_ref[1, :, wide:] = contract_rows(d_attn_out_ref[:, at], heads_ref[...]).astype(LOW)


def attend_grads(attn_in, d_attn_out, heads_out, d_qkv):
    rows, features = attn_in.shape
    wide = heads_out.shape[1]
    return pl.pallas_call(
        grads_kernel,
        out_shape=(jax.ShapeDtypeStruct((2, features // 2, 2 * wide), LOW),) * 2,
        in_specs=whole_specs(4),
        out_specs=tuple(whole_specs(2)),
        compiler_params=pltpu.CompilerParams(vmem_limit_bytes=56 << 20),
        cost_estimate=pl.CostEstimate(
            flops=8 * rows * features * wide,
            bytes_accessed=8 * features * wide + 8 * rows * features,
            transcendentals=0,
        ),
        name="attend_grads",
    )(attn_in, d_attn_out, heads_out, d_qkv)


class Exchange:
    def __init__(self, mesh):
        self.batch = mesh.shape["batch"]
        self.tensor = mesh.shape["tensor"]
        bits = []
        bit = self.batch // 2
        while bit:
            bits.append(bit)
            bit //= 2
        self.core = bits[-1]
        self.chips = bits[:-1]

    def swap(self, array, bit):
        with jax.named_scope(f"swap{bit}"):
            return lax.ppermute(array, "batch", [(i, i ^ bit) for i in range(self.batch)])

    def shift(self, array, step):
        size = self.tensor
        with jax.named_scope(f"shift{step}"):
            return lax.ppermute(array, "tensor", [(i, (i + step) % size) for i in range(size)])

    def block_order(self):
        order = [0]
        for bit in reversed([self.core] + self.chips):
            order = order + [place ^ bit for place in order]
        return order

    def gather_small(self, array):
        total = array[None]
        for bit in reversed([self.core] + self.chips):
            total = jnp.concatenate([total, self.swap(total, bit)], axis=0)
        return total.transpose(1, 0, 2).reshape(array.shape[0], -1)

    def axis(self, stream, step):
        return step if stream else len(self.chips) - 1 - step

    def swap_step(self, pair, step):
        return [self.swap(array, self.chips[self.axis(i, step)]) for i, array in enumerate(pair)]


def small_kernel(kernel, out_shape, *arrays, name):
    return pl.pallas_call(
        kernel,
        out_shape=out_shape,
        in_specs=whole_specs(len(arrays)),
        out_specs=tuple(whole_specs(len(out_shape))),
        compiler_params=pltpu.CompilerParams(vmem_limit_bytes=40 << 20),
        cost_estimate=pl.CostEstimate(
            flops=0, bytes_accessed=4 * sum(a.size for a in arrays), transcendentals=0
        ),
        name=name,
    )(*arrays)


def streams_kernel(parts, *refs):
    pieces, outs = refs[:-2], refs[-2:]
    count = len(pieces)
    width = pieces[0].shape[1] // (2 * parts)
    for stream, out_ref in enumerate(outs):
        lead = (0,) * (len(out_ref.shape) - 2)
        for i in range(parts):
            source = (stream * parts + i) * width
            for k, piece in enumerate(pieces):
                target = (i * count + k) * width
                out_ref[lead + (slice(None), slice(target, target + width))] = piece[
                    :, source : source + width
                ]


def to_streams(pieces, parts, places):
    rows, columns = pieces[0].shape
    shape = (1,) * places + (rows, columns * len(pieces) // 2)
    out = jax.ShapeDtypeStruct(shape, pieces[0].dtype)
    return small_kernel(functools.partial(streams_kernel, parts), (out, out), *pieces, name="streams")


def join_kernel(axes, stacked, *refs):
    ins, outs = refs[:4], refs[4:]
    for stream in range(2):
        for side in range(2):
            source = ins[2 * stream + side]
            at = [slice(None)] * len(source.shape)
            size = source.shape[axes[stream]]
            at[axes[stream]] = slice(side * size, (side + 1) * size)
            if stacked:
                outs[0][(stream,) + tuple(at)] = source[...]
            else:
                outs[stream][tuple(at)] = source[...]


def join(pair, arrived, axes, stacked):
    columns = pair[0].shape[-1]
    tile = min(TILE, columns)
    shapes = []
    for array, axis in zip(pair, axes):
        shape = list(array.shape)
        shape[axis] *= 2
        shapes.append(tuple(shape))
    if stacked:
        shapes = [(2,) + shapes[0]]

    def tiled(shape):
        return pl.BlockSpec(tuple(shape[:-1]) + (tile,), column_block(len(shape)))

    got = pl.pallas_call(
        functools.partial(join_kernel, axes, stacked),
        grid=(columns // tile,),
        out_shape=tuple(jax.ShapeDtypeStruct(shape, LOW) for shape in shapes),
        in_specs=[tiled(pair[i // 2].shape) for i in range(4)],
        out_specs=tuple(tiled(shape) for shape in shapes),
        compiler_params=pltpu.CompilerParams(vmem_limit_bytes=40 << 20),
        cost_estimate=pl.CostEstimate(
            flops=0, bytes_accessed=8 * sum(a.size for a in pair), transcendentals=0
        ),
        name="join",
    )(pair[0], arrived[0], pair[1], arrived[1])
    return got[0] if stacked else got


def added(refs, at):
    total = refs[0][at].astype(FULL)
    for ref in refs[1:]:
        total = total + ref[at].astype(FULL)
    return total.astype(LOW)


def split_kernel(axes, stacked, *refs):
    ins, (kept_one, kept_two, sent_one, sent_two) = refs[:-4], refs[-4:]
    for stream, (kept_ref, sent_ref) in enumerate(((kept_one, sent_one), (kept_two, sent_two))):
        sources = ins if stacked else ins[stream::2]
        for side, out_ref in ((1, sent_ref), (0, kept_ref)):
            at = [slice(None)] * len(out_ref.shape)
            at[axes[stream]] = slice(side, side + 1)
            at = ((stream,) if stacked else ()) + tuple(at)
            out_ref[...] = added(sources, at)


def split(arrays, axes, stacked):
    full = arrays[0].shape[1:] if stacked else arrays[0].shape
    columns = full[-1]
    tile = min(TILE, columns)
    outs, specs = [], []
    for stream in range(2):
        shape = list(full if stacked else arrays[stream].shape)
        shape[axes[stream]] = 1
        outs.append(jax.ShapeDtypeStruct(tuple(shape), LOW))
        specs.append(pl.BlockSpec(tuple(shape[:-1]) + (tile,), column_block(len(shape))))
    got = pl.pallas_call(
        functools.partial(split_kernel, axes, stacked),
        grid=(columns // tile,),
        out_shape=tuple(outs * 2),
        in_specs=[
            pl.BlockSpec(array.shape[:-1] + (tile,), column_block(array.ndim)) for array in arrays
        ],
        out_specs=tuple(specs * 2),
        compiler_params=pltpu.CompilerParams(vmem_limit_bytes=40 << 20),
        cost_estimate=pl.CostEstimate(
            flops=0, bytes_accessed=3 * sum(a.size for a in arrays), transcendentals=0
        ),
        name="split",
    )(*arrays)
    return got[:2], got[2:]


def column_block(rank):
    return lambda i: (0,) * (rank - 1) + (i,)


def pieces_kernel(parts, *refs):
    ins, outs = refs[:4], refs[4:]
    count = len(outs)
    width = outs[0].shape[1] // (2 * parts)
    lead = (0,) * (len(ins[0].shape) - 2)
    for k in reversed(range(count)):
        for stream in range(2):
            for i in range(parts):
                source = (i * count + k) * width
                target = (stream * parts + i) * width
                outs[k][:, target : target + width] = added(
                    ins[stream::2], lead + (slice(None), slice(source, source + width))
                )


def to_pieces(kept, arrived, parts, count):
    rows, columns = kept[0].shape[-2:]
    out = jax.ShapeDtypeStruct((rows, 2 * columns // count), LOW)
    return small_kernel(
        functools.partial(pieces_kernel, parts), (out,) * count, *kept, *arrived, name="pieces"
    )


def total_of(addends):
    total = addends[0].astype(FULL)
    for array in addends[1:]:
        total = total + array.astype(FULL)
    return total.astype(LOW)


def after(values, *others):
    return lax.optimization_barrier((values, others))[0]


class Line:
    def __init__(self):
        self.last = None

    def wait(self, *arrays):
        self.last = (self.last, arrays)

    def __call__(self, kernel, *arrays, **rest):
        if self.last is not None:
            arrays = after(arrays, self.last)
        out = kernel(*arrays, **rest)
        leaves = jax.tree.leaves(out)
        self.last = min(leaves, key=lambda leaf: leaf.size)
        return out


def shards(
    mesh,
    tokens,
    lengths,
    routes,
    w_query,
    w_key,
    w_value,
    w_out,
    w_up,
    w_down,
    gain_attn,
    gain_mlp,
    w_router,
    cotangent,
):
    moves = Exchange(mesh)
    device = lax.axis_index("batch")
    column = lax.axis_index("tensor")
    seq_count, capacity = routes.shape
    features = tokens.shape[1]
    tokens = tokens.reshape(seq_count, -1, features)
    cotangent = cotangent.reshape(tokens.shape)

    repeats = max(1, moves.tensor // seq_count)
    local_count = max(1, seq_count // moves.tensor)
    first = column // repeats if repeats > 1 else column * local_count
    order = (first + jnp.arange(local_count)).astype(jnp.int32)
    counts_once = (column % repeats) == 0

    def once(values):
        return jnp.where(counts_once, values, jnp.zeros_like(values)) if repeats > 1 else values

    own = features // moves.batch
    place_block = jnp.asarray(moves.block_order(), jnp.int32)
    source = ((place_block ^ device)[:, None] * own + jnp.arange(own, dtype=jnp.int32)).reshape(-1)
    turn = (jnp.arange(features, dtype=jnp.int32)[:, None] == source[None, :]).astype(LOW)

    wide = w_query.shape[1]
    steps = len(moves.chips)
    shard_q = jnp.concatenate(
        [w_query.astype(LOW), w_key.astype(LOW), w_value.astype(LOW), w_out.astype(LOW).T], axis=1
    )
    shard_u = w_up.astype(LOW)
    shard_d = w_down.astype(LOW).T

    def ring(array, hops):
        pieces = [array]
        for _ in range(hops):
            pieces.append(moves.shift(pieces[-1], 1))
        return pieces

    hops = moves.tensor - 1
    line = Line()
    rows_total = local_count * capacity
    live_count = lax.dynamic_slice_in_dim(lengths, first, local_count) // 8

    def flat(array):
        return array.reshape(rows_total, features)

    def named(name, function, *arrays):
        with jax.named_scope(name):
            return function(*arrays)

    def axes_of(step):
        return tuple(moves.axis(stream, step) for stream in range(2))

    def gather(name, pair, step):
        arrived = named(name, moves.swap_step, pair, step)
        last = step == steps - 1
        return lambda: line(lambda *a: join(a[:2], a[2:], axes_of(step), last), *pair, *arrived)

    def whole(name, stacked):
        own_side = stacked.reshape(2, features // 2, stacked.shape[-1])
        return own_side, named(name, moves.swap, own_side, moves.core)

    def first_step(name, shard):
        half = shard.shape[1] // 2
        arrived = named(name, moves.swap_step, [shard[:, :half], shard[:, half:]], 0)
        return jnp.concatenate([shard, jnp.concatenate(arrived, axis=1)], axis=0)

    def doubled(pieces, parts):
        got = line(lambda *a: to_streams(a, parts, steps), *pieces)
        pair = []
        for stream, array in enumerate(got):
            lead = [1] * steps
            lead[moves.axis(stream, 0)] = 2
            pair.append(array.reshape(tuple(lead) + (array.shape[-2] // 2, array.shape[-1])))
        return pair

    def wide_open(array):
        return once(array).reshape((2,) + (2,) * steps + (own, array.shape[-1]))

    def split_step(arrays, step, stacked):
        return split(arrays, axes_of(step), stacked)

    def together(*values):
        return lax.optimization_barrier(values)

    def place_all(pieces, table):
        kept = pieces[::repeats] if repeats > 1 else pieces
        values = jnp.concatenate(
            [piece.reshape(local_count, capacity, features) for piece in kept], axis=0
        )
        owners = ((column - jnp.arange(0, moves.tensor, repeats)) % moves.tensor).astype(jnp.int32)
        if repeats > 1:
            places = owners // repeats
        else:
            places = (owners[:, None] * local_count + jnp.arange(local_count)).reshape(-1)
        return place_rows(table, values, routes, places.astype(jnp.int32)).reshape(-1, features)

    ahead = moves.tensor // 2

    def out_both(name, array):
        with jax.named_scope("z_" + name):
            onward = [array, moves.shift(array, 1)]
            behind = [array]
            for _ in range(moves.tensor - 1 - ahead):
                behind.append(moves.shift(behind[-1], -1))
        return onward, behind[:0:-1]

    def out_on(name, onward, behind):
        onward = list(onward)
        with jax.named_scope("z_" + name):
            for _ in range(ahead - 1):
                onward.append(moves.shift(onward[-1], 1))
        return onward + list(behind)

    def sum_ahead(name, pieces):
        with jax.named_scope("z_" + name):
            fore = pieces[ahead + 1] if ahead + 1 < moves.tensor else jnp.zeros_like(pieces[0])
            for piece in pieces[ahead + 2 :]:
                fore = total_of([piece, moves.shift(fore, 1)])
            return moves.shift(fore, 1) if ahead + 1 < moves.tensor else fore

    def sum_back(name, pieces):
        with jax.named_scope("z_" + name):
            back = None
            for piece in pieces[ahead:1:-1]:
                back = moves.shift(piece if back is None else total_of([piece, back]), -1)
        return pieces[1] if back is None else total_of([pieces[1], back])

    def sum_both(name, pieces):
        return sum_ahead(name, pieces), sum_back(name, pieces)

    def sum_on(name, back):
        with jax.named_scope("z_" + name):
            return moves.shift(back, -1)

    both_q = out_both("q", shard_q)
    routed, cot_routed = pick_rows(tokens, cotangent, routes, order, local_count, turn)
    line.last = cot_routed
    both_q = after(both_q, cot_routed)
    pieces_q = out_on("q", *both_q)
    routed, cot_routed = flat(routed), flat(cot_routed)
    wide_d = first_step("out0_d", after(shard_d, shard_q))
    small = after(jnp.stack([gain_attn, gain_mlp, w_router]).astype(LOW), pieces_q)
    small = named("small", moves.gather_small, small).astype(FULL)
    pieces_q = after(pieces_q, wide_d)
    pair_q = line(lambda *a: to_streams(a, 2, steps), *pieces_q)
    both_u = out_both("u", after(shard_u, pieces_q))
    pieces_u = out_on("u", *both_u)
    line.wait(both_u, small)
    for step in range(steps - 1):
        pair_q = gather(f"out{step}_q", pair_q, step)()
    joined_q = gather("last_q", pair_q, steps - 1)
    pair_u = line(lambda *a: to_streams(a, 1, steps), *pieces_u)
    joined_u = gather("out0_u", pair_u, 0)
    pieces_d = named("z_d", ring, after(wide_d, pieces_u), hops)
    line.wait(pieces_d[1])
    attn_weights = whole("core_q", joined_q())
    line.wait(pieces_d[2 % moves.tensor])
    for step in range(1, steps):
        joined_u = gather(f"out{step}_u", joined_u(), step)
    attn_in, qkv, heads_out, attn_out, mlp_in, d_mlp_out = line(
        lambda *a: attend(*a[:4], a[4:], capacity), live_count, routed, cot_routed, small, *attn_weights
    )
    pair_d = doubled(pieces_d, 1)
    for step in range(1, steps - 1):
        pair_d = gather(f"out{step}_d", pair_d, step)()
    joined_d = gather("last_d", pair_d, steps - 1)
    ups = whole("core_u", joined_u())
    pre, hidden, dn_kept, dn_sent = line(
        lambda *a: up_layer(*a[:2], a[2:]), mlp_in, d_mlp_out, *ups
    )
    joined_d = joined_d()

    joined_d, dn_kept, dn_sent = together(joined_d, dn_kept, dn_sent)
    dn_arrived = named("core_dn", moves.swap, once(dn_sent), moves.core)
    downs = whole("core_d", joined_d)
    dn = (wide_open(dn_kept), wide_open(dn_arrived))

    last = steps - 1
    dn_kept, dn_sent = split_step(dn, last, True)
    dn_sent, *rest = after((dn_sent, mlp_in, pre, hidden), downs)
    dn_sent, rest = together(dn_sent, rest)
    dn_arrived = named("back_dn", moves.swap_step, dn_sent, last)
    update, d_mlp_in, dot, up_kept, up_sent = down_layer(
        live_count, routed, cot_routed, small, turn, attn_out, rest[0], d_mlp_out, ups, downs, *rest[1:], capacity
    )
    dn = (*dn_kept, *dn_arrived)
    for step in reversed(range(1, last)):
        dn_kept, dn_sent = split_step(dn, step, False)
        dn = (*dn_kept, *named("back_dn", moves.swap_step, dn_sent, step))

    def halve_small(array, bit):
        mine = array.shape[1] // 2
        with jax.named_scope("small"):
            return array[:, :mine] + moves.swap(array[:, mine:], bit)

    def spread_small(array, bit):
        with jax.named_scope("small"):
            pairs = [(i, i ^ bit) for i in range(moves.tensor)]
            return array + lax.ppermute(array, "tensor", pairs)

    def from_behind(name, rows):
        pieces = [rows]
        with jax.named_scope("z_" + name):
            for _ in range(moves.tensor - 1 - ahead):
                pieces.append(moves.shift(pieces[-1], -1))
        return pieces[:0:-1]

    dn, update, d_mlp_in, dot, up_kept, up_sent = together(dn, update, d_mlp_in, dot, up_kept, up_sent)
    up_arrived = named("core_up", moves.swap, once(up_sent), moves.core)
    dn_kept, dn_sent = split_step(dn, 0, False)
    dn = (*dn_kept, *named("back0_dn", moves.swap_step, dn_sent, 0))
    with jax.named_scope("z_update"):
        next_update = moves.shift(update, 1)
    behind_update = from_behind("update", update)
    d_routed, d_attn_out, d_qkv, small_grads = attend_back(
        live_count, routed, cot_routed, small, turn, attn_out, d_mlp_in, dot, qkv, attn_weights, capacity
    )
    q_kept, q_sent = attend_grads(attn_in, d_attn_out, heads_out, d_qkv)

    up_kept, up_arrived, dn, update, next_update, behind_update, d_routed, small_grads, q_kept, q_sent = together(
        up_kept, up_arrived, dn, update, next_update, behind_update, d_routed, small_grads, q_kept, q_sent
    )
    up_kept, up_sent = split_step((wide_open(up_kept), wide_open(up_arrived)), last, True)
    up = (*up_kept, *named("back1_up", moves.swap_step, up_sent, last))
    q_arrived = named("core_q", moves.swap, once(q_sent), moves.core)
    updates = out_on("update", (update, next_update), behind_update)
    with jax.named_scope("z_routed"):
        next_routed = moves.shift(d_routed, 1)
    dn_pieces = to_pieces(dn[:2], dn[2:], 1, moves.tensor)
    small_grads = once(small_grads)
    for step in reversed(range(1, last)):
        up_kept, up_sent = split_step(up, step, False)
        up = (*up_kept, *named("back_up", moves.swap_step, up_sent, step))

    up, q_kept, q_arrived, updates, d_routed, next_routed, dn_pieces, small_grads = together(
        up, q_kept, q_arrived, updates, d_routed, next_routed, dn_pieces, small_grads
    )
    up_kept, up_sent = split_step(up, 0, False)
    up = (*up_kept, *named("back0_up", moves.swap_step, up_sent, 0))
    q_kept, q_sent = split_step((wide_open(q_kept), wide_open(q_arrived)), last, True)
    q = (*q_kept, *named("back1_q", moves.swap_step, q_sent, last))
    d_routeds = out_on("routed", (d_routed, next_routed), ())
    output = place_all(updates, tokens)
    behind_routed = from_behind("routed", after(d_routed, d_routeds, output))
    for step in reversed(range(1, last)):
        q_kept, q_sent = split_step(q, step, False)
        q = (*q_kept, *named("back_q", moves.swap_step, q_sent, step))

    q, up, d_routeds, behind_routed, output, small_grads, dn_pieces = together(
        q, up, d_routeds, behind_routed, output, small_grads, dn_pieces
    )
    q_kept, q_sent = split_step(q, 0, False)
    q = (*q_kept, *named("back0_q", moves.swap_step, q_sent, 0))
    both_dn = sum_both("dn", dn_pieces)
    up_pieces = to_pieces(up[:2], up[2:], 1, moves.tensor)
    back_up = sum_back("up", up_pieces)

    q, both_dn, up_pieces, back_up, small_grads, d_routeds = together(
        q, both_dn, up_pieces, back_up, small_grads, d_routeds
    )
    q_pieces = to_pieces(q[:2], q[2:], 2, moves.tensor)
    both_q = sum_both("q", q_pieces)
    last_dn = sum_on("dn", both_dn[1])
    fore_up = sum_ahead("up", up_pieces)
    grad_tokens = place_all(list(d_routeds) + list(behind_routed), cotangent)
    for bit in (moves.core, *moves.chips):
        small_grads = halve_small(small_grads, bit)
    small_grads = spread_small(small_grads, 1)

    both_q, last_dn, fore_up, back_up, grad_tokens, small_grads = together(
        both_q, last_dn, fore_up, back_up, grad_tokens, small_grads
    )
    last_q = sum_on("q", both_q[1])
    last_up = sum_on("up", back_up)
    bit = 2
    while bit < moves.tensor:
        small_grads = spread_small(small_grads, bit)
        bit *= 2
    grad_d = total_of([dn_pieces[0], both_dn[0], last_dn])
    grad_q = total_of([q_pieces[0], both_q[0], last_q])
    grad_u = total_of([up_pieces[0], fore_up, last_up])

    return (
        output,
        grad_tokens,
        grad_q[:, :wide].astype(FULL),
        grad_q[:, wide : 2 * wide].astype(FULL),
        grad_q[:, 2 * wide : 3 * wide].astype(FULL),
        grad_q[:, 3 * wide :].T.astype(FULL),
        grad_u.astype(FULL),
        grad_d.T.astype(FULL),
        small_grads[0],
        small_grads[1],
        small_grads[2],
    )


def solution(mesh):
    in_specs = (
        P("batch", None),
        P("batch"),
        P("batch", None),
        P("batch", "tensor"),
        P("batch", "tensor"),
        P("batch", "tensor"),
        P("tensor", "batch"),
        P("batch", "tensor"),
        P("tensor", "batch"),
        P("batch"),
        P("batch"),
        P("batch"),
        P("batch", None),
    )
    out_specs = (
        P("batch", None),
        P("batch", None),
        P("batch", "tensor"),
        P("batch", "tensor"),
        P("batch", "tensor"),
        P("tensor", "batch"),
        P("batch", "tensor"),
        P("tensor", "batch"),
        P("batch"),
        P("batch"),
        P("batch"),
    )
    return jax.shard_map(
        functools.partial(shards, mesh),
        mesh=mesh,
        in_specs=in_specs,
        out_specs=out_specs,
        check_vma=False,
    )
```

```python
import functools

import jax
import jax.numpy as jnp
from jax import lax
from jax.experimental import pallas as pl
from jax.experimental.pallas import tpu as pltpu
from jax.sharding import PartitionSpec as P

HEAD_DIM = 64
SLOT_BLOCK = 512
PLACE_BLOCK = 2048
EPSILON = 1e-06


CURVE = 0.7978845608028654
CUBIC = 0.044715


def gelu_tanh(values):
    return 0.5 * values * (1.0 + jnp.tanh(CURVE * (values + CUBIC * values * values * values)))


def gelu_slope(values):
    square = values * values
    bend = jnp.tanh(CURVE * (values + CUBIC * values * square))
    inner = CURVE * (1.0 + 3.0 * CUBIC * square)
    return 0.5 * (1.0 + bend) + 0.5 * values * (1.0 - bend * bend) * inner


def product(left, right):
    return jnp.dot(left, right, preferred_element_type=jnp.float32)


def contract_rows(left, right):
    return lax.dot_general(
        left, right, (((0,), (0,)), ((), ())), preferred_element_type=jnp.float32
    )


def times_transposed(left, right):
    return lax.dot_general(
        left, right, (((1,), (1,)), ((), ())), preferred_element_type=jnp.float32
    )


def norm_backward(d_normed_in, normed, inverse, gain_vec):
    d_scaled = d_normed_in * gain_vec
    d_input = inverse * (d_scaled - normed * jnp.mean(d_scaled * normed, axis=-1, keepdims=True))
    return (d_input, jnp.sum(d_normed_in * normed, axis=0, keepdims=True))


def norm_forward(values):
    inverse = lax.rsqrt(jnp.mean(values * values, axis=-1, keepdims=True) + EPSILON)
    return (values * inverse, inverse)


LOW = jnp.bfloat16
FULL = jnp.float32


def pick_kernel(order_ref, routes_ref, turn_ref, tokens_ref, cot_ref, routed_ref, cot_routed_ref, total, cot_total):
    block = pl.program_id(1)
    capacity = routes_ref.shape[1]
    slots = tokens_ref.shape[1]
    column = lax.broadcasted_iota(jnp.int32, (capacity, slots), 1) + block * slots
    chooser = (routes_ref[0] == column).astype(LOW)
    part = product(chooser, tokens_ref[0])
    cot_part = product(chooser, cot_ref[0])

    @pl.when(block == 0)
    def _():
        total[...] = part
        cot_total[...] = cot_part

    @pl.when(block > 0)
    def _():
        total[...] += part
        cot_total[...] += cot_part

    @pl.when(block == pl.num_programs(1) - 1)
    def _():
        routed_ref[0] = product(total[...].astype(LOW), turn_ref[...]).astype(LOW)
        cot_routed_ref[0] = product(cot_total[...].astype(LOW), turn_ref[...]).astype(LOW)


def pick_rows(tokens, cotangent, routes, order, count, turn):
    seq_count, slots, features = tokens.shape
    capacity = routes.shape[1]
    per_block = min(SLOT_BLOCK, slots)
    table = pl.BlockSpec((1, per_block, features), lambda i, j, order: (order[i], j, 0))
    picked = pl.BlockSpec((1, capacity, features), lambda i, j, order: (i, 0, 0))
    shape = jax.ShapeDtypeStruct((count, capacity, features), LOW)
    return pl.pallas_call(
        pick_kernel,
        out_shape=(shape, shape),
        grid_spec=pltpu.PrefetchScalarGridSpec(
            num_scalar_prefetch=1,
            grid=(count, slots // per_block),
            in_specs=[
                pl.BlockSpec((1, capacity, 1), lambda i, j, order: (order[i], 0, 0)),
                pl.BlockSpec((features, features), lambda i, j, order: (0, 0)),
                table,
                table,
            ],
            out_specs=[picked, picked],
            scratch_shapes=[pltpu.VMEM((capacity, features), FULL)] * 2,
        ),
        compiler_params=pltpu.CompilerParams(vmem_limit_bytes=48 << 20),
        cost_estimate=pl.CostEstimate(
            flops=4 * count * capacity * slots * features,
            bytes_accessed=4 * count * slots * features,
            transcendentals=0,
        ),
        name="pick_rows",
    )(order, routes[:, :, None], turn, tokens, cotangent)


def place_kernel(order_ref, routes_ref, table_ref, values_ref, out_ref):
    block = pl.program_id(1)
    slots = table_ref.shape[1]
    capacity = routes_ref.shape[2]
    row = lax.broadcasted_iota(jnp.int32, (slots, capacity), 0) + block * slots
    chooser = (routes_ref[0] == row).astype(LOW)
    placed = product(chooser, values_ref[0])
    out_ref[0] = (table_ref[0].astype(FULL) + placed).astype(LOW)


def place_rows(table, values, routes, order):
    seq_count, slots, features = table.shape
    capacity = routes.shape[1]
    per_block = min(PLACE_BLOCK, slots)
    tall = pl.BlockSpec((1, per_block, features), lambda i, j, order: (order[i], j, 0))
    return pl.pallas_call(
        place_kernel,
        out_shape=jax.ShapeDtypeStruct(table.shape, table.dtype),
        grid_spec=pltpu.PrefetchScalarGridSpec(
            num_scalar_prefetch=1,
            grid=(seq_count, slots // per_block),
            in_specs=[
                pl.BlockSpec((1, 1, capacity), lambda i, j, order: (order[i], 0, 0)),
                tall,
                pl.BlockSpec((1, capacity, features), lambda i, j, order: (i, 0, 0)),
            ],
            out_specs=tall,
        ),
        compiler_params=pltpu.CompilerParams(vmem_limit_bytes=56 << 20),
        cost_estimate=pl.CostEstimate(
            flops=2 * seq_count * capacity * slots * features,
            bytes_accessed=4 * seq_count * slots * features,
            transcendentals=0,
        ),
        name="place_rows",
    )(order, routes[:, None, :], table, values)


def gates(routed, router_vec, live_ref, capacity):
    rows = routed.shape[0]
    score = jnp.sum(routed * router_vec, axis=-1, keepdims=True)
    gate_prob = 1.0 / (1.0 + jnp.exp(-score))
    live = [
        lax.broadcasted_iota(jnp.int32, (capacity, 1), 0) < live_ref[seq]
        for seq in range(rows // capacity)
    ]
    live = live[0] if len(live) == 1 else jnp.concatenate(live, axis=0)
    return gate_prob, jnp.where(live, gate_prob, 0.0)


def probabilities(queries, keys_all, live_count, scale_qk):
    scores = times_transposed(queries, keys_all) * scale_qk
    row = lax.broadcasted_iota(jnp.int32, scores.shape, 0)
    column = lax.broadcasted_iota(jnp.int32, scores.shape, 1)
    masked = jnp.where((column <= row) & (column < live_count), scores, -1e30)
    exp_scores = jnp.exp(masked - jnp.max(masked, axis=-1, keepdims=True))
    return exp_scores / jnp.sum(exp_scores, axis=-1, keepdims=True)


def split_heads(pair):
    owner = lax.broadcasted_iota(jnp.int32, pair.shape, 1) // HEAD_DIM
    return [jnp.where(owner == i, pair, jnp.zeros_like(pair)) for i in range(pair.shape[1] // HEAD_DIM)]


def attend_kernel(
    capacity, live_ref, routed_ref, cot_ref, small_ref, own, other,
    attn_in_ref, qkv_ref, heads_ref, attn_out_ref, mlp_in_ref, d_mlp_out_ref,
):
    routed = routed_ref[...].astype(FULL)
    rows, features = routed.shape
    half = features // 2
    wide = qkv_ref.shape[1] // 3
    _, gate_live = gates(routed, small_ref[2:3], live_ref, capacity)
    d_mlp_out_ref[...] = (gate_live * cot_ref[...].astype(FULL)).astype(LOW)
    normed, _ = norm_forward(routed)
    attn_in = (normed * small_ref[0:1]).astype(LOW)
    attn_in_ref[...] = attn_in
    left, right = attn_in[:, :half], attn_in[:, half:]
    qkv_ref[:, : 2 * wide] = (product(left, own[0]) + product(right, other[0])).astype(LOW)
    qkv_ref[:, 2 * wide :] = (
        product(left, own[1, :, :wide]) + product(right, other[1, :, :wide])
    ).astype(LOW)
    tile = 2 * HEAD_DIM
    for seq in range(rows // capacity):
        at = slice(seq * capacity, (seq + 1) * capacity)
        for start in range(0, wide, tile):
            keys_all = qkv_ref[at, wide + start : wide + start + tile]
            queries = split_heads(qkv_ref[at, start : start + tile])
            vals = split_heads(qkv_ref[at, 2 * wide + start : 2 * wide + start + tile])
            total = None
            for query, val in zip(queries, vals):
                probs = probabilities(query, keys_all, live_ref[seq], HEAD_DIM ** (-0.5))
                part = product(probs.astype(LOW), val)
                total = part if total is None else total + part
            heads_ref[at, start : start + tile] = total.astype(LOW)
    heads_out = heads_ref[...]
    attn_out_ref[:, :half] = times_transposed(heads_out, own[1, :, wide:])
    attn_out_ref[:, half:] = times_transposed(heads_out, other[1, :, wide:])
    normed_two, _ = norm_forward(routed + attn_out_ref[...])
    mlp_in_ref[...] = (normed_two * small_ref[1:2]).astype(LOW)


def whole_specs(count):
    return [pl.BlockSpec(memory_space=pltpu.VMEM)] * count


def attend(live_count, routed, cot_routed, small, weights, capacity):
    rows, features = routed.shape
    wide = weights[0].shape[2] // 2
    return pl.pallas_call(
        functools.partial(attend_kernel, capacity),
        out_shape=(
            jax.ShapeDtypeStruct((rows, features), LOW),
            jax.ShapeDtypeStruct((rows, 3 * wide), LOW),
            jax.ShapeDtypeStruct((rows, wide), LOW),
            jax.ShapeDtypeStruct((rows, features), FULL),
            jax.ShapeDtypeStruct((rows, features), LOW),
            jax.ShapeDtypeStruct((rows, features), LOW),
        ),
        in_specs=[pl.BlockSpec(memory_space=pltpu.SMEM)] + whole_specs(5),
        out_specs=tuple(whole_specs(6)),
        compiler_params=pltpu.CompilerParams(vmem_limit_bytes=56 << 20),
        cost_estimate=pl.CostEstimate(
            flops=8 * rows * features * wide + 4 * rows * capacity * wide,
            bytes_accessed=8 * features * wide + 14 * rows * features,
            transcendentals=rows * capacity * wide // HEAD_DIM,
        ),
        name="attend",
    )(live_count, routed, cot_routed, small, *weights)


def up_kernel(mlp_in_ref, d_mlp_out_ref, own, other, pre_ref, hidden_ref, kept_ref, sent_ref):
    mlp_in = mlp_in_ref[...]
    d_mlp_out = d_mlp_out_ref[...]
    half = mlp_in.shape[1] // 2
    for stream in range(2):
        pre = product(mlp_in[:, :half], own[stream]) + product(mlp_in[:, half:], other[stream])
        hidden = gelu_tanh(pre).astype(LOW)
        pre_ref[stream] = pre
        hidden_ref[stream] = hidden
        sent_ref[stream] = contract_rows(d_mlp_out[:, half:], hidden).astype(LOW)
        kept_ref[stream] = contract_rows(d_mlp_out[:, :half], hidden).astype(LOW)


TILE = 512


def up_layer(mlp_in, d_mlp_out, ups):
    rows, features = mlp_in.shape
    streams, half, width = ups[0].shape
    tile = min(TILE, width)
    whole = pl.BlockSpec((rows, features), lambda i: (0, 0))
    weight = pl.BlockSpec((streams, half, tile), lambda i: (0, 0, i))
    tall = pl.BlockSpec((streams, rows, tile), lambda i: (0, 0, i))
    return pl.pallas_call(
        up_kernel,
        grid=(width // tile,),
        out_shape=(
            jax.ShapeDtypeStruct((streams, rows, width), FULL),
            jax.ShapeDtypeStruct((streams, rows, width), LOW),
            jax.ShapeDtypeStruct(ups[0].shape, LOW),
            jax.ShapeDtypeStruct(ups[0].shape, LOW),
        ),
        in_specs=[whole, whole, weight, weight],
        out_specs=(tall, tall, weight, weight),
        compiler_params=pltpu.CompilerParams(vmem_limit_bytes=56 << 20),
        cost_estimate=pl.CostEstimate(
            flops=8 * rows * features * width,
            bytes_accessed=8 * features * width + 12 * rows * width,
            transcendentals=2 * rows * width,
        ),
        name="up_layer",
    )(mlp_in, d_mlp_out, *ups)


def down_kernel(
    capacity, live_ref, routed_ref, cot_ref, small_ref, turn_ref, attn_out_ref, mlp_in_ref, d_mlp_out_ref,
    up_own, up_other, down_own, down_other, pre_ref, hidden_ref,
    update_ref, d_mlp_in_ref, dot_ref, kept_ref, sent_ref, mlp_out,
):
    mlp_in = mlp_in_ref[...]
    d_mlp_out = d_mlp_out_ref[...]
    half = mlp_in.shape[1] // 2

    @pl.when(pl.program_id(0) == 0)
    def _():
        mlp_out[...] = jnp.zeros_like(mlp_out)
        d_mlp_in_ref[...] = jnp.zeros_like(d_mlp_in_ref)

    for stream in range(2):
        d_hidden = product(d_mlp_out[:, :half], down_own[stream]) + product(
            d_mlp_out[:, half:], down_other[stream]
        )
        d_pre = (d_hidden * gelu_slope(pre_ref[stream])).astype(LOW)
        sent_ref[stream] = contract_rows(mlp_in[:, half:], d_pre).astype(LOW)
        kept_ref[stream] = contract_rows(mlp_in[:, :half], d_pre).astype(LOW)
        d_mlp_in_ref[:, :half] += times_transposed(d_pre, up_own[stream])
        d_mlp_in_ref[:, half:] += times_transposed(d_pre, up_other[stream])
        hidden = hidden_ref[stream]
        mlp_out[:, :half] += times_transposed(hidden, down_own[stream])
        mlp_out[:, half:] += times_transposed(hidden, down_other[stream])

    @pl.when(pl.program_id(0) == pl.num_programs(0) - 1)
    def _():
        _, gate_live = gates(routed_ref[...].astype(FULL), small_ref[2:3], live_ref, capacity)
        branch = attn_out_ref[...] + mlp_out[...]
        update = (gate_live * branch).astype(LOW)
        update_ref[...] = times_transposed(update, turn_ref[...]).astype(LOW)
        dot_ref[...] = jnp.sum(cot_ref[...].astype(FULL) * branch, axis=-1, keepdims=True)


def down_layer(live_count, routed, cot_routed, small, turn, attn_out, mlp_in, d_mlp_out, ups, downs, pre, hidden, capacity):
    rows, features = mlp_in.shape
    streams, half, width = ups[0].shape
    tile = min(TILE, width)
    whole = pl.BlockSpec((rows, features), lambda i: (0, 0))
    weight = pl.BlockSpec((streams, half, tile), lambda i: (0, 0, i))
    tall = pl.BlockSpec((streams, rows, tile), lambda i: (0, 0, i))
    return pl.pallas_call(
        functools.partial(down_kernel, capacity),
        grid=(width // tile,),
        out_shape=(
            jax.ShapeDtypeStruct((rows, features), LOW),
            jax.ShapeDtypeStruct((rows, features), FULL),
            jax.ShapeDtypeStruct((rows, 1), FULL),
            jax.ShapeDtypeStruct(ups[0].shape, LOW),
            jax.ShapeDtypeStruct(ups[0].shape, LOW),
        ),
        in_specs=[
            pl.BlockSpec(memory_space=pltpu.SMEM),
            whole,
            whole,
            pl.BlockSpec(small.shape, lambda i: (0, 0)),
            pl.BlockSpec(turn.shape, lambda i: (0, 0)),
            whole,
            whole,
            whole,
        ]
        + [weight] * 4
        + [tall] * 2,
        out_specs=(whole, whole, pl.BlockSpec((rows, 1), lambda i: (0, 0)), weight, weight),
        scratch_shapes=[pltpu.VMEM((rows, features), FULL)],
        compiler_params=pltpu.CompilerParams(vmem_limit_bytes=56 << 20),
        cost_estimate=pl.CostEstimate(
            flops=16 * rows * features * width,
            bytes_accessed=12 * features * width + 12 * rows * width,
            transcendentals=2 * rows * width,
        ),
        name="down_layer",
    )(live_count, routed, cot_routed, small, turn, attn_out, mlp_in, d_mlp_out, *ups, *downs, pre, hidden)


def attend_back_kernel(
    capacity, live_ref, routed_ref, cot_ref, small_ref, turn_ref, attn_out_ref, d_mlp_in_ref, dot_ref, qkv_ref,
    own, other, d_routed_ref, d_attn_out_ref, d_qkv_ref, small_grads_ref, d_heads_ref,
):
    routed = routed_ref[...].astype(FULL)
    rows, features = routed.shape
    half = features // 2
    wide = qkv_ref.shape[1] // 3
    scale_qk = HEAD_DIM ** (-0.5)
    gate_prob, gate_live = gates(routed, small_ref[2:3], live_ref, capacity)
    normed_two, inverse_two = norm_forward(routed + attn_out_ref[...])
    d_middle, small_grads_ref[1:2] = norm_backward(
        d_mlp_in_ref[...], normed_two, inverse_two, small_ref[1:2]
    )
    d_attn_out = (d_middle + gate_live * cot_ref[...].astype(FULL)).astype(LOW)
    d_attn_out_ref[...] = d_attn_out
    d_heads_ref[...] = (
        product(d_attn_out[:, :half], own[1, :, wide:]) + product(d_attn_out[:, half:], other[1, :, wide:])
    ).astype(LOW)
    tile = 2 * HEAD_DIM
    for seq in range(rows // capacity):
        at = slice(seq * capacity, (seq + 1) * capacity)
        for start in range(0, wide, tile):
            query_pair = qkv_ref[at, start : start + tile]
            key_pair = qkv_ref[at, wide + start : wide + start + tile]
            val_pair = qkv_ref[at, 2 * wide + start : 2 * wide + start + tile]
            d_query, d_key, d_val = 0.0, 0.0, 0.0
            for query, key, d_head in zip(
                split_heads(query_pair), split_heads(key_pair), split_heads(d_heads_ref[at, start : start + tile])
            ):
                probs = probabilities(query, key_pair, live_ref[seq], scale_qk)
                d_val = d_val + contract_rows(probs.astype(LOW), d_head)
                d_probs = times_transposed(d_head, val_pair)
                d_scores = (
                    probs * (d_probs - jnp.sum(d_probs * probs, axis=-1, keepdims=True))
                ).astype(LOW)
                d_query = d_query + product(d_scores, key)
                d_key = d_key + contract_rows(d_scores, query)
            d_qkv_ref[at, start : start + tile] = (d_query * scale_qk).astype(LOW)
            d_qkv_ref[at, wide + start : wide + start + tile] = (d_key * scale_qk).astype(LOW)
            d_qkv_ref[at, 2 * wide + start : 2 * wide + start + tile] = d_val.astype(LOW)
    d_both = d_qkv_ref[:, : 2 * wide]
    d_vals = d_qkv_ref[:, 2 * wide :]
    d_attn_in = jnp.concatenate(
        [
            times_transposed(d_both, side[0]) + times_transposed(d_vals, side[1, :, :wide])
            for side in (own, other)
        ],
        axis=1,
    )
    normed_one, inverse_one = norm_forward(routed)
    d_from_norm, small_grads_ref[0:1] = norm_backward(d_attn_in, normed_one, inverse_one, small_ref[0:1])
    d_score = gate_live * (1.0 - gate_prob) * dot_ref[...]
    small_grads_ref[2:3] = jnp.sum(routed * d_score, axis=0, keepdims=True)
    d_routed = (d_middle + d_from_norm + d_score * small_ref[2:3]).astype(LOW)
    d_routed_ref[...] = times_transposed(d_routed, turn_ref[...]).astype(LOW)


def attend_back(live_count, routed, cot_routed, small, turn, attn_out, d_mlp_in, dot, qkv, weights, capacity):
    rows, features = routed.shape
    wide = weights[0].shape[2] // 2
    return pl.pallas_call(
        functools.partial(attend_back_kernel, capacity),
        out_shape=(
            jax.ShapeDtypeStruct((rows, features), LOW),
            jax.ShapeDtypeStruct((rows, features), LOW),
            jax.ShapeDtypeStruct((rows, 3 * wide), LOW),
            jax.ShapeDtypeStruct((3, features), FULL),
        ),
        in_specs=[pl.BlockSpec(memory_space=pltpu.SMEM)] + whole_specs(10),
        out_specs=tuple(whole_specs(4)),
        scratch_shapes=[pltpu.VMEM((rows, wide), LOW)],
        compiler_params=pltpu.CompilerParams(vmem_limit_bytes=56 << 20),
        cost_estimate=pl.CostEstimate(
            flops=8 * rows * features * wide + 10 * rows * capacity * wide,
            bytes_accessed=8 * features * wide + 14 * rows * features,
            transcendentals=rows * capacity * wide // HEAD_DIM,
        ),
        name="attend_back",
    )(live_count, routed, cot_routed, small, turn, attn_out, d_mlp_in, dot, qkv, *weights)


def grads_kernel(attn_in_ref, d_attn_out_ref, heads_ref, d_qkv_ref, kept_ref, sent_ref):
    half = attn_in_ref.shape[1] // 2
    wide = heads_ref.shape[1]
    for at, out_ref in ((slice(half, 2 * half), sent_ref), (slice(0, half), kept_ref)):
        attn_in = attn_in_ref[:, at]
        out_ref[0] = contract_rows(attn_in, d_qkv_ref[:, : 2 * wide]).astype(LOW)
        out_ref[1, :, :wide] = contract_rows(attn_in, d_qkv_ref[:, 2 * wide :]).astype(LOW)
        out_ref[1, :, wide:] = contract_rows(d_attn_out_ref[:, at], heads_ref[...]).astype(LOW)


def attend_grads(attn_in, d_attn_out, heads_out, d_qkv):
    rows, features = attn_in.shape
    wide = heads_out.shape[1]
    return pl.pallas_call(
        grads_kernel,
        out_shape=(jax.ShapeDtypeStruct((2, features // 2, 2 * wide), LOW),) * 2,
        in_specs=whole_specs(4),
        out_specs=tuple(whole_specs(2)),
        compiler_params=pltpu.CompilerParams(vmem_limit_bytes=56 << 20),
        cost_estimate=pl.CostEstimate(
            flops=8 * rows * features * wide,
            bytes_accessed=8 * features * wide + 8 * rows * features,
            transcendentals=0,
        ),
        name="attend_grads",
    )(attn_in, d_attn_out, heads_out, d_qkv)


class Exchange:
    def __init__(self, mesh):
        self.batch = mesh.shape["batch"]
        self.tensor = mesh.shape["tensor"]
        bits = []
        bit = self.batch // 2
        while bit:
            bits.append(bit)
            bit //= 2
        self.core = bits[-1]
        self.chips = bits[:-1]

    def swap(self, array, bit):
        with jax.named_scope(f"swap{bit}"):
            return lax.ppermute(array, "batch", [(i, i ^ bit) for i in range(self.batch)])

    def shift(self, array, step):
        size = self.tensor
        with jax.named_scope(f"shift{step}"):
            return lax.ppermute(array, "tensor", [(i, (i + step) % size) for i in range(size)])

    def block_order(self):
        order = [0]
        for bit in reversed([self.core] + self.chips):
            order = order + [place ^ bit for place in order]
        return order

    def gather_small(self, array):
        total = array[None]
        for bit in reversed([self.core] + self.chips):
            total = jnp.concatenate([total, self.swap(total, bit)], axis=0)
        return total.transpose(1, 0, 2).reshape(array.shape[0], -1)

    def axis(self, stream, step):
        return step if stream else len(self.chips) - 1 - step

    def swap_step(self, pair, step):
        return [self.swap(array, self.chips[self.axis(i, step)]) for i, array in enumerate(pair)]


def small_kernel(kernel, out_shape, *arrays, name):
    return pl.pallas_call(
        kernel,
        out_shape=out_shape,
        in_specs=whole_specs(len(arrays)),
        out_specs=tuple(whole_specs(len(out_shape))),
        compiler_params=pltpu.CompilerParams(vmem_limit_bytes=40 << 20),
        cost_estimate=pl.CostEstimate(
            flops=0, bytes_accessed=4 * sum(a.size for a in arrays), transcendentals=0
        ),
        name=name,
    )(*arrays)


def streams_kernel(parts, *refs):
    pieces, outs = refs[:-2], refs[-2:]
    count = len(pieces)
    width = pieces[0].shape[1] // (2 * parts)
    for stream, out_ref in enumerate(outs):
        lead = (0,) * (len(out_ref.shape) - 2)
        for i in range(parts):
            source = (stream * parts + i) * width
            for k, piece in enumerate(pieces):
                target = (i * count + k) * width
                out_ref[lead + (slice(None), slice(target, target + width))] = piece[
                    :, source : source + width
                ]


def to_streams(pieces, parts, places):
    rows, columns = pieces[0].shape
    shape = (1,) * places + (rows, columns * len(pieces) // 2)
    out = jax.ShapeDtypeStruct(shape, pieces[0].dtype)
    return small_kernel(functools.partial(streams_kernel, parts), (out, out), *pieces, name="streams")


def join_kernel(axes, stacked, *refs):
    ins, outs = refs[:4], refs[4:]
    for stream in range(2):
        for side in range(2):
            source = ins[2 * stream + side]
            at = [slice(None)] * len(source.shape)
            size = source.shape[axes[stream]]
            at[axes[stream]] = slice(side * size, (side + 1) * size)
            if stacked:
                outs[0][(stream,) + tuple(at)] = source[...]
            else:
                outs[stream][tuple(at)] = source[...]


def join(pair, arrived, axes, stacked):
    columns = pair[0].shape[-1]
    tile = min(TILE, columns)
    shapes = []
    for array, axis in zip(pair, axes):
        shape = list(array.shape)
        shape[axis] *= 2
        shapes.append(tuple(shape))
    if stacked:
        shapes = [(2,) + shapes[0]]

    def tiled(shape):
        return pl.BlockSpec(tuple(shape[:-1]) + (tile,), column_block(len(shape)))

    got = pl.pallas_call(
        functools.partial(join_kernel, axes, stacked),
        grid=(columns // tile,),
        out_shape=tuple(jax.ShapeDtypeStruct(shape, LOW) for shape in shapes),
        in_specs=[tiled(pair[i // 2].shape) for i in range(4)],
        out_specs=tuple(tiled(shape) for shape in shapes),
        compiler_params=pltpu.CompilerParams(vmem_limit_bytes=40 << 20),
        cost_estimate=pl.CostEstimate(
            flops=0, bytes_accessed=8 * sum(a.size for a in pair), transcendentals=0
        ),
        name="join",
    )(pair[0], arrived[0], pair[1], arrived[1])
    return got[0] if stacked else got


def added(refs, at):
    shape = refs[0].shape
    total = refs[0][at].astype(FULL)
    for ref in refs[1:]:
        part = ref[at] if len(ref.shape) == len(shape) else ref[...].reshape(shape)[at]
        total = total + part.astype(FULL)
    return total.astype(LOW)


def split_kernel(axes, stacked, *refs):
    ins, (kept_one, kept_two, sent_one, sent_two) = refs[:-4], refs[-4:]
    for stream, (kept_ref, sent_ref) in enumerate(((kept_one, sent_one), (kept_two, sent_two))):
        sources = ins if stacked else ins[stream::2]
        for side, out_ref in ((1, sent_ref), (0, kept_ref)):
            at = [slice(None)] * len(out_ref.shape)
            at[axes[stream]] = slice(side, side + 1)
            at = ((stream,) if stacked else ()) + tuple(at)
            out_ref[...] = added(sources, at)


def split(arrays, axes, stacked):
    full = arrays[0].shape[1:] if stacked else arrays[0].shape
    columns = full[-1]
    tile = min(TILE, columns)
    outs, specs = [], []
    for stream in range(2):
        shape = list(full if stacked else arrays[stream].shape)
        shape[axes[stream]] = 1
        outs.append(jax.ShapeDtypeStruct(tuple(shape), LOW))
        specs.append(pl.BlockSpec(tuple(shape[:-1]) + (tile,), column_block(len(shape))))
    got = pl.pallas_call(
        functools.partial(split_kernel, axes, stacked),
        grid=(columns // tile,),
        out_shape=tuple(outs * 2),
        in_specs=[
            pl.BlockSpec(leading(array, arrays[i % 2]) + (tile,), column_block(array.ndim))
            for i, array in enumerate(arrays)
        ],
        out_specs=tuple(specs * 2),
        compiler_params=pltpu.CompilerParams(vmem_limit_bytes=40 << 20),
        cost_estimate=pl.CostEstimate(
            flops=0, bytes_accessed=3 * sum(a.size for a in arrays), transcendentals=0
        ),
        name="split",
    )(*arrays)
    return got[:2], got[2:]


def leading(array, like):
    if array.ndim >= like.ndim:
        return array.shape[:-1]
    return (like.size // (like.shape[-1] * like.shape[-2]), array.shape[-2])


def split_both_kernel(up_axes, q_axes, *refs):
    ups, qs, up_kept, q_kept, messages = refs[:4], refs[4:6], refs[6:8], refs[8:10], refs[10:]
    for stream, message in enumerate(messages):
        other = q_axes.index(up_axes[stream])
        blocks = message.shape[0] - 1
        for side in (1, 0):
            at = [slice(None)] * len(up_kept[0].shape)
            at[up_axes[stream]] = slice(side, side + 1)
            up_part = added(ups[stream::2], tuple(at))
            q_part = added(qs, (other,) + tuple(at))
            if side:
                message[:blocks] = q_part.reshape((blocks,) + message.shape[1:])
                message[blocks:] = up_part.reshape((1,) + message.shape[1:])
            else:
                up_kept[stream][...] = up_part
                q_kept[other][...] = q_part


def split_both(ups, qs, up_axes, q_axes):
    columns = ups[0].shape[-1]
    tile = min(TILE, columns)
    kept = []
    for arrays, axes in ((ups, up_axes), ((qs[0][0], qs[0][1]), q_axes)):
        for stream in range(2):
            shape = list(arrays[stream].shape)
            shape[axes[stream]] = 1
            kept.append(tuple(shape))
    rows = ups[0].shape[-2]
    blocks = 1 + qs[0].size // (4 * rows * columns)
    shapes = kept + [(blocks, rows, columns)] * 2

    def tiled(shape):
        return pl.BlockSpec(tuple(shape[:-1]) + (tile,), column_block(len(shape)))

    arrays = (*ups, *qs)
    got = pl.pallas_call(
        functools.partial(split_both_kernel, up_axes, q_axes),
        grid=(columns // tile,),
        out_shape=tuple(jax.ShapeDtypeStruct(shape, LOW) for shape in shapes),
        in_specs=[tiled(array.shape) for array in arrays],
        out_specs=tuple(tiled(shape) for shape in shapes),
        compiler_params=pltpu.CompilerParams(vmem_limit_bytes=40 << 20),
        cost_estimate=pl.CostEstimate(
            flops=0, bytes_accessed=3 * sum(a.size for a in arrays), transcendentals=0
        ),
        name="split_both",
    )(*arrays)
    return got[:2], got[2:4], got[4:]


def column_block(rank):
    return lambda i: (0,) * (rank - 1) + (i,)


def pieces_kernel(parts, *refs):
    ins, outs = refs[:4], refs[4:]
    count = len(outs)
    width = outs[0].shape[1] // (2 * parts)
    flat = [ref.at[(ref.shape[0] - 1,) + (0,) * (len(ref.shape) - 3)] for ref in ins]
    for k in reversed(range(count)):
        for stream in range(2):
            for i in range(parts):
                source = (i * count + k) * width
                target = (stream * parts + i) * width
                outs[k][:, target : target + width] = added(
                    flat[stream::2], (slice(None), slice(source, source + width))
                )


def to_pieces(kept, arrived, parts, count):
    rows, columns = kept[0].shape[-2:]
    out = jax.ShapeDtypeStruct((rows, 2 * columns // count), LOW)
    return small_kernel(
        functools.partial(pieces_kernel, parts), (out,) * count, *kept, *arrived, name="pieces"
    )


def total_of(addends):
    total = addends[0].astype(FULL)
    for array in addends[1:]:
        total = total + array.astype(FULL)
    return total.astype(LOW)


def after(values, *others):
    return lax.optimization_barrier((values, others))[0]


class Line:
    def __init__(self):
        self.last = None

    def wait(self, *arrays):
        self.last = (self.last, arrays)

    def __call__(self, kernel, *arrays, **rest):
        if self.last is not None:
            arrays = after(arrays, self.last)
        out = kernel(*arrays, **rest)
        leaves = jax.tree.leaves(out)
        self.last = min(leaves, key=lambda leaf: leaf.size)
        return out


def shards(
    mesh,
    tokens,
    lengths,
    routes,
    w_query,
    w_key,
    w_value,
    w_out,
    w_up,
    w_down,
    gain_attn,
    gain_mlp,
    w_router,
    cotangent,
):
    moves = Exchange(mesh)
    device = lax.axis_index("batch")
    column = lax.axis_index("tensor")
    seq_count, capacity = routes.shape
    features = tokens.shape[1]
    tokens = tokens.reshape(seq_count, -1, features)
    cotangent = cotangent.reshape(tokens.shape)

    repeats = max(1, moves.tensor // seq_count)
    local_count = max(1, seq_count // moves.tensor)
    first = column // repeats if repeats > 1 else column * local_count
    order = (first + jnp.arange(local_count)).astype(jnp.int32)
    counts_once = (column % repeats) == 0

    def once(values):
        return jnp.where(counts_once, values, jnp.zeros_like(values)) if repeats > 1 else values

    own = features // moves.batch
    place_block = jnp.asarray(moves.block_order(), jnp.int32)
    source = ((place_block ^ device)[:, None] * own + jnp.arange(own, dtype=jnp.int32)).reshape(-1)
    turn = (jnp.arange(features, dtype=jnp.int32)[:, None] == source[None, :]).astype(LOW)

    wide = w_query.shape[1]
    steps = len(moves.chips)
    shard_q = jnp.concatenate(
        [w_query.astype(LOW), w_key.astype(LOW), w_value.astype(LOW), w_out.astype(LOW).T], axis=1
    )
    shard_u = w_up.astype(LOW)
    shard_d = w_down.astype(LOW).T

    def ring(array, hops):
        pieces = [array]
        for _ in range(hops):
            pieces.append(moves.shift(pieces[-1], 1))
        return pieces

    hops = moves.tensor - 1
    line = Line()
    rows_total = local_count * capacity
    live_count = lax.dynamic_slice_in_dim(lengths, first, local_count) // 8

    def flat(array):
        return array.reshape(rows_total, features)

    def named(name, function, *arrays):
        with jax.named_scope(name):
            return function(*arrays)

    def axes_of(step):
        return tuple(moves.axis(stream, step) for stream in range(2))

    def gather(name, pair, step):
        arrived = named(name, moves.swap_step, pair, step)
        last = step == steps - 1
        return lambda: line(lambda *a: join(a[:2], a[2:], axes_of(step), last), *pair, *arrived)

    def whole(name, stacked):
        own_side = stacked.reshape(2, features // 2, stacked.shape[-1])
        return own_side, named(name, moves.swap, own_side, moves.core)

    def first_step(name, shard):
        half = shard.shape[1] // 2
        arrived = named(name, moves.swap_step, [shard[:, :half], shard[:, half:]], 0)
        return jnp.concatenate([shard, jnp.concatenate(arrived, axis=1)], axis=0)

    def doubled(pieces, parts):
        got = line(lambda *a: to_streams(a, parts, steps), *pieces)
        pair = []
        for stream, array in enumerate(got):
            lead = [1] * steps
            lead[moves.axis(stream, 0)] = 2
            pair.append(array.reshape(tuple(lead) + (array.shape[-2] // 2, array.shape[-1])))
        return pair

    def wide_open(array):
        return once(array).reshape((2,) + (2,) * steps + (own, array.shape[-1]))

    def split_step(arrays, step, stacked):
        return split(arrays, axes_of(step), stacked)

    def together(*values):
        return lax.optimization_barrier(values)

    def place_all(pieces, table):
        kept = pieces[::repeats] if repeats > 1 else pieces
        values = jnp.concatenate(
            [piece.reshape(local_count, capacity, features) for piece in kept], axis=0
        )
        owners = ((column - jnp.arange(0, moves.tensor, repeats)) % moves.tensor).astype(jnp.int32)
        if repeats > 1:
            places = owners // repeats
        else:
            places = (owners[:, None] * local_count + jnp.arange(local_count)).reshape(-1)
        return place_rows(table, values, routes, places.astype(jnp.int32)).reshape(-1, features)

    ahead = moves.tensor // 2

    def out_both(name, array):
        with jax.named_scope("z_" + name):
            onward = [array, moves.shift(array, 1)]
            behind = [array]
            for _ in range(moves.tensor - 1 - ahead):
                behind.append(moves.shift(behind[-1], -1))
        return onward, behind[:0:-1]

    def out_on(name, onward, behind):
        onward = list(onward)
        with jax.named_scope("z_" + name):
            for _ in range(ahead - 1):
                onward.append(moves.shift(onward[-1], 1))
        return onward + list(behind)

    def sum_ahead(name, pieces):
        with jax.named_scope("z_" + name):
            fore = pieces[ahead + 1] if ahead + 1 < moves.tensor else jnp.zeros_like(pieces[0])
            for piece in pieces[ahead + 2 :]:
                fore = total_of([piece, moves.shift(fore, 1)])
            return moves.shift(fore, 1) if ahead + 1 < moves.tensor else fore

    def sum_back(name, pieces):
        with jax.named_scope("z_" + name):
            back = None
            for piece in pieces[ahead:1:-1]:
                back = moves.shift(piece if back is None else total_of([piece, back]), -1)
        return pieces[1] if back is None else total_of([pieces[1], back])

    def sum_both(name, pieces):
        return sum_ahead(name, pieces), sum_back(name, pieces)

    def sum_on(name, back):
        with jax.named_scope("z_" + name):
            return moves.shift(back, -1)

    both_q = out_both("q", shard_q)
    routed, cot_routed = pick_rows(tokens, cotangent, routes, order, local_count, turn)
    line.last = cot_routed
    both_q = after(both_q, cot_routed)
    pieces_q = out_on("q", *both_q)
    routed, cot_routed = flat(routed), flat(cot_routed)
    wide_d = first_step("out0_d", after(shard_d, shard_q))
    small = after(jnp.stack([gain_attn, gain_mlp, w_router]).astype(LOW), pieces_q)
    small = named("small", moves.gather_small, small).astype(FULL)
    pieces_q = after(pieces_q, wide_d)
    pair_q = line(lambda *a: to_streams(a, 2, steps), *pieces_q)
    both_u = out_both("u", after(shard_u, pieces_q))
    pieces_u = out_on("u", *both_u)
    line.wait(both_u, small)
    for step in range(steps - 1):
        pair_q = gather(f"out{step}_q", pair_q, step)()
    joined_q = gather("last_q", pair_q, steps - 1)
    pair_u = line(lambda *a: to_streams(a, 1, steps), *pieces_u)
    joined_u = gather("out0_u", pair_u, 0)
    pieces_d = named("z_d", ring, after(wide_d, pieces_u), hops)
    line.wait(pieces_d[1])
    attn_weights = whole("core_q", joined_q())
    line.wait(pieces_d[2 % moves.tensor])
    for step in range(1, steps):
        joined_u = gather(f"out{step}_u", joined_u(), step)
    attn_in, qkv, heads_out, attn_out, mlp_in, d_mlp_out = line(
        lambda *a: attend(*a[:4], a[4:], capacity), live_count, routed, cot_routed, small, *attn_weights
    )
    pair_d = doubled(pieces_d, 1)
    for step in range(1, steps - 1):
        pair_d = gather(f"out{step}_d", pair_d, step)()
    joined_d = gather("last_d", pair_d, steps - 1)
    ups = whole("core_u", joined_u())
    pre, hidden, dn_kept, dn_sent = line(
        lambda *a: up_layer(*a[:2], a[2:]), mlp_in, d_mlp_out, *ups
    )
    joined_d = joined_d()

    joined_d, dn_kept, dn_sent = together(joined_d, dn_kept, dn_sent)
    dn_arrived = named("core_dn", moves.swap, once(dn_sent), moves.core)
    downs = whole("core_d", joined_d)
    dn = (wide_open(dn_kept), wide_open(dn_arrived))

    last = steps - 1
    dn_kept, dn_sent = split_step(dn, last, True)
    dn_sent, *rest = after((dn_sent, mlp_in, pre, hidden), downs)
    dn_sent, rest = together(dn_sent, rest)
    dn_arrived = named("back_dn", moves.swap_step, dn_sent, last)
    update, d_mlp_in, dot, up_kept, up_sent = down_layer(
        live_count, routed, cot_routed, small, turn, attn_out, rest[0], d_mlp_out, ups, downs, *rest[1:], capacity
    )
    dn = (*dn_kept, *dn_arrived)
    for step in reversed(range(1, last)):
        dn_kept, dn_sent = split_step(dn, step, False)
        dn = (*dn_kept, *named("back_dn", moves.swap_step, dn_sent, step))

    def halve_small(array, bit):
        mine = array.shape[1] // 2
        with jax.named_scope("small"):
            return array[:, :mine] + moves.swap(array[:, mine:], bit)

    def spread_small(array, bit):
        with jax.named_scope("small"):
            pairs = [(i, i ^ bit) for i in range(moves.tensor)]
            return array + lax.ppermute(array, "tensor", pairs)

    def from_behind(name, rows):
        pieces = [rows]
        with jax.named_scope("z_" + name):
            for _ in range(moves.tensor - 1 - ahead):
                pieces.append(moves.shift(pieces[-1], -1))
        return pieces[:0:-1]

    dn, update, d_mlp_in, dot, up_kept, up_sent = together(dn, update, d_mlp_in, dot, up_kept, up_sent)
    up_arrived = named("core_up", moves.swap, once(up_sent), moves.core)
    dn_kept, dn_sent = split_step(dn, 0, False)
    dn = (*dn_kept, *named("back0_dn", moves.swap_step, dn_sent, 0))
    with jax.named_scope("z_update"):
        next_update = moves.shift(update, 1)
    behind_update = from_behind("update", update)
    d_routed, d_attn_out, d_qkv, small_grads = attend_back(
        live_count, routed, cot_routed, small, turn, attn_out, d_mlp_in, dot, qkv, attn_weights, capacity
    )
    q_kept, q_sent = attend_grads(attn_in, d_attn_out, heads_out, d_qkv)

    up_kept, up_arrived, dn, update, next_update, behind_update, d_routed, small_grads, q_kept, q_sent = together(
        up_kept, up_arrived, dn, update, next_update, behind_update, d_routed, small_grads, q_kept, q_sent
    )
    up_kept, up_sent = split_step((wide_open(up_kept), wide_open(up_arrived)), last, True)
    up = (*up_kept, *named("back1_up", moves.swap_step, up_sent, last))
    q_arrived = named("core_q", moves.swap, once(q_sent), moves.core)
    updates = out_on("update", (update, next_update), behind_update)
    with jax.named_scope("z_routed"):
        next_routed = moves.shift(d_routed, 1)
    dn_pieces = to_pieces(dn[:2], dn[2:], 1, moves.tensor)
    small_grads = once(small_grads)
    for step in reversed(range(1, last)):
        up_kept, up_sent = split_step(up, step, False)
        up = (*up_kept, *named("back_up", moves.swap_step, up_sent, step))

    up, q_kept, q_arrived, updates, d_routed, next_routed, dn_pieces, small_grads = together(
        up, q_kept, q_arrived, updates, d_routed, next_routed, dn_pieces, small_grads
    )
    ends = axes_of(0)
    up_kept, q_kept, messages = split_both(
        up, (wide_open(q_kept), wide_open(q_arrived)), ends, axes_of(last)
    )
    with jax.named_scope("back_both"):
        messages = [moves.swap(part, moves.chips[axis]) for part, axis in zip(messages, ends)]
    up = (*up_kept, *messages)
    q = (*q_kept, *reversed(messages))
    d_routeds = out_on("routed", (d_routed, next_routed), ())
    output = place_all(updates, tokens)
    behind_routed = from_behind("routed", d_routed)
    back_dn = sum_back("dn", dn_pieces)
    for step in reversed(range(1, last)):
        q_kept, q_sent = split_step(q, step, False)
        q = (*q_kept, *named("back_q", moves.swap_step, q_sent, step))

    q, up, d_routeds, behind_routed, output, small_grads, dn_pieces, back_dn = together(
        q, up, d_routeds, behind_routed, output, small_grads, dn_pieces, back_dn
    )
    q_kept, q_sent = split_step(q, 0, False)
    q = (*q_kept, *named("back0_q", moves.swap_step, q_sent, 0))
    fore_dn = sum_ahead("dn", dn_pieces)
    last_dn = sum_on("dn", back_dn)
    up_pieces = to_pieces(up[:2], up[2:], 1, moves.tensor)
    back_up = sum_back("up", up_pieces)

    q, fore_dn, last_dn, up_pieces, back_up, small_grads, d_routeds = together(
        q, fore_dn, last_dn, up_pieces, back_up, small_grads, d_routeds
    )
    q_pieces = to_pieces(q[:2], q[2:], 2, moves.tensor)
    both_q = sum_both("q", q_pieces)
    last_up = sum_on("up", back_up)
    fore_up = sum_ahead("up", up_pieces)
    grad_tokens = place_all(list(d_routeds) + list(behind_routed), cotangent)
    for bit in (moves.core, *moves.chips):
        small_grads = halve_small(small_grads, bit)
    small_grads = spread_small(small_grads, 1)

    both_q, last_up, fore_up, grad_tokens, small_grads = together(
        both_q, last_up, fore_up, grad_tokens, small_grads
    )
    last_q = sum_on("q", both_q[1])
    bit = 2
    while bit < moves.tensor:
        small_grads = spread_small(small_grads, bit)
        bit *= 2
    grad_d = total_of([dn_pieces[0], fore_dn, last_dn])
    grad_q = total_of([q_pieces[0], both_q[0], last_q])
    grad_u = total_of([up_pieces[0], fore_up, last_up])

    return (
        output,
        grad_tokens,
        grad_q[:, :wide].astype(FULL),
        grad_q[:, wide : 2 * wide].astype(FULL),
        grad_q[:, 2 * wide : 3 * wide].astype(FULL),
        grad_q[:, 3 * wide :].T.astype(FULL),
        grad_u.astype(FULL),
        grad_d.T.astype(FULL),
        small_grads[0],
        small_grads[1],
        small_grads[2],
    )


def solution(mesh):
    in_specs = (
        P("batch", None),
        P("batch"),
        P("batch", None),
        P("batch", "tensor"),
        P("batch", "tensor"),
        P("batch", "tensor"),
        P("tensor", "batch"),
        P("batch", "tensor"),
        P("tensor", "batch"),
        P("batch"),
        P("batch"),
        P("batch"),
        P("batch", None),
    )
    out_specs = (
        P("batch", None),
        P("batch", None),
        P("batch", "tensor"),
        P("batch", "tensor"),
        P("batch", "tensor"),
        P("tensor", "batch"),
        P("batch", "tensor"),
        P("tensor", "batch"),
        P("batch"),
        P("batch"),
        P("batch"),
    )
    return jax.shard_map(
        functools.partial(shards, mesh),
        mesh=mesh,
        in_specs=in_specs,
        out_specs=out_specs,
        check_vma=False,
    )
```

```python
import functools

import jax
import jax.numpy as jnp
from jax import lax
from jax.experimental import pallas as pl
from jax.experimental.pallas import tpu as pltpu
from jax.sharding import PartitionSpec as P

HEAD_DIM = 64
SLOT_BLOCK = 512
PLACE_BLOCK = 2048
EPSILON = 1e-06


CURVE = 0.7978845608028654
CUBIC = 0.044715


def gelu_tanh(values):
    return 0.5 * values * (1.0 + jnp.tanh(CURVE * (values + CUBIC * values * values * values)))


def gelu_slope(values):
    square = values * values
    bend = jnp.tanh(CURVE * (values + CUBIC * values * square))
    inner = CURVE * (1.0 + 3.0 * CUBIC * square)
    return 0.5 * (1.0 + bend) + 0.5 * values * (1.0 - bend * bend) * inner


def product(left, right):
    return jnp.dot(left, right, preferred_element_type=jnp.float32)


def contract_rows(left, right):
    return lax.dot_general(
        left, right, (((0,), (0,)), ((), ())), preferred_element_type=jnp.float32
    )


def times_transposed(left, right):
    return lax.dot_general(
        left, right, (((1,), (1,)), ((), ())), preferred_element_type=jnp.float32
    )


def norm_backward(d_normed_in, normed, inverse, gain_vec):
    d_scaled = d_normed_in * gain_vec
    d_input = inverse * (d_scaled - normed * jnp.mean(d_scaled * normed, axis=-1, keepdims=True))
    return (d_input, jnp.sum(d_normed_in * normed, axis=0, keepdims=True))


def norm_forward(values):
    inverse = lax.rsqrt(jnp.mean(values * values, axis=-1, keepdims=True) + EPSILON)
    return (values * inverse, inverse)


LOW = jnp.bfloat16
FULL = jnp.float32


def pick_kernel(order_ref, routes_ref, turn_ref, tokens_ref, cot_ref, routed_ref, cot_routed_ref, total, cot_total):
    block = pl.program_id(1)
    capacity = routes_ref.shape[1]
    slots = tokens_ref.shape[1]
    column = lax.broadcasted_iota(jnp.int32, (capacity, slots), 1) + block * slots
    chooser = (routes_ref[0] == column).astype(LOW)
    part = product(chooser, tokens_ref[0])
    cot_part = product(chooser, cot_ref[0])

    @pl.when(block == 0)
    def _():
        total[...] = part
        cot_total[...] = cot_part

    @pl.when(block > 0)
    def _():
        total[...] += part
        cot_total[...] += cot_part

    @pl.when(block == pl.num_programs(1) - 1)
    def _():
        routed_ref[0] = product(total[...].astype(LOW), turn_ref[...]).astype(LOW)
        cot_routed_ref[0] = product(cot_total[...].astype(LOW), turn_ref[...]).astype(LOW)


def pick_rows(tokens, cotangent, routes, order, count, turn):
    seq_count, slots, features = tokens.shape
    capacity = routes.shape[1]
    per_block = min(SLOT_BLOCK, slots)
    table = pl.BlockSpec((1, per_block, features), lambda i, j, order: (order[i], j, 0))
    picked = pl.BlockSpec((1, capacity, features), lambda i, j, order: (i, 0, 0))
    shape = jax.ShapeDtypeStruct((count, capacity, features), LOW)
    return pl.pallas_call(
        pick_kernel,
        out_shape=(shape, shape),
        grid_spec=pltpu.PrefetchScalarGridSpec(
            num_scalar_prefetch=1,
            grid=(count, slots // per_block),
            in_specs=[
                pl.BlockSpec((1, capacity, 1), lambda i, j, order: (order[i], 0, 0)),
                pl.BlockSpec((features, features), lambda i, j, order: (0, 0)),
                table,
                table,
            ],
            out_specs=[picked, picked],
            scratch_shapes=[pltpu.VMEM((capacity, features), FULL)] * 2,
        ),
        compiler_params=pltpu.CompilerParams(vmem_limit_bytes=48 << 20),
        cost_estimate=pl.CostEstimate(
            flops=4 * count * capacity * slots * features,
            bytes_accessed=4 * count * slots * features,
            transcendentals=0,
        ),
        name="pick_rows",
    )(order, routes[:, :, None], turn, tokens, cotangent)


def place_kernel(order_ref, routes_ref, table_ref, values_ref, out_ref):
    block = pl.program_id(1)
    slots = table_ref.shape[1]
    capacity = routes_ref.shape[2]
    row = lax.broadcasted_iota(jnp.int32, (slots, capacity), 0) + block * slots
    chooser = (routes_ref[0] == row).astype(LOW)
    placed = product(chooser, values_ref[0])
    out_ref[0] = (table_ref[0].astype(FULL) + placed).astype(LOW)


def place_rows(table, values, routes, order):
    seq_count, slots, features = table.shape
    capacity = routes.shape[1]
    per_block = min(PLACE_BLOCK, slots)
    tall = pl.BlockSpec((1, per_block, features), lambda i, j, order: (order[i], j, 0))
    return pl.pallas_call(
        place_kernel,
        out_shape=jax.ShapeDtypeStruct(table.shape, table.dtype),
        grid_spec=pltpu.PrefetchScalarGridSpec(
            num_scalar_prefetch=1,
            grid=(seq_count, slots // per_block),
            in_specs=[
                pl.BlockSpec((1, 1, capacity), lambda i, j, order: (order[i], 0, 0)),
                tall,
                pl.BlockSpec((1, capacity, features), lambda i, j, order: (i, 0, 0)),
            ],
            out_specs=tall,
        ),
        compiler_params=pltpu.CompilerParams(vmem_limit_bytes=56 << 20),
        cost_estimate=pl.CostEstimate(
            flops=2 * seq_count * capacity * slots * features,
            bytes_accessed=4 * seq_count * slots * features,
            transcendentals=0,
        ),
        name="place_rows",
    )(order, routes[:, None, :], table, values)


def gates(routed, router_vec, live_ref, capacity):
    rows = routed.shape[0]
    score = jnp.sum(routed * router_vec, axis=-1, keepdims=True)
    gate_prob = 1.0 / (1.0 + jnp.exp(-score))
    live = [
        lax.broadcasted_iota(jnp.int32, (capacity, 1), 0) < live_ref[seq]
        for seq in range(rows // capacity)
    ]
    live = live[0] if len(live) == 1 else jnp.concatenate(live, axis=0)
    return gate_prob, jnp.where(live, gate_prob, 0.0)


def probabilities(queries, keys_all, live_count, scale_qk):
    scores = times_transposed(queries, keys_all) * scale_qk
    row = lax.broadcasted_iota(jnp.int32, scores.shape, 0)
    column = lax.broadcasted_iota(jnp.int32, scores.shape, 1)
    masked = jnp.where((column <= row) & (column < live_count), scores, -1e30)
    exp_scores = jnp.exp(masked - jnp.max(masked, axis=-1, keepdims=True))
    return exp_scores / jnp.sum(exp_scores, axis=-1, keepdims=True)


def split_heads(pair):
    owner = lax.broadcasted_iota(jnp.int32, pair.shape, 1) // HEAD_DIM
    return [jnp.where(owner == i, pair, jnp.zeros_like(pair)) for i in range(pair.shape[1] // HEAD_DIM)]


def attend_kernel(
    capacity, live_ref, routed_ref, cot_ref, small_ref, own, other,
    attn_in_ref, qkv_ref, heads_ref, attn_out_ref, mlp_in_ref, d_mlp_out_ref,
):
    routed = routed_ref[...].astype(FULL)
    rows, features = routed.shape
    half = features // 2
    wide = qkv_ref.shape[1] // 3
    _, gate_live = gates(routed, small_ref[2:3], live_ref, capacity)
    d_mlp_out_ref[...] = (gate_live * cot_ref[...].astype(FULL)).astype(LOW)
    normed, _ = norm_forward(routed)
    attn_in = (normed * small_ref[0:1]).astype(LOW)
    attn_in_ref[...] = attn_in
    left, right = attn_in[:, :half], attn_in[:, half:]
    qkv_ref[:, : 2 * wide] = (product(left, own[0]) + product(right, other[0])).astype(LOW)
    qkv_ref[:, 2 * wide :] = (
        product(left, own[1, :, :wide]) + product(right, other[1, :, :wide])
    ).astype(LOW)
    tile = 2 * HEAD_DIM
    for seq in range(rows // capacity):
        at = slice(seq * capacity, (seq + 1) * capacity)
        for start in range(0, wide, tile):
            keys_all = qkv_ref[at, wide + start : wide + start + tile]
            queries = split_heads(qkv_ref[at, start : start + tile])
            vals = split_heads(qkv_ref[at, 2 * wide + start : 2 * wide + start + tile])
            total = None
            for query, val in zip(queries, vals):
                probs = probabilities(query, keys_all, live_ref[seq], HEAD_DIM ** (-0.5))
                part = product(probs.astype(LOW), val)
                total = part if total is None else total + part
            heads_ref[at, start : start + tile] = total.astype(LOW)
    heads_out = heads_ref[...]
    attn_out_ref[:, :half] = times_transposed(heads_out, own[1, :, wide:])
    attn_out_ref[:, half:] = times_transposed(heads_out, other[1, :, wide:])
    normed_two, _ = norm_forward(routed + attn_out_ref[...])
    mlp_in_ref[...] = (normed_two * small_ref[1:2]).astype(LOW)


def whole_specs(count):
    return [pl.BlockSpec(memory_space=pltpu.VMEM)] * count


def attend(live_count, routed, cot_routed, small, weights, capacity):
    rows, features = routed.shape
    wide = weights[0].shape[2] // 2
    return pl.pallas_call(
        functools.partial(attend_kernel, capacity),
        out_shape=(
            jax.ShapeDtypeStruct((rows, features), LOW),
            jax.ShapeDtypeStruct((rows, 3 * wide), LOW),
            jax.ShapeDtypeStruct((rows, wide), LOW),
            jax.ShapeDtypeStruct((rows, features), FULL),
            jax.ShapeDtypeStruct((rows, features), LOW),
            jax.ShapeDtypeStruct((rows, features), LOW),
        ),
        in_specs=[pl.BlockSpec(memory_space=pltpu.SMEM)] + whole_specs(5),
        out_specs=tuple(whole_specs(6)),
        compiler_params=pltpu.CompilerParams(vmem_limit_bytes=56 << 20),
        cost_estimate=pl.CostEstimate(
            flops=8 * rows * features * wide + 4 * rows * capacity * wide,
            bytes_accessed=8 * features * wide + 14 * rows * features,
            transcendentals=rows * capacity * wide // HEAD_DIM,
        ),
        name="attend",
    )(live_count, routed, cot_routed, small, *weights)


def up_kernel(mlp_in_ref, d_mlp_out_ref, own, other, pre_ref, hidden_ref, kept_ref, sent_ref):
    mlp_in = mlp_in_ref[...]
    d_mlp_out = d_mlp_out_ref[...]
    half = mlp_in.shape[1] // 2
    for stream in range(2):
        pre = product(mlp_in[:, :half], own[stream]) + product(mlp_in[:, half:], other[stream])
        hidden = gelu_tanh(pre).astype(LOW)
        pre_ref[stream] = pre
        hidden_ref[stream] = hidden
        sent_ref[stream] = contract_rows(d_mlp_out[:, half:], hidden).astype(LOW)
        kept_ref[stream] = contract_rows(d_mlp_out[:, :half], hidden).astype(LOW)


TILE = 512


def up_layer(mlp_in, d_mlp_out, ups):
    rows, features = mlp_in.shape
    streams, half, width = ups[0].shape
    tile = min(TILE, width)
    whole = pl.BlockSpec((rows, features), lambda i: (0, 0))
    weight = pl.BlockSpec((streams, half, tile), lambda i: (0, 0, i))
    tall = pl.BlockSpec((streams, rows, tile), lambda i: (0, 0, i))
    return pl.pallas_call(
        up_kernel,
        grid=(width // tile,),
        out_shape=(
            jax.ShapeDtypeStruct((streams, rows, width), FULL),
            jax.ShapeDtypeStruct((streams, rows, width), LOW),
            jax.ShapeDtypeStruct(ups[0].shape, LOW),
            jax.ShapeDtypeStruct(ups[0].shape, LOW),
        ),
        in_specs=[whole, whole, weight, weight],
        out_specs=(tall, tall, weight, weight),
        compiler_params=pltpu.CompilerParams(vmem_limit_bytes=56 << 20),
        cost_estimate=pl.CostEstimate(
            flops=8 * rows * features * width,
            bytes_accessed=8 * features * width + 12 * rows * width,
            transcendentals=2 * rows * width,
        ),
        name="up_layer",
    )(mlp_in, d_mlp_out, *ups)


def down_kernel(
    capacity, live_ref, routed_ref, cot_ref, small_ref, turn_ref, attn_out_ref, mlp_in_ref, d_mlp_out_ref,
    up_own, up_other, down_own, down_other, pre_ref, hidden_ref,
    update_ref, d_mlp_in_ref, dot_ref, kept_ref, sent_ref, mlp_out,
):
    mlp_in = mlp_in_ref[...]
    d_mlp_out = d_mlp_out_ref[...]
    half = mlp_in.shape[1] // 2

    @pl.when(pl.program_id(0) == 0)
    def _():
        mlp_out[...] = jnp.zeros_like(mlp_out)
        d_mlp_in_ref[...] = jnp.zeros_like(d_mlp_in_ref)

    for stream in range(2):
        d_hidden = product(d_mlp_out[:, :half], down_own[stream]) + product(
            d_mlp_out[:, half:], down_other[stream]
        )
        d_pre = (d_hidden * gelu_slope(pre_ref[stream])).astype(LOW)
        sent_ref[stream] = contract_rows(mlp_in[:, half:], d_pre).astype(LOW)
        kept_ref[stream] = contract_rows(mlp_in[:, :half], d_pre).astype(LOW)
        d_mlp_in_ref[:, :half] += times_transposed(d_pre, up_own[stream])
        d_mlp_in_ref[:, half:] += times_transposed(d_pre, up_other[stream])
        hidden = hidden_ref[stream]
        mlp_out[:, :half] += times_transposed(hidden, down_own[stream])
        mlp_out[:, half:] += times_transposed(hidden, down_other[stream])

    @pl.when(pl.program_id(0) == pl.num_programs(0) - 1)
    def _():
        _, gate_live = gates(routed_ref[...].astype(FULL), small_ref[2:3], live_ref, capacity)
        branch = attn_out_ref[...] + mlp_out[...]
        update = (gate_live * branch).astype(LOW)
        update_ref[...] = times_transposed(update, turn_ref[...]).astype(LOW)
        dot_ref[...] = jnp.sum(cot_ref[...].astype(FULL) * branch, axis=-1, keepdims=True)


def down_layer(live_count, routed, cot_routed, small, turn, attn_out, mlp_in, d_mlp_out, ups, downs, pre, hidden, capacity):
    rows, features = mlp_in.shape
    streams, half, width = ups[0].shape
    tile = min(TILE, width)
    whole = pl.BlockSpec((rows, features), lambda i: (0, 0))
    weight = pl.BlockSpec((streams, half, tile), lambda i: (0, 0, i))
    tall = pl.BlockSpec((streams, rows, tile), lambda i: (0, 0, i))
    return pl.pallas_call(
        functools.partial(down_kernel, capacity),
        grid=(width // tile,),
        out_shape=(
            jax.ShapeDtypeStruct((rows, features), LOW),
            jax.ShapeDtypeStruct((rows, features), FULL),
            jax.ShapeDtypeStruct((rows, 1), FULL),
            jax.ShapeDtypeStruct(ups[0].shape, LOW),
            jax.ShapeDtypeStruct(ups[0].shape, LOW),
        ),
        in_specs=[
            pl.BlockSpec(memory_space=pltpu.SMEM),
            whole,
            whole,
            pl.BlockSpec(small.shape, lambda i: (0, 0)),
            pl.BlockSpec(turn.shape, lambda i: (0, 0)),
            whole,
            whole,
            whole,
        ]
        + [weight] * 4
        + [tall] * 2,
        out_specs=(whole, whole, pl.BlockSpec((rows, 1), lambda i: (0, 0)), weight, weight),
        scratch_shapes=[pltpu.VMEM((rows, features), FULL)],
        compiler_params=pltpu.CompilerParams(vmem_limit_bytes=56 << 20),
        cost_estimate=pl.CostEstimate(
            flops=16 * rows * features * width,
            bytes_accessed=12 * features * width + 12 * rows * width,
            transcendentals=2 * rows * width,
        ),
        name="down_layer",
    )(live_count, routed, cot_routed, small, turn, attn_out, mlp_in, d_mlp_out, *ups, *downs, pre, hidden)


def attend_back_kernel(
    capacity, live_ref, routed_ref, cot_ref, small_ref, turn_ref, attn_out_ref, d_mlp_in_ref, dot_ref, qkv_ref,
    own, other, d_routed_ref, d_attn_out_ref, d_qkv_ref, small_grads_ref, d_heads_ref,
):
    routed = routed_ref[...].astype(FULL)
    rows, features = routed.shape
    half = features // 2
    wide = qkv_ref.shape[1] // 3
    scale_qk = HEAD_DIM ** (-0.5)
    gate_prob, gate_live = gates(routed, small_ref[2:3], live_ref, capacity)
    normed_two, inverse_two = norm_forward(routed + attn_out_ref[...])
    d_middle, small_grads_ref[1:2] = norm_backward(
        d_mlp_in_ref[...], normed_two, inverse_two, small_ref[1:2]
    )
    d_attn_out = (d_middle + gate_live * cot_ref[...].astype(FULL)).astype(LOW)
    d_attn_out_ref[...] = d_attn_out
    d_heads_ref[...] = (
        product(d_attn_out[:, :half], own[1, :, wide:]) + product(d_attn_out[:, half:], other[1, :, wide:])
    ).astype(LOW)
    tile = 2 * HEAD_DIM
    for seq in range(rows // capacity):
        at = slice(seq * capacity, (seq + 1) * capacity)
        for start in range(0, wide, tile):
            query_pair = qkv_ref[at, start : start + tile]
            key_pair = qkv_ref[at, wide + start : wide + start + tile]
            val_pair = qkv_ref[at, 2 * wide + start : 2 * wide + start + tile]
            d_query, d_key, d_val = 0.0, 0.0, 0.0
            for query, key, d_head in zip(
                split_heads(query_pair), split_heads(key_pair), split_heads(d_heads_ref[at, start : start + tile])
            ):
                probs = probabilities(query, key_pair, live_ref[seq], scale_qk)
                d_val = d_val + contract_rows(probs.astype(LOW), d_head)
                d_probs = times_transposed(d_head, val_pair)
                d_scores = (
                    probs * (d_probs - jnp.sum(d_probs * probs, axis=-1, keepdims=True))
                ).astype(LOW)
                d_query = d_query + product(d_scores, key)
                d_key = d_key + contract_rows(d_scores, query)
            d_qkv_ref[at, start : start + tile] = (d_query * scale_qk).astype(LOW)
            d_qkv_ref[at, wide + start : wide + start + tile] = (d_key * scale_qk).astype(LOW)
            d_qkv_ref[at, 2 * wide + start : 2 * wide + start + tile] = d_val.astype(LOW)
    d_both = d_qkv_ref[:, : 2 * wide]
    d_vals = d_qkv_ref[:, 2 * wide :]
    d_attn_in = jnp.concatenate(
        [
            times_transposed(d_both, side[0]) + times_transposed(d_vals, side[1, :, :wide])
            for side in (own, other)
        ],
        axis=1,
    )
    normed_one, inverse_one = norm_forward(routed)
    d_from_norm, small_grads_ref[0:1] = norm_backward(d_attn_in, normed_one, inverse_one, small_ref[0:1])
    d_score = gate_live * (1.0 - gate_prob) * dot_ref[...]
    small_grads_ref[2:3] = jnp.sum(routed * d_score, axis=0, keepdims=True)
    d_routed = (d_middle + d_from_norm + d_score * small_ref[2:3]).astype(LOW)
    d_routed_ref[...] = times_transposed(d_routed, turn_ref[...]).astype(LOW)


def attend_back(live_count, routed, cot_routed, small, turn, attn_out, d_mlp_in, dot, qkv, weights, capacity):
    rows, features = routed.shape
    wide = weights[0].shape[2] // 2
    return pl.pallas_call(
        functools.partial(attend_back_kernel, capacity),
        out_shape=(
            jax.ShapeDtypeStruct((rows, features), LOW),
            jax.ShapeDtypeStruct((rows, features), LOW),
            jax.ShapeDtypeStruct((rows, 3 * wide), LOW),
            jax.ShapeDtypeStruct((3, features), FULL),
        ),
        in_specs=[pl.BlockSpec(memory_space=pltpu.SMEM)] + whole_specs(10),
        out_specs=tuple(whole_specs(4)),
        scratch_shapes=[pltpu.VMEM((rows, wide), LOW)],
        compiler_params=pltpu.CompilerParams(vmem_limit_bytes=56 << 20),
        cost_estimate=pl.CostEstimate(
            flops=8 * rows * features * wide + 10 * rows * capacity * wide,
            bytes_accessed=8 * features * wide + 14 * rows * features,
            transcendentals=rows * capacity * wide // HEAD_DIM,
        ),
        name="attend_back",
    )(live_count, routed, cot_routed, small, turn, attn_out, d_mlp_in, dot, qkv, *weights)


def grads_kernel(attn_in_ref, d_attn_out_ref, heads_ref, d_qkv_ref, kept_ref, sent_ref):
    half = attn_in_ref.shape[1] // 2
    wide = heads_ref.shape[1]
    for at, out_ref in ((slice(half, 2 * half), sent_ref), (slice(0, half), kept_ref)):
        attn_in = attn_in_ref[:, at]
        out_ref[0] = contract_rows(attn_in, d_qkv_ref[:, : 2 * wide]).astype(LOW)
        out_ref[1, :, :wide] = contract_rows(attn_in, d_qkv_ref[:, 2 * wide :]).astype(LOW)
        out_ref[1, :, wide:] = contract_rows(d_attn_out_ref[:, at], heads_ref[...]).astype(LOW)


def attend_grads(attn_in, d_attn_out, heads_out, d_qkv):
    rows, features = attn_in.shape
    wide = heads_out.shape[1]
    return pl.pallas_call(
        grads_kernel,
        out_shape=(jax.ShapeDtypeStruct((2, features // 2, 2 * wide), LOW),) * 2,
        in_specs=whole_specs(4),
        out_specs=tuple(whole_specs(2)),
        compiler_params=pltpu.CompilerParams(vmem_limit_bytes=56 << 20),
        cost_estimate=pl.CostEstimate(
            flops=8 * rows * features * wide,
            bytes_accessed=8 * features * wide + 8 * rows * features,
            transcendentals=0,
        ),
        name="attend_grads",
    )(attn_in, d_attn_out, heads_out, d_qkv)


class Exchange:
    def __init__(self, mesh):
        self.batch = mesh.shape["batch"]
        self.tensor = mesh.shape["tensor"]
        bits = []
        bit = self.batch // 2
        while bit:
            bits.append(bit)
            bit //= 2
        self.core = bits[-1]
        self.chips = bits[:-1]

    def swap(self, array, bit):
        with jax.named_scope(f"swap{bit}"):
            return lax.ppermute(array, "batch", [(i, i ^ bit) for i in range(self.batch)])

    def shift(self, array, step):
        size = self.tensor
        with jax.named_scope(f"shift{step}"):
            return lax.ppermute(array, "tensor", [(i, (i + step) % size) for i in range(size)])

    def block_order(self):
        order = [0]
        for bit in reversed([self.core] + self.chips):
            order = order + [place ^ bit for place in order]
        return order

    def gather_small(self, array):
        total = array[None]
        for bit in reversed([self.core] + self.chips):
            total = jnp.concatenate([total, self.swap(total, bit)], axis=0)
        return total.transpose(1, 0, 2).reshape(array.shape[0], -1)

    def axis(self, stream, step):
        return step if stream else len(self.chips) - 1 - step

    def swap_step(self, pair, step):
        return [self.swap(array, self.chips[self.axis(i, step)]) for i, array in enumerate(pair)]


def small_kernel(kernel, out_shape, *arrays, name):
    return pl.pallas_call(
        kernel,
        out_shape=out_shape,
        in_specs=whole_specs(len(arrays)),
        out_specs=tuple(whole_specs(len(out_shape))),
        compiler_params=pltpu.CompilerParams(vmem_limit_bytes=40 << 20),
        cost_estimate=pl.CostEstimate(
            flops=0, bytes_accessed=4 * sum(a.size for a in arrays), transcendentals=0
        ),
        name=name,
    )(*arrays)


def streams_kernel(parts, *refs):
    pieces, outs = refs[:-2], refs[-2:]
    count = len(pieces)
    width = pieces[0].shape[1] // (2 * parts)
    for stream, out_ref in enumerate(outs):
        lead = (0,) * (len(out_ref.shape) - 2)
        for i in range(parts):
            source = (stream * parts + i) * width
            for k, piece in enumerate(pieces):
                target = (i * count + k) * width
                out_ref[lead + (slice(None), slice(target, target + width))] = piece[
                    :, source : source + width
                ]


def to_streams(pieces, parts, places):
    rows, columns = pieces[0].shape
    shape = (1,) * places + (rows, columns * len(pieces) // 2)
    out = jax.ShapeDtypeStruct(shape, pieces[0].dtype)
    return small_kernel(functools.partial(streams_kernel, parts), (out, out), *pieces, name="streams")


def join_kernel(axes, stacked, *refs):
    ins, outs = refs[:4], refs[4:]
    for stream in range(2):
        for side in range(2):
            source = ins[2 * stream + side]
            at = [slice(None)] * len(source.shape)
            size = source.shape[axes[stream]]
            at[axes[stream]] = slice(side * size, (side + 1) * size)
            if stacked:
                outs[0][(stream,) + tuple(at)] = source[...]
            else:
                outs[stream][tuple(at)] = source[...]


def join(pair, arrived, axes, stacked):
    columns = pair[0].shape[-1]
    tile = min(TILE, columns)
    shapes = []
    for array, axis in zip(pair, axes):
        shape = list(array.shape)
        shape[axis] *= 2
        shapes.append(tuple(shape))
    if stacked:
        shapes = [(2,) + shapes[0]]

    def tiled(shape):
        return pl.BlockSpec(tuple(shape[:-1]) + (tile,), column_block(len(shape)))

    got = pl.pallas_call(
        functools.partial(join_kernel, axes, stacked),
        grid=(columns // tile,),
        out_shape=tuple(jax.ShapeDtypeStruct(shape, LOW) for shape in shapes),
        in_specs=[tiled(pair[i // 2].shape) for i in range(4)],
        out_specs=tuple(tiled(shape) for shape in shapes),
        compiler_params=pltpu.CompilerParams(vmem_limit_bytes=40 << 20),
        cost_estimate=pl.CostEstimate(
            flops=0, bytes_accessed=8 * sum(a.size for a in pair), transcendentals=0
        ),
        name="join",
    )(pair[0], arrived[0], pair[1], arrived[1])
    return got[0] if stacked else got


def added(refs, at):
    shape = refs[0].shape
    total = refs[0][at].astype(FULL)
    for ref in refs[1:]:
        part = ref[at] if len(ref.shape) == len(shape) else ref[...].reshape(shape)[at]
        total = total + part.astype(FULL)
    return total.astype(LOW)


def split_kernel(axes, stacked, *refs):
    ins, (kept_one, kept_two, sent_one, sent_two) = refs[:-4], refs[-4:]
    for stream, (kept_ref, sent_ref) in enumerate(((kept_one, sent_one), (kept_two, sent_two))):
        sources = ins if stacked else ins[stream::2]
        for side, out_ref in ((1, sent_ref), (0, kept_ref)):
            at = [slice(None)] * len(out_ref.shape)
            at[axes[stream]] = slice(side, side + 1)
            at = ((stream,) if stacked else ()) + tuple(at)
            out_ref[...] = added(sources, at)


def split(arrays, axes, stacked):
    full = arrays[0].shape[1:] if stacked else arrays[0].shape
    columns = full[-1]
    tile = min(TILE, columns)
    outs, specs = [], []
    for stream in range(2):
        shape = list(full if stacked else arrays[stream].shape)
        shape[axes[stream]] = 1
        outs.append(jax.ShapeDtypeStruct(tuple(shape), LOW))
        specs.append(pl.BlockSpec(tuple(shape[:-1]) + (tile,), column_block(len(shape))))
    got = pl.pallas_call(
        functools.partial(split_kernel, axes, stacked),
        grid=(columns // tile,),
        out_shape=tuple(outs * 2),
        in_specs=[
            pl.BlockSpec(leading(array, arrays[i % 2]) + (tile,), column_block(array.ndim))
            for i, array in enumerate(arrays)
        ],
        out_specs=tuple(specs * 2),
        compiler_params=pltpu.CompilerParams(vmem_limit_bytes=40 << 20),
        cost_estimate=pl.CostEstimate(
            flops=0, bytes_accessed=3 * sum(a.size for a in arrays), transcendentals=0
        ),
        name="split",
    )(*arrays)
    return got[:2], got[2:]


def leading(array, like):
    if array.ndim >= like.ndim:
        return array.shape[:-1]
    return (like.size // (like.shape[-1] * like.shape[-2]), array.shape[-2])


def split_both_kernel(up_axes, q_axes, *refs):
    ups, qs, up_kept, q_kept, messages = refs[:4], refs[4:6], refs[6:8], refs[8:10], refs[10:]
    for stream, message in enumerate(messages):
        other = q_axes.index(up_axes[stream])
        blocks = message.shape[0] - 1
        for side in (1, 0):
            at = [slice(None)] * len(up_kept[0].shape)
            at[up_axes[stream]] = slice(side, side + 1)
            up_part = added(ups[stream::2], tuple(at))
            q_part = added(qs, (other,) + tuple(at))
            if side:
                message[:blocks] = q_part.reshape((blocks,) + message.shape[1:])
                message[blocks:] = up_part.reshape((1,) + message.shape[1:])
            else:
                up_kept[stream][...] = up_part
                q_kept[other][...] = q_part


def split_both(ups, qs, up_axes, q_axes):
    columns = ups[0].shape[-1]
    tile = min(TILE, columns)
    kept = []
    for arrays, axes in ((ups, up_axes), ((qs[0][0], qs[0][1]), q_axes)):
        for stream in range(2):
            shape = list(arrays[stream].shape)
            shape[axes[stream]] = 1
            kept.append(tuple(shape))
    rows = ups[0].shape[-2]
    blocks = 1 + qs[0].size // (4 * rows * columns)
    shapes = kept + [(blocks, rows, columns)] * 2

    def tiled(shape):
        return pl.BlockSpec(tuple(shape[:-1]) + (tile,), column_block(len(shape)))

    arrays = (*ups, *qs)
    got = pl.pallas_call(
        functools.partial(split_both_kernel, up_axes, q_axes),
        grid=(columns // tile,),
        out_shape=tuple(jax.ShapeDtypeStruct(shape, LOW) for shape in shapes),
        in_specs=[tiled(array.shape) for array in arrays],
        out_specs=tuple(tiled(shape) for shape in shapes),
        compiler_params=pltpu.CompilerParams(vmem_limit_bytes=40 << 20),
        cost_estimate=pl.CostEstimate(
            flops=0, bytes_accessed=3 * sum(a.size for a in arrays), transcendentals=0
        ),
        name="split_both",
    )(*arrays)
    return got[:2], got[2:4], got[4:]


def column_block(rank):
    return lambda i: (0,) * (rank - 1) + (i,)


def pieces_kernel(parts, *refs):
    ins, outs = refs[:4], refs[4:]
    count = len(outs)
    width = outs[0].shape[1] // (2 * parts)
    flat = [ref.at[(ref.shape[0] - 1,) + (0,) * (len(ref.shape) - 3)] for ref in ins]
    for k in reversed(range(count)):
        for stream in range(2):
            for i in range(parts):
                source = (i * count + k) * width
                target = (stream * parts + i) * width
                outs[k][:, target : target + width] = added(
                    flat[stream::2], (slice(None), slice(source, source + width))
                )


def to_pieces(kept, arrived, parts, count):
    rows, columns = kept[0].shape[-2:]
    out = jax.ShapeDtypeStruct((rows, 2 * columns // count), LOW)
    return small_kernel(
        functools.partial(pieces_kernel, parts), (out,) * count, *kept, *arrived, name="pieces"
    )


def total_of(addends):
    total = addends[0].astype(FULL)
    for array in addends[1:]:
        total = total + array.astype(FULL)
    return total.astype(LOW)


def after(values, *others):
    return lax.optimization_barrier((values, others))[0]


class Line:
    def __init__(self):
        self.last = None

    def wait(self, *arrays):
        self.last = (self.last, arrays)

    def __call__(self, kernel, *arrays, **rest):
        if self.last is not None:
            arrays = after(arrays, self.last)
        out = kernel(*arrays, **rest)
        leaves = jax.tree.leaves(out)
        self.last = min(leaves, key=lambda leaf: leaf.size)
        return out


def shards(
    mesh,
    tokens,
    lengths,
    routes,
    w_query,
    w_key,
    w_value,
    w_out,
    w_up,
    w_down,
    gain_attn,
    gain_mlp,
    w_router,
    cotangent,
):
    moves = Exchange(mesh)
    device = lax.axis_index("batch")
    column = lax.axis_index("tensor")
    seq_count, capacity = routes.shape
    features = tokens.shape[1]
    tokens = tokens.reshape(seq_count, -1, features)
    cotangent = cotangent.reshape(tokens.shape)

    repeats = max(1, moves.tensor // seq_count)
    local_count = max(1, seq_count // moves.tensor)
    first = column // repeats if repeats > 1 else column * local_count
    order = (first + jnp.arange(local_count)).astype(jnp.int32)
    counts_once = (column % repeats) == 0

    def once(values):
        return jnp.where(counts_once, values, jnp.zeros_like(values)) if repeats > 1 else values

    own = features // moves.batch
    place_block = jnp.asarray(moves.block_order(), jnp.int32)
    source = ((place_block ^ device)[:, None] * own + jnp.arange(own, dtype=jnp.int32)).reshape(-1)
    turn = (jnp.arange(features, dtype=jnp.int32)[:, None] == source[None, :]).astype(LOW)

    wide = w_query.shape[1]
    steps = len(moves.chips)
    shard_q = jnp.concatenate(
        [w_query.astype(LOW), w_key.astype(LOW), w_value.astype(LOW), w_out.astype(LOW).T], axis=1
    )
    shard_u = w_up.astype(LOW)
    shard_d = w_down.astype(LOW).T

    def ring(array, hops):
        pieces = [array]
        for _ in range(hops):
            pieces.append(moves.shift(pieces[-1], 1))
        return pieces

    hops = moves.tensor - 1
    line = Line()
    rows_total = local_count * capacity
    live_count = lax.dynamic_slice_in_dim(lengths, first, local_count) // 8

    def flat(array):
        return array.reshape(rows_total, features)

    def named(name, function, *arrays):
        with jax.named_scope(name):
            return function(*arrays)

    def axes_of(step):
        return tuple(moves.axis(stream, step) for stream in range(2))

    def gather(name, pair, step):
        arrived = named(name, moves.swap_step, pair, step)
        last = step == steps - 1
        return lambda: line(lambda *a: join(a[:2], a[2:], axes_of(step), last), *pair, *arrived)

    def whole(name, stacked):
        own_side = stacked.reshape(2, features // 2, stacked.shape[-1])
        return own_side, named(name, moves.swap, own_side, moves.core)

    def first_step(name, shard):
        half = shard.shape[1] // 2
        arrived = named(name, moves.swap_step, [shard[:, :half], shard[:, half:]], 0)
        return jnp.concatenate([shard, jnp.concatenate(arrived, axis=1)], axis=0)

    def doubled(pieces, parts):
        got = line(lambda *a: to_streams(a, parts, steps), *pieces)
        pair = []
        for stream, array in enumerate(got):
            lead = [1] * steps
            lead[moves.axis(stream, 0)] = 2
            pair.append(array.reshape(tuple(lead) + (array.shape[-2] // 2, array.shape[-1])))
        return pair

    def wide_open(array):
        return once(array).reshape((2,) + (2,) * steps + (own, array.shape[-1]))

    def split_step(arrays, step, stacked):
        return split(arrays, axes_of(step), stacked)

    def together(*values):
        return lax.optimization_barrier(values)

    def end_to_end(pieces):
        kept = pieces[::repeats] if repeats > 1 else pieces
        return jnp.concatenate(
            [piece.reshape(local_count, capacity, features) for piece in kept], axis=0
        )

    def place_all(values, table):
        owners = ((column - jnp.arange(0, moves.tensor, repeats)) % moves.tensor).astype(jnp.int32)
        if repeats > 1:
            places = owners // repeats
        else:
            places = (owners[:, None] * local_count + jnp.arange(local_count)).reshape(-1)
        return place_rows(table, values, routes, places.astype(jnp.int32)).reshape(-1, features)

    ahead = moves.tensor // 2

    def out_both(name, array):
        with jax.named_scope("z_" + name):
            onward = [array, moves.shift(array, 1)]
            behind = [array]
            for _ in range(moves.tensor - 1 - ahead):
                behind.append(moves.shift(behind[-1], -1))
        return onward, behind[:0:-1]

    def out_on(name, onward, behind):
        onward = list(onward)
        with jax.named_scope("z_" + name):
            for _ in range(ahead - 1):
                onward.append(moves.shift(onward[-1], 1))
        return onward + list(behind)

    def sum_ahead(name, pieces):
        with jax.named_scope("z_" + name):
            fore = pieces[ahead + 1] if ahead + 1 < moves.tensor else jnp.zeros_like(pieces[0])
            for piece in pieces[ahead + 2 :]:
                fore = total_of([piece, moves.shift(fore, 1)])
            return moves.shift(fore, 1) if ahead + 1 < moves.tensor else fore

    def sum_back(name, pieces):
        with jax.named_scope("z_" + name):
            back = None
            for piece in pieces[ahead:1:-1]:
                back = moves.shift(piece if back is None else total_of([piece, back]), -1)
        return pieces[1] if back is None else total_of([pieces[1], back])

    def sum_both(name, pieces):
        return sum_ahead(name, pieces), sum_back(name, pieces)

    def sum_on(name, back):
        with jax.named_scope("z_" + name):
            return moves.shift(back, -1)

    both_q = out_both("q", shard_q)
    routed, cot_routed = pick_rows(tokens, cotangent, routes, order, local_count, turn)
    line.last = cot_routed
    both_q = after(both_q, cot_routed)
    pieces_q = out_on("q", *both_q)
    routed, cot_routed = flat(routed), flat(cot_routed)
    wide_d = first_step("out0_d", after(shard_d, shard_q))
    small = after(jnp.stack([gain_attn, gain_mlp, w_router]).astype(LOW), pieces_q)
    small = named("small", moves.gather_small, small).astype(FULL)
    pieces_q = after(pieces_q, wide_d)
    pair_q = line(lambda *a: to_streams(a, 2, steps), *pieces_q)
    both_u = out_both("u", after(shard_u, pieces_q))
    pieces_u = out_on("u", *both_u)
    line.wait(both_u, small)
    for step in range(steps - 1):
        pair_q = gather(f"out{step}_q", pair_q, step)()
    joined_q = gather("last_q", pair_q, steps - 1)
    pair_u = line(lambda *a: to_streams(a, 1, steps), *pieces_u)
    joined_u = gather("out0_u", pair_u, 0)
    pieces_d = named("z_d", ring, after(wide_d, pieces_u), hops)
    line.wait(pieces_d[1])
    attn_weights = whole("core_q", joined_q())
    line.wait(pieces_d[2 % moves.tensor])
    for step in range(1, steps):
        joined_u = gather(f"out{step}_u", joined_u(), step)
    attn_in, qkv, heads_out, attn_out, mlp_in, d_mlp_out = line(
        lambda *a: attend(*a[:4], a[4:], capacity), live_count, routed, cot_routed, small, *attn_weights
    )
    pair_d = doubled(pieces_d, 1)
    for step in range(1, steps - 1):
        pair_d = gather(f"out{step}_d", pair_d, step)()
    joined_d = gather("last_d", pair_d, steps - 1)
    ups = whole("core_u", joined_u())
    pre, hidden, dn_kept, dn_sent = line(
        lambda *a: up_layer(*a[:2], a[2:]), mlp_in, d_mlp_out, *ups
    )
    joined_d = joined_d()

    joined_d, dn_kept, dn_sent = together(joined_d, dn_kept, dn_sent)
    dn_arrived = named("core_dn", moves.swap, once(dn_sent), moves.core)
    downs = whole("core_d", joined_d)
    dn = (wide_open(dn_kept), wide_open(dn_arrived))

    last = steps - 1
    dn_kept, dn_sent = split_step(dn, last, True)
    dn_sent, *rest = after((dn_sent, mlp_in, pre, hidden), downs)
    dn_sent, rest = together(dn_sent, rest)
    dn_arrived = named("back_dn", moves.swap_step, dn_sent, last)
    update, d_mlp_in, dot, up_kept, up_sent = down_layer(
        live_count, routed, cot_routed, small, turn, attn_out, rest[0], d_mlp_out, ups, downs, *rest[1:], capacity
    )
    dn = (*dn_kept, *dn_arrived)
    for step in reversed(range(1, last)):
        dn_kept, dn_sent = split_step(dn, step, False)
        dn = (*dn_kept, *named("back_dn", moves.swap_step, dn_sent, step))

    def halve_small(array, bit):
        mine = array.shape[1] // 2
        with jax.named_scope("small"):
            return array[:, :mine] + moves.swap(array[:, mine:], bit)

    def spread_small(array, bit):
        with jax.named_scope("small"):
            pairs = [(i, i ^ bit) for i in range(moves.tensor)]
            return array + lax.ppermute(array, "tensor", pairs)

    def from_behind(name, rows):
        pieces = [rows]
        with jax.named_scope("z_" + name):
            for _ in range(moves.tensor - 1 - ahead):
                pieces.append(moves.shift(pieces[-1], -1))
        return pieces[:0:-1]

    dn, update, d_mlp_in, dot, up_kept, up_sent = together(dn, update, d_mlp_in, dot, up_kept, up_sent)
    up_arrived = named("core_up", moves.swap, once(up_sent), moves.core)
    dn_kept, dn_sent = split_step(dn, 0, False)
    dn = (*dn_kept, *named("back0_dn", moves.swap_step, dn_sent, 0))
    with jax.named_scope("z_update"):
        next_update = moves.shift(update, 1)
    behind_update = from_behind("update", update)
    d_routed, d_attn_out, d_qkv, small_grads = attend_back(
        live_count, routed, cot_routed, small, turn, attn_out, d_mlp_in, dot, qkv, attn_weights, capacity
    )
    q_kept, q_sent = attend_grads(attn_in, d_attn_out, heads_out, d_qkv)

    up_kept, up_arrived, dn, update, next_update, behind_update, d_routed, small_grads, q_kept, q_sent = together(
        up_kept, up_arrived, dn, update, next_update, behind_update, d_routed, small_grads, q_kept, q_sent
    )
    up_kept, up_sent = split_step((wide_open(up_kept), wide_open(up_arrived)), last, True)
    up = (*up_kept, *named("back1_up", moves.swap_step, up_sent, last))
    q_arrived = named("core_q", moves.swap, once(q_sent), moves.core)
    updates = out_on("update", (update, next_update), behind_update)
    with jax.named_scope("z_routed"):
        next_routed = moves.shift(d_routed, 1)
    dn_pieces = to_pieces(dn[:2], dn[2:], 1, moves.tensor)
    small_grads = once(small_grads)
    for step in reversed(range(1, last)):
        up_kept, up_sent = split_step(up, step, False)
        up = (*up_kept, *named("back_up", moves.swap_step, up_sent, step))

    up, q_kept, q_arrived, updates, d_routed, next_routed, dn_pieces, small_grads = together(
        up, q_kept, q_arrived, updates, d_routed, next_routed, dn_pieces, small_grads
    )
    ends = axes_of(0)
    up_kept, q_kept, messages = split_both(
        up, (wide_open(q_kept), wide_open(q_arrived)), ends, axes_of(last)
    )
    with jax.named_scope("back_both"):
        messages = [moves.swap(part, moves.chips[axis]) for part, axis in zip(messages, ends)]
    up = (*up_kept, *messages)
    q = (*q_kept, *reversed(messages))
    d_routeds = out_on("routed", (d_routed, next_routed), ())
    output = place_all(end_to_end(updates), tokens)
    behind_routed = from_behind("routed", d_routed)
    back_dn = sum_back("dn", dn_pieces)
    for step in reversed(range(1, last)):
        q_kept, q_sent = split_step(q, step, False)
        q = (*q_kept, *named("back_q", moves.swap_step, q_sent, step))

    q, up, d_routeds, behind_routed, output, small_grads, dn_pieces, back_dn = together(
        q, up, d_routeds, behind_routed, output, small_grads, dn_pieces, back_dn
    )
    q_kept, q_sent = split_step(q, 0, False)
    q = (*q_kept, *named("back0_q", moves.swap_step, q_sent, 0))
    fore_dn = sum_ahead("dn", dn_pieces)
    last_dn = sum_on("dn", back_dn)
    up_pieces = to_pieces(up[:2], up[2:], 1, moves.tensor)
    back_up = sum_back("up", up_pieces)

    routed_rows = end_to_end(list(d_routeds) + list(behind_routed))
    small_grads = halve_small(small_grads, moves.core)

    q, fore_dn, last_dn, up_pieces, back_up, small_grads, routed_rows = together(
        q, fore_dn, last_dn, up_pieces, back_up, small_grads, routed_rows
    )
    q_pieces = to_pieces(q[:2], q[2:], 2, moves.tensor)
    both_q = sum_both("q", q_pieces)
    last_up = sum_on("up", back_up)
    fore_up = sum_ahead("up", up_pieces)
    grad_tokens = place_all(routed_rows, cotangent)
    for bit in moves.chips:
        small_grads = halve_small(small_grads, bit)
    small_grads = spread_small(small_grads, 1)

    both_q, last_up, fore_up, grad_tokens, small_grads = together(
        both_q, last_up, fore_up, grad_tokens, small_grads
    )
    last_q = sum_on("q", both_q[1])
    bit = 2
    while bit < moves.tensor:
        small_grads = spread_small(small_grads, bit)
        bit *= 2
    grad_d = total_of([dn_pieces[0], fore_dn, last_dn])
    grad_q = total_of([q_pieces[0], both_q[0], last_q])
    grad_u = total_of([up_pieces[0], fore_up, last_up])

    return (
        output,
        grad_tokens,
        grad_q[:, :wide].astype(FULL),
        grad_q[:, wide : 2 * wide].astype(FULL),
        grad_q[:, 2 * wide : 3 * wide].astype(FULL),
        grad_q[:, 3 * wide :].T.astype(FULL),
        grad_u.astype(FULL),
        grad_d.T.astype(FULL),
        small_grads[0],
        small_grads[1],
        small_grads[2],
    )


def solution(mesh):
    in_specs = (
        P("batch", None),
        P("batch"),
        P("batch", None),
        P("batch", "tensor"),
        P("batch", "tensor"),
        P("batch", "tensor"),
        P("tensor", "batch"),
        P("batch", "tensor"),
        P("tensor", "batch"),
        P("batch"),
        P("batch"),
        P("batch"),
        P("batch", None),
    )
    out_specs = (
        P("batch", None),
        P("batch", None),
        P("batch", "tensor"),
        P("batch", "tensor"),
        P("batch", "tensor"),
        P("tensor", "batch"),
        P("batch", "tensor"),
        P("tensor", "batch"),
        P("batch"),
        P("batch"),
        P("batch"),
    )
    return jax.shard_map(
        functools.partial(shards, mesh),
        mesh=mesh,
        in_specs=in_specs,
        out_specs=out_specs,
        check_vma=False,
    )
```

```python
import functools

import jax
import jax.numpy as jnp
from jax import lax
from jax.experimental import pallas as pl
from jax.experimental.pallas import tpu as pltpu
from jax.sharding import PartitionSpec as P

HEAD_DIM = 64
SLOT_BLOCK = 512
PLACE_BLOCK = 2048
EPSILON = 1e-06


CURVE = 0.7978845608028654
CUBIC = 0.044715


def gelu_tanh(values):
    return 0.5 * values * (1.0 + jnp.tanh(CURVE * (values + CUBIC * values * values * values)))


def gelu_slope(values):
    square = values * values
    bend = jnp.tanh(CURVE * (values + CUBIC * values * square))
    inner = CURVE * (1.0 + 3.0 * CUBIC * square)
    return 0.5 * (1.0 + bend) + 0.5 * values * (1.0 - bend * bend) * inner


def product(left, right):
    return jnp.dot(left, right, preferred_element_type=jnp.float32)


def contract_rows(left, right):
    return lax.dot_general(
        left, right, (((0,), (0,)), ((), ())), preferred_element_type=jnp.float32
    )


def times_transposed(left, right):
    return lax.dot_general(
        left, right, (((1,), (1,)), ((), ())), preferred_element_type=jnp.float32
    )


def norm_backward(d_normed_in, normed, inverse, gain_vec):
    d_scaled = d_normed_in * gain_vec
    d_input = inverse * (d_scaled - normed * jnp.mean(d_scaled * normed, axis=-1, keepdims=True))
    return (d_input, jnp.sum(d_normed_in * normed, axis=0, keepdims=True))


def norm_forward(values):
    inverse = lax.rsqrt(jnp.mean(values * values, axis=-1, keepdims=True) + EPSILON)
    return (values * inverse, inverse)


LOW = jnp.bfloat16
FULL = jnp.float32


def pick_kernel(order_ref, routes_ref, turn_ref, tokens_ref, cot_ref, routed_ref, cot_routed_ref, total, cot_total):
    block = pl.program_id(1)
    capacity = routes_ref.shape[1]
    slots = tokens_ref.shape[1]
    column = lax.broadcasted_iota(jnp.int32, (capacity, slots), 1) + block * slots
    chooser = (routes_ref[0] == column).astype(LOW)
    part = product(chooser, tokens_ref[0])
    cot_part = product(chooser, cot_ref[0])

    @pl.when(block == 0)
    def _():
        total[...] = part
        cot_total[...] = cot_part

    @pl.when(block > 0)
    def _():
        total[...] += part
        cot_total[...] += cot_part

    @pl.when(block == pl.num_programs(1) - 1)
    def _():
        routed_ref[0] = product(total[...].astype(LOW), turn_ref[...]).astype(LOW)
        cot_routed_ref[0] = product(cot_total[...].astype(LOW), turn_ref[...]).astype(LOW)


def pick_rows(tokens, cotangent, routes, order, count, turn):
    seq_count, slots, features = tokens.shape
    capacity = routes.shape[1]
    per_block = min(SLOT_BLOCK, slots)
    table = pl.BlockSpec((1, per_block, features), lambda i, j, order: (order[i], j, 0))
    picked = pl.BlockSpec((1, capacity, features), lambda i, j, order: (i, 0, 0))
    shape = jax.ShapeDtypeStruct((count, capacity, features), LOW)
    return pl.pallas_call(
        pick_kernel,
        out_shape=(shape, shape),
        grid_spec=pltpu.PrefetchScalarGridSpec(
            num_scalar_prefetch=1,
            grid=(count, slots // per_block),
            in_specs=[
                pl.BlockSpec((1, capacity, 1), lambda i, j, order: (order[i], 0, 0)),
                pl.BlockSpec((features, features), lambda i, j, order: (0, 0)),
                table,
                table,
            ],
            out_specs=[picked, picked],
            scratch_shapes=[pltpu.VMEM((capacity, features), FULL)] * 2,
        ),
        compiler_params=pltpu.CompilerParams(vmem_limit_bytes=48 << 20),
        cost_estimate=pl.CostEstimate(
            flops=4 * count * capacity * slots * features,
            bytes_accessed=4 * count * slots * features,
            transcendentals=0,
        ),
        name="pick_rows",
    )(order, routes[:, :, None], turn, tokens, cotangent)


def place_kernel(order_ref, routes_ref, table_ref, values_ref, out_ref):
    block = pl.program_id(1)
    slots = table_ref.shape[1]
    capacity = routes_ref.shape[2]
    row = lax.broadcasted_iota(jnp.int32, (slots, capacity), 0) + block * slots
    chooser = (routes_ref[0] == row).astype(LOW)
    placed = product(chooser, values_ref[0])
    out_ref[0] = (table_ref[0].astype(FULL) + placed).astype(LOW)


def place_rows(table, values, routes, order):
    seq_count, slots, features = table.shape
    capacity = routes.shape[1]
    per_block = min(PLACE_BLOCK, slots)
    tall = pl.BlockSpec((1, per_block, features), lambda i, j, order: (order[i], j, 0))
    return pl.pallas_call(
        place_kernel,
        out_shape=jax.ShapeDtypeStruct(table.shape, table.dtype),
        grid_spec=pltpu.PrefetchScalarGridSpec(
            num_scalar_prefetch=1,
            grid=(seq_count, slots // per_block),
            in_specs=[
                pl.BlockSpec((1, 1, capacity), lambda i, j, order: (order[i], 0, 0)),
                tall,
                pl.BlockSpec((1, capacity, features), lambda i, j, order: (i, 0, 0)),
            ],
            out_specs=tall,
        ),
        compiler_params=pltpu.CompilerParams(vmem_limit_bytes=56 << 20),
        cost_estimate=pl.CostEstimate(
            flops=2 * seq_count * capacity * slots * features,
            bytes_accessed=4 * seq_count * slots * features,
            transcendentals=0,
        ),
        name="place_rows",
    )(order, routes[:, None, :], table, values)


def gates(routed, router_vec, live_ref, capacity):
    rows = routed.shape[0]
    score = jnp.sum(routed * router_vec, axis=-1, keepdims=True)
    gate_prob = 1.0 / (1.0 + jnp.exp(-score))
    live = [
        lax.broadcasted_iota(jnp.int32, (capacity, 1), 0) < live_ref[seq]
        for seq in range(rows // capacity)
    ]
    live = live[0] if len(live) == 1 else jnp.concatenate(live, axis=0)
    return gate_prob, jnp.where(live, gate_prob, 0.0)


def probabilities(queries, keys_all, live_count, scale_qk):
    scores = times_transposed(queries, keys_all) * scale_qk
    row = lax.broadcasted_iota(jnp.int32, scores.shape, 0)
    column = lax.broadcasted_iota(jnp.int32, scores.shape, 1)
    masked = jnp.where((column <= row) & (column < live_count), scores, -1e30)
    exp_scores = jnp.exp(masked - jnp.max(masked, axis=-1, keepdims=True))
    return exp_scores / jnp.sum(exp_scores, axis=-1, keepdims=True)


def split_heads(pair):
    owner = lax.broadcasted_iota(jnp.int32, pair.shape, 1) // HEAD_DIM
    return [jnp.where(owner == i, pair, jnp.zeros_like(pair)) for i in range(pair.shape[1] // HEAD_DIM)]


def attend_kernel(
    capacity, live_ref, routed_ref, cot_ref, small_ref, own, other,
    attn_in_ref, qkv_ref, heads_ref, attn_out_ref, mlp_in_ref, d_mlp_out_ref,
):
    routed = routed_ref[...].astype(FULL)
    rows, features = routed.shape
    half = features // 2
    wide = qkv_ref.shape[1] // 3
    _, gate_live = gates(routed, small_ref[2:3], live_ref, capacity)
    d_mlp_out_ref[...] = (gate_live * cot_ref[...].astype(FULL)).astype(LOW)
    normed, _ = norm_forward(routed)
    attn_in = (normed * small_ref[0:1]).astype(LOW)
    attn_in_ref[...] = attn_in
    left, right = attn_in[:, :half], attn_in[:, half:]
    qkv_ref[:, : 2 * wide] = (product(left, own[0]) + product(right, other[0])).astype(LOW)
    qkv_ref[:, 2 * wide :] = (
        product(left, own[1, :, :wide]) + product(right, other[1, :, :wide])
    ).astype(LOW)
    tile = 2 * HEAD_DIM
    for seq in range(rows // capacity):
        at = slice(seq * capacity, (seq + 1) * capacity)
        for start in range(0, wide, tile):
            keys_all = qkv_ref[at, wide + start : wide + start + tile]
            queries = split_heads(qkv_ref[at, start : start + tile])
            vals = split_heads(qkv_ref[at, 2 * wide + start : 2 * wide + start + tile])
            total = None
            for query, val in zip(queries, vals):
                probs = probabilities(query, keys_all, live_ref[seq], HEAD_DIM ** (-0.5))
                part = product(probs.astype(LOW), val)
                total = part if total is None else total + part
            heads_ref[at, start : start + tile] = total.astype(LOW)
    heads_out = heads_ref[...]
    attn_out_ref[:, :half] = times_transposed(heads_out, own[1, :, wide:])
    attn_out_ref[:, half:] = times_transposed(heads_out, other[1, :, wide:])
    normed_two, _ = norm_forward(routed + attn_out_ref[...])
    mlp_in_ref[...] = (normed_two * small_ref[1:2]).astype(LOW)


def whole_specs(count):
    return [pl.BlockSpec(memory_space=pltpu.VMEM)] * count


def attend(live_count, routed, cot_routed, small, weights, capacity):
    rows, features = routed.shape
    wide = weights[0].shape[2] // 2
    return pl.pallas_call(
        functools.partial(attend_kernel, capacity),
        out_shape=(
            jax.ShapeDtypeStruct((rows, features), LOW),
            jax.ShapeDtypeStruct((rows, 3 * wide), LOW),
            jax.ShapeDtypeStruct((rows, wide), LOW),
            jax.ShapeDtypeStruct((rows, features), FULL),
            jax.ShapeDtypeStruct((rows, features), LOW),
            jax.ShapeDtypeStruct((rows, features), LOW),
        ),
        in_specs=[pl.BlockSpec(memory_space=pltpu.SMEM)] + whole_specs(5),
        out_specs=tuple(whole_specs(6)),
        compiler_params=pltpu.CompilerParams(vmem_limit_bytes=56 << 20),
        cost_estimate=pl.CostEstimate(
            flops=8 * rows * features * wide + 4 * rows * capacity * wide,
            bytes_accessed=8 * features * wide + 14 * rows * features,
            transcendentals=rows * capacity * wide // HEAD_DIM,
        ),
        name="attend",
    )(live_count, routed, cot_routed, small, *weights)


def up_kernel(mlp_in_ref, d_mlp_out_ref, own, other, pre_ref, hidden_ref, kept_ref, sent_ref):
    mlp_in = mlp_in_ref[...]
    d_mlp_out = d_mlp_out_ref[...]
    half = mlp_in.shape[1] // 2
    for stream in range(2):
        pre = product(mlp_in[:, :half], own[stream]) + product(mlp_in[:, half:], other[stream])
        hidden = gelu_tanh(pre).astype(LOW)
        pre_ref[stream] = pre
        hidden_ref[stream] = hidden
        sent_ref[stream] = contract_rows(d_mlp_out[:, half:], hidden).astype(LOW)
        kept_ref[stream] = contract_rows(d_mlp_out[:, :half], hidden).astype(LOW)


TILE = 512


def up_layer(mlp_in, d_mlp_out, ups):
    rows, features = mlp_in.shape
    streams, half, width = ups[0].shape
    tile = min(TILE, width)
    whole = pl.BlockSpec((rows, features), lambda i: (0, 0))
    weight = pl.BlockSpec((streams, half, tile), lambda i: (0, 0, i))
    tall = pl.BlockSpec((streams, rows, tile), lambda i: (0, 0, i))
    return pl.pallas_call(
        up_kernel,
        grid=(width // tile,),
        out_shape=(
            jax.ShapeDtypeStruct((streams, rows, width), FULL),
            jax.ShapeDtypeStruct((streams, rows, width), LOW),
            jax.ShapeDtypeStruct(ups[0].shape, LOW),
            jax.ShapeDtypeStruct(ups[0].shape, LOW),
        ),
        in_specs=[whole, whole, weight, weight],
        out_specs=(tall, tall, weight, weight),
        compiler_params=pltpu.CompilerParams(vmem_limit_bytes=56 << 20),
        cost_estimate=pl.CostEstimate(
            flops=8 * rows * features * width,
            bytes_accessed=8 * features * width + 12 * rows * width,
            transcendentals=2 * rows * width,
        ),
        name="up_layer",
    )(mlp_in, d_mlp_out, *ups)


def down_kernel(
    capacity, live_ref, routed_ref, cot_ref, small_ref, turn_ref, attn_out_ref, mlp_in_ref, d_mlp_out_ref,
    up_own, up_other, down_own, down_other, pre_ref, hidden_ref,
    update_ref, d_mlp_in_ref, dot_ref, kept_ref, sent_ref, mlp_out,
):
    mlp_in = mlp_in_ref[...]
    d_mlp_out = d_mlp_out_ref[...]
    half = mlp_in.shape[1] // 2

    @pl.when(pl.program_id(0) == 0)
    def _():
        mlp_out[...] = jnp.zeros_like(mlp_out)
        d_mlp_in_ref[...] = jnp.zeros_like(d_mlp_in_ref)

    for stream in range(2):
        d_hidden = product(d_mlp_out[:, :half], down_own[stream]) + product(
            d_mlp_out[:, half:], down_other[stream]
        )
        d_pre = (d_hidden * gelu_slope(pre_ref[stream])).astype(LOW)
        sent_ref[stream] = contract_rows(mlp_in[:, half:], d_pre).astype(LOW)
        kept_ref[stream] = contract_rows(mlp_in[:, :half], d_pre).astype(LOW)
        d_mlp_in_ref[:, :half] += times_transposed(d_pre, up_own[stream])
        d_mlp_in_ref[:, half:] += times_transposed(d_pre, up_other[stream])
        hidden = hidden_ref[stream]
        mlp_out[:, :half] += times_transposed(hidden, down_own[stream])
        mlp_out[:, half:] += times_transposed(hidden, down_other[stream])

    @pl.when(pl.program_id(0) == pl.num_programs(0) - 1)
    def _():
        _, gate_live = gates(routed_ref[...].astype(FULL), small_ref[2:3], live_ref, capacity)
        branch = attn_out_ref[...] + mlp_out[...]
        update = (gate_live * branch).astype(LOW)
        update_ref[...] = times_transposed(update, turn_ref[...]).astype(LOW)
        dot_ref[...] = jnp.sum(cot_ref[...].astype(FULL) * branch, axis=-1, keepdims=True)


def down_layer(live_count, routed, cot_routed, small, turn, attn_out, mlp_in, d_mlp_out, ups, downs, pre, hidden, capacity):
    rows, features = mlp_in.shape
    streams, half, width = ups[0].shape
    tile = min(TILE, width)
    whole = pl.BlockSpec((rows, features), lambda i: (0, 0))
    weight = pl.BlockSpec((streams, half, tile), lambda i: (0, 0, i))
    tall = pl.BlockSpec((streams, rows, tile), lambda i: (0, 0, i))
    return pl.pallas_call(
        functools.partial(down_kernel, capacity),
        grid=(width // tile,),
        out_shape=(
            jax.ShapeDtypeStruct((rows, features), LOW),
            jax.ShapeDtypeStruct((rows, features), FULL),
            jax.ShapeDtypeStruct((rows, 1), FULL),
            jax.ShapeDtypeStruct(ups[0].shape, LOW),
            jax.ShapeDtypeStruct(ups[0].shape, LOW),
        ),
        in_specs=[
            pl.BlockSpec(memory_space=pltpu.SMEM),
            whole,
            whole,
            pl.BlockSpec(small.shape, lambda i: (0, 0)),
            pl.BlockSpec(turn.shape, lambda i: (0, 0)),
            whole,
            whole,
            whole,
        ]
        + [weight] * 4
        + [tall] * 2,
        out_specs=(whole, whole, pl.BlockSpec((rows, 1), lambda i: (0, 0)), weight, weight),
        scratch_shapes=[pltpu.VMEM((rows, features), FULL)],
        compiler_params=pltpu.CompilerParams(vmem_limit_bytes=56 << 20),
        cost_estimate=pl.CostEstimate(
            flops=16 * rows * features * width,
            bytes_accessed=12 * features * width + 12 * rows * width,
            transcendentals=2 * rows * width,
        ),
        name="down_layer",
    )(live_count, routed, cot_routed, small, turn, attn_out, mlp_in, d_mlp_out, *ups, *downs, pre, hidden)


def attend_back_kernel(
    capacity, live_ref, routed_ref, cot_ref, small_ref, turn_ref, attn_out_ref, d_mlp_in_ref, dot_ref, qkv_ref,
    own, other, d_routed_ref, d_attn_out_ref, d_qkv_ref, small_grads_ref, d_heads_ref,
):
    routed = routed_ref[...].astype(FULL)
    rows, features = routed.shape
    half = features // 2
    wide = qkv_ref.shape[1] // 3
    scale_qk = HEAD_DIM ** (-0.5)
    gate_prob, gate_live = gates(routed, small_ref[2:3], live_ref, capacity)
    normed_two, inverse_two = norm_forward(routed + attn_out_ref[...])
    d_middle, small_grads_ref[1:2] = norm_backward(
        d_mlp_in_ref[...], normed_two, inverse_two, small_ref[1:2]
    )
    d_attn_out = (d_middle + gate_live * cot_ref[...].astype(FULL)).astype(LOW)
    d_attn_out_ref[...] = d_attn_out
    d_heads_ref[...] = (
        product(d_attn_out[:, :half], own[1, :, wide:]) + product(d_attn_out[:, half:], other[1, :, wide:])
    ).astype(LOW)
    tile = 2 * HEAD_DIM
    for seq in range(rows // capacity):
        at = slice(seq * capacity, (seq + 1) * capacity)
        for start in range(0, wide, tile):
            query_pair = qkv_ref[at, start : start + tile]
            key_pair = qkv_ref[at, wide + start : wide + start + tile]
            val_pair = qkv_ref[at, 2 * wide + start : 2 * wide + start + tile]
            d_query, d_key, d_val = 0.0, 0.0, 0.0
            for query, key, d_head in zip(
                split_heads(query_pair), split_heads(key_pair), split_heads(d_heads_ref[at, start : start + tile])
            ):
                probs = probabilities(query, key_pair, live_ref[seq], scale_qk)
                d_val = d_val + contract_rows(probs.astype(LOW), d_head)
                d_probs = times_transposed(d_head, val_pair)
                d_scores = (
                    probs * (d_probs - jnp.sum(d_probs * probs, axis=-1, keepdims=True))
                ).astype(LOW)
                d_query = d_query + product(d_scores, key)
                d_key = d_key + contract_rows(d_scores, query)
            d_qkv_ref[at, start : start + tile] = (d_query * scale_qk).astype(LOW)
            d_qkv_ref[at, wide + start : wide + start + tile] = (d_key * scale_qk).astype(LOW)
            d_qkv_ref[at, 2 * wide + start : 2 * wide + start + tile] = d_val.astype(LOW)
    d_both = d_qkv_ref[:, : 2 * wide]
    d_vals = d_qkv_ref[:, 2 * wide :]
    d_attn_in = jnp.concatenate(
        [
            times_transposed(d_both, side[0]) + times_transposed(d_vals, side[1, :, :wide])
            for side in (own, other)
        ],
        axis=1,
    )
    normed_one, inverse_one = norm_forward(routed)
    d_from_norm, small_grads_ref[0:1] = norm_backward(d_attn_in, normed_one, inverse_one, small_ref[0:1])
    d_score = gate_live * (1.0 - gate_prob) * dot_ref[...]
    small_grads_ref[2:3] = jnp.sum(routed * d_score, axis=0, keepdims=True)
    d_routed = (d_middle + d_from_norm + d_score * small_ref[2:3]).astype(LOW)
    d_routed_ref[...] = times_transposed(d_routed, turn_ref[...]).astype(LOW)


def attend_back(live_count, routed, cot_routed, small, turn, attn_out, d_mlp_in, dot, qkv, weights, capacity):
    rows, features = routed.shape
    wide = weights[0].shape[2] // 2
    return pl.pallas_call(
        functools.partial(attend_back_kernel, capacity),
        out_shape=(
            jax.ShapeDtypeStruct((rows, features), LOW),
            jax.ShapeDtypeStruct((rows, features), LOW),
            jax.ShapeDtypeStruct((rows, 3 * wide), LOW),
            jax.ShapeDtypeStruct((3, features), FULL),
        ),
        in_specs=[pl.BlockSpec(memory_space=pltpu.SMEM)] + whole_specs(10),
        out_specs=tuple(whole_specs(4)),
        scratch_shapes=[pltpu.VMEM((rows, wide), LOW)],
        compiler_params=pltpu.CompilerParams(vmem_limit_bytes=56 << 20),
        cost_estimate=pl.CostEstimate(
            flops=8 * rows * features * wide + 10 * rows * capacity * wide,
            bytes_accessed=8 * features * wide + 14 * rows * features,
            transcendentals=rows * capacity * wide // HEAD_DIM,
        ),
        name="attend_back",
    )(live_count, routed, cot_routed, small, turn, attn_out, d_mlp_in, dot, qkv, *weights)


def grads_kernel(attn_in_ref, d_attn_out_ref, heads_ref, d_qkv_ref, kept_ref, sent_ref):
    half = attn_in_ref.shape[1] // 2
    wide = heads_ref.shape[1]
    for at, out_ref in ((slice(half, 2 * half), sent_ref), (slice(0, half), kept_ref)):
        attn_in = attn_in_ref[:, at]
        out_ref[0] = contract_rows(attn_in, d_qkv_ref[:, : 2 * wide]).astype(LOW)
        out_ref[1, :, :wide] = contract_rows(attn_in, d_qkv_ref[:, 2 * wide :]).astype(LOW)
        out_ref[1, :, wide:] = contract_rows(d_attn_out_ref[:, at], heads_ref[...]).astype(LOW)


def attend_grads(attn_in, d_attn_out, heads_out, d_qkv):
    rows, features = attn_in.shape
    wide = heads_out.shape[1]
    return pl.pallas_call(
        grads_kernel,
        out_shape=(jax.ShapeDtypeStruct((2, features // 2, 2 * wide), LOW),) * 2,
        in_specs=whole_specs(4),
        out_specs=tuple(whole_specs(2)),
        compiler_params=pltpu.CompilerParams(vmem_limit_bytes=56 << 20),
        cost_estimate=pl.CostEstimate(
            flops=8 * rows * features * wide,
            bytes_accessed=8 * features * wide + 8 * rows * features,
            transcendentals=0,
        ),
        name="attend_grads",
    )(attn_in, d_attn_out, heads_out, d_qkv)


class Exchange:
    def __init__(self, mesh):
        self.batch = mesh.shape["batch"]
        self.tensor = mesh.shape["tensor"]
        bits = []
        bit = self.batch // 2
        while bit:
            bits.append(bit)
            bit //= 2
        self.core = bits[-1]
        self.chips = bits[:-1]

    def swap(self, array, bit):
        with jax.named_scope(f"swap{bit}"):
            return lax.ppermute(array, "batch", [(i, i ^ bit) for i in range(self.batch)])

    def shift(self, array, step):
        size = self.tensor
        with jax.named_scope(f"shift{step}"):
            return lax.ppermute(array, "tensor", [(i, (i + step) % size) for i in range(size)])

    def block_order(self):
        order = [0]
        for bit in reversed([self.core] + self.chips):
            order = order + [place ^ bit for place in order]
        return order

    def gather_small(self, array):
        total = array[None]
        for bit in reversed([self.core] + self.chips):
            total = jnp.concatenate([total, self.swap(total, bit)], axis=0)
        return total.transpose(1, 0, 2).reshape(array.shape[0], -1)

    def axis(self, stream, step):
        return step if stream else len(self.chips) - 1 - step

    def swap_step(self, pair, step):
        return [self.swap(array, self.chips[self.axis(i, step)]) for i, array in enumerate(pair)]


def small_kernel(kernel, out_shape, *arrays, name):
    return pl.pallas_call(
        kernel,
        out_shape=out_shape,
        in_specs=whole_specs(len(arrays)),
        out_specs=tuple(whole_specs(len(out_shape))),
        compiler_params=pltpu.CompilerParams(vmem_limit_bytes=40 << 20),
        cost_estimate=pl.CostEstimate(
            flops=0, bytes_accessed=4 * sum(a.size for a in arrays), transcendentals=0
        ),
        name=name,
    )(*arrays)


def streams_kernel(parts, *refs):
    pieces, outs = refs[:-2], refs[-2:]
    count = len(pieces)
    width = pieces[0].shape[1] // (2 * parts)
    for stream, out_ref in enumerate(outs):
        lead = (0,) * (len(out_ref.shape) - 2)
        for i in range(parts):
            source = (stream * parts + i) * width
            for k, piece in enumerate(pieces):
                target = (i * count + k) * width
                out_ref[lead + (slice(None), slice(target, target + width))] = piece[
                    :, source : source + width
                ]


def to_streams(pieces, parts, places):
    rows, columns = pieces[0].shape
    shape = (1,) * places + (rows, columns * len(pieces) // 2)
    out = jax.ShapeDtypeStruct(shape, pieces[0].dtype)
    return small_kernel(functools.partial(streams_kernel, parts), (out, out), *pieces, name="streams")


def join_kernel(axes, stacked, *refs):
    ins, outs = refs[:4], refs[4:]
    for stream in range(2):
        for side in range(2):
            source = ins[2 * stream + side]
            at = [slice(None)] * len(source.shape)
            size = source.shape[axes[stream]]
            at[axes[stream]] = slice(side * size, (side + 1) * size)
            if stacked:
                outs[0][(stream,) + tuple(at)] = source[...]
            else:
                outs[stream][tuple(at)] = source[...]


def join(pair, arrived, axes, stacked):
    columns = pair[0].shape[-1]
    tile = min(TILE, columns)
    shapes = []
    for array, axis in zip(pair, axes):
        shape = list(array.shape)
        shape[axis] *= 2
        shapes.append(tuple(shape))
    if stacked:
        shapes = [(2,) + shapes[0]]

    def tiled(shape):
        return pl.BlockSpec(tuple(shape[:-1]) + (tile,), column_block(len(shape)))

    got = pl.pallas_call(
        functools.partial(join_kernel, axes, stacked),
        grid=(columns // tile,),
        out_shape=tuple(jax.ShapeDtypeStruct(shape, LOW) for shape in shapes),
        in_specs=[tiled(pair[i // 2].shape) for i in range(4)],
        out_specs=tuple(tiled(shape) for shape in shapes),
        compiler_params=pltpu.CompilerParams(vmem_limit_bytes=40 << 20),
        cost_estimate=pl.CostEstimate(
            flops=0, bytes_accessed=8 * sum(a.size for a in pair), transcendentals=0
        ),
        name="join",
    )(pair[0], arrived[0], pair[1], arrived[1])
    return got[0] if stacked else got


def added(refs, at):
    shape = refs[0].shape
    total = refs[0][at].astype(FULL)
    for ref in refs[1:]:
        part = ref[at] if len(ref.shape) == len(shape) else ref[...].reshape(shape)[at]
        total = total + part.astype(FULL)
    return total.astype(LOW)


def split_kernel(axes, stacked, *refs):
    ins, (kept_one, kept_two, sent_one, sent_two) = refs[:-4], refs[-4:]
    for stream, (kept_ref, sent_ref) in enumerate(((kept_one, sent_one), (kept_two, sent_two))):
        sources = ins if stacked else ins[stream::2]
        for side, out_ref in ((1, sent_ref), (0, kept_ref)):
            at = [slice(None)] * len(out_ref.shape)
            at[axes[stream]] = slice(side, side + 1)
            at = ((stream,) if stacked else ()) + tuple(at)
            out_ref[...] = added(sources, at)


def split(arrays, axes, stacked):
    full = arrays[0].shape[1:] if stacked else arrays[0].shape
    columns = full[-1]
    tile = min(TILE, columns)
    outs, specs = [], []
    for stream in range(2):
        shape = list(full if stacked else arrays[stream].shape)
        shape[axes[stream]] = 1
        outs.append(jax.ShapeDtypeStruct(tuple(shape), LOW))
        specs.append(pl.BlockSpec(tuple(shape[:-1]) + (tile,), column_block(len(shape))))
    got = pl.pallas_call(
        functools.partial(split_kernel, axes, stacked),
        grid=(columns // tile,),
        out_shape=tuple(outs * 2),
        in_specs=[
            pl.BlockSpec(leading(array, arrays[i % 2]) + (tile,), column_block(array.ndim))
            for i, array in enumerate(arrays)
        ],
        out_specs=tuple(specs * 2),
        compiler_params=pltpu.CompilerParams(vmem_limit_bytes=40 << 20),
        cost_estimate=pl.CostEstimate(
            flops=0, bytes_accessed=3 * sum(a.size for a in arrays), transcendentals=0
        ),
        name="split",
    )(*arrays)
    return got[:2], got[2:]


def leading(array, like):
    if array.ndim >= like.ndim:
        return array.shape[:-1]
    return (like.size // (like.shape[-1] * like.shape[-2]), array.shape[-2])


def split_both_kernel(up_axes, q_axes, *refs):
    ups, qs, up_kept, q_kept, messages = refs[:4], refs[4:6], refs[6:8], refs[8:10], refs[10:]
    for stream, message in enumerate(messages):
        other = q_axes.index(up_axes[stream])
        blocks = message.shape[0] - 1
        for side in (1, 0):
            at = [slice(None)] * len(up_kept[0].shape)
            at[up_axes[stream]] = slice(side, side + 1)
            up_part = added(ups[stream::2], tuple(at))
            q_part = added(qs, (other,) + tuple(at))
            if side:
                message[:blocks] = q_part.reshape((blocks,) + message.shape[1:])
                message[blocks:] = up_part.reshape((1,) + message.shape[1:])
            else:
                up_kept[stream][...] = up_part
                q_kept[other][...] = q_part


def split_both(ups, qs, up_axes, q_axes):
    columns = ups[0].shape[-1]
    tile = min(TILE, columns)
    kept = []
    for arrays, axes in ((ups, up_axes), ((qs[0][0], qs[0][1]), q_axes)):
        for stream in range(2):
            shape = list(arrays[stream].shape)
            shape[axes[stream]] = 1
            kept.append(tuple(shape))
    rows = ups[0].shape[-2]
    blocks = 1 + qs[0].size // (4 * rows * columns)
    shapes = kept + [(blocks, rows, columns)] * 2

    def tiled(shape):
        return pl.BlockSpec(tuple(shape[:-1]) + (tile,), column_block(len(shape)))

    arrays = (*ups, *qs)
    got = pl.pallas_call(
        functools.partial(split_both_kernel, up_axes, q_axes),
        grid=(columns // tile,),
        out_shape=tuple(jax.ShapeDtypeStruct(shape, LOW) for shape in shapes),
        in_specs=[tiled(array.shape) for array in arrays],
        out_specs=tuple(tiled(shape) for shape in shapes),
        compiler_params=pltpu.CompilerParams(vmem_limit_bytes=40 << 20),
        cost_estimate=pl.CostEstimate(
            flops=0, bytes_accessed=3 * sum(a.size for a in arrays), transcendentals=0
        ),
        name="split_both",
    )(*arrays)
    return got[:2], got[2:4], got[4:]


def column_block(rank):
    return lambda i: (0,) * (rank - 1) + (i,)


def pieces_kernel(parts, *refs):
    ins, outs = refs[:4], refs[4:]
    count = len(outs)
    width = outs[0].shape[1] // (2 * parts)
    flat = [ref.at[(ref.shape[0] - 1,) + (0,) * (len(ref.shape) - 3)] for ref in ins]
    for k in reversed(range(count)):
        for stream in range(2):
            for i in range(parts):
                source = (i * count + k) * width
                target = (stream * parts + i) * width
                outs[k][:, target : target + width] = added(
                    flat[stream::2], (slice(None), slice(source, source + width))
                )


def to_pieces(kept, arrived, parts, count):
    rows, columns = kept[0].shape[-2:]
    out = jax.ShapeDtypeStruct((rows, 2 * columns // count), LOW)
    return small_kernel(
        functools.partial(pieces_kernel, parts), (out,) * count, *kept, *arrived, name="pieces"
    )


def total_of(addends):
    total = addends[0].astype(FULL)
    for array in addends[1:]:
        total = total + array.astype(FULL)
    return total.astype(LOW)


def after(values, *others):
    return lax.optimization_barrier((values, others))[0]


class Line:
    def __init__(self):
        self.last = None

    def wait(self, *arrays):
        self.last = (self.last, arrays)

    def __call__(self, kernel, *arrays, **rest):
        if self.last is not None:
            arrays = after(arrays, self.last)
        out = kernel(*arrays, **rest)
        leaves = jax.tree.leaves(out)
        self.last = min(leaves, key=lambda leaf: leaf.size)
        return out


def shards(
    mesh,
    tokens,
    lengths,
    routes,
    w_query,
    w_key,
    w_value,
    w_out,
    w_up,
    w_down,
    gain_attn,
    gain_mlp,
    w_router,
    cotangent,
):
    moves = Exchange(mesh)
    device = lax.axis_index("batch")
    column = lax.axis_index("tensor")
    seq_count, capacity = routes.shape
    features = tokens.shape[1]
    tokens = tokens.reshape(seq_count, -1, features)
    cotangent = cotangent.reshape(tokens.shape)

    repeats = max(1, moves.tensor // seq_count)
    local_count = max(1, seq_count // moves.tensor)
    first = column // repeats if repeats > 1 else column * local_count
    order = (first + jnp.arange(local_count)).astype(jnp.int32)
    counts_once = (column % repeats) == 0

    def once(values):
        return jnp.where(counts_once, values, jnp.zeros_like(values)) if repeats > 1 else values

    own = features // moves.batch
    place_block = jnp.asarray(moves.block_order(), jnp.int32)
    source = ((place_block ^ device)[:, None] * own + jnp.arange(own, dtype=jnp.int32)).reshape(-1)
    turn = (jnp.arange(features, dtype=jnp.int32)[:, None] == source[None, :]).astype(LOW)

    wide = w_query.shape[1]
    steps = len(moves.chips)
    shard_q = jnp.concatenate(
        [w_query.astype(LOW), w_key.astype(LOW), w_value.astype(LOW), w_out.astype(LOW).T], axis=1
    )
    shard_u = w_up.astype(LOW)
    shard_d = w_down.astype(LOW).T

    def ring(array, hops):
        pieces = [array]
        for _ in range(hops):
            pieces.append(moves.shift(pieces[-1], 1))
        return pieces

    hops = moves.tensor - 1
    line = Line()
    rows_total = local_count * capacity
    live_count = lax.dynamic_slice_in_dim(lengths, first, local_count) // 8

    def flat(array):
        return array.reshape(rows_total, features)

    def named(name, function, *arrays):
        with jax.named_scope(name):
            return function(*arrays)

    def axes_of(step):
        return tuple(moves.axis(stream, step) for stream in range(2))

    def gather(name, pair, step):
        arrived = named(name, moves.swap_step, pair, step)
        last = step == steps - 1
        return lambda: line(lambda *a: join(a[:2], a[2:], axes_of(step), last), *pair, *arrived)

    def whole(name, stacked):
        own_side = stacked.reshape(2, features // 2, stacked.shape[-1])
        return own_side, named(name, moves.swap, own_side, moves.core)

    def first_step(name, shard):
        half = shard.shape[1] // 2
        arrived = named(name, moves.swap_step, [shard[:, :half], shard[:, half:]], 0)
        return jnp.concatenate([shard, jnp.concatenate(arrived, axis=1)], axis=0)

    def doubled(pieces, parts):
        got = line(lambda *a: to_streams(a, parts, steps), *pieces)
        pair = []
        for stream, array in enumerate(got):
            lead = [1] * steps
            lead[moves.axis(stream, 0)] = 2
            pair.append(array.reshape(tuple(lead) + (array.shape[-2] // 2, array.shape[-1])))
        return pair

    def wide_open(array):
        return once(array).reshape((2,) + (2,) * steps + (own, array.shape[-1]))

    def split_step(arrays, step, stacked):
        return split(arrays, axes_of(step), stacked)

    def together(*values):
        return lax.optimization_barrier(values)

    def end_to_end(pieces):
        kept = pieces[::repeats] if repeats > 1 else pieces
        return jnp.concatenate(
            [piece.reshape(local_count, capacity, features) for piece in kept], axis=0
        )

    def place_all(values, table):
        owners = ((column - jnp.arange(0, moves.tensor, repeats)) % moves.tensor).astype(jnp.int32)
        if repeats > 1:
            places = owners // repeats
        else:
            places = (owners[:, None] * local_count + jnp.arange(local_count)).reshape(-1)
        return place_rows(table, values, routes, places.astype(jnp.int32)).reshape(-1, features)

    ahead = moves.tensor // 2

    def out_both(name, array):
        with jax.named_scope("z_" + name):
            onward = [array, moves.shift(array, 1)]
            behind = [array]
            for _ in range(moves.tensor - 1 - ahead):
                behind.append(moves.shift(behind[-1], -1))
        return onward, behind[:0:-1]

    def out_on(name, onward, behind):
        onward = list(onward)
        with jax.named_scope("z_" + name):
            for _ in range(ahead - 1):
                onward.append(moves.shift(onward[-1], 1))
        return onward + list(behind)

    def sum_ahead(name, pieces):
        with jax.named_scope("z_" + name):
            fore = pieces[ahead + 1] if ahead + 1 < moves.tensor else jnp.zeros_like(pieces[0])
            for piece in pieces[ahead + 2 :]:
                fore = total_of([piece, moves.shift(fore, 1)])
            return moves.shift(fore, 1) if ahead + 1 < moves.tensor else fore

    def sum_back(name, pieces):
        with jax.named_scope("z_" + name):
            back = None
            for piece in pieces[ahead:1:-1]:
                back = moves.shift(piece if back is None else total_of([piece, back]), -1)
        return pieces[1] if back is None else total_of([pieces[1], back])

    def sum_both(name, pieces):
        return sum_ahead(name, pieces), sum_back(name, pieces)

    def sum_on(name, back):
        with jax.named_scope("z_" + name):
            return moves.shift(back, -1)

    both_q = out_both("q", shard_q)
    both_q, turn = after((both_q, turn))
    routed, cot_routed = pick_rows(tokens, cotangent, routes, order, local_count, turn)
    line.last = cot_routed
    pieces_q = out_on("q", *both_q)
    routed, cot_routed = flat(routed), flat(cot_routed)
    wide_d = first_step("out0_d", after(shard_d, shard_q))
    small = after(jnp.stack([gain_attn, gain_mlp, w_router]).astype(LOW), pieces_q)
    small = named("small", moves.gather_small, small).astype(FULL)
    pieces_q = after(pieces_q, wide_d)
    pair_q = line(lambda *a: to_streams(a, 2, steps), *pieces_q)
    both_u = out_both("u", after(shard_u, pieces_q))
    pieces_u = out_on("u", *both_u)
    line.wait(both_u, small)
    for step in range(steps - 1):
        pair_q = gather(f"out{step}_q", pair_q, step)()
    joined_q = gather("last_q", pair_q, steps - 1)
    pair_u = line(lambda *a: to_streams(a, 1, steps), *pieces_u)
    joined_u = gather("out0_u", pair_u, 0)
    pieces_d = named("z_d", ring, after(wide_d, pieces_u), hops)
    line.wait(pieces_d[1])
    attn_weights = whole("core_q", joined_q())
    line.wait(pieces_d[2 % moves.tensor])
    for step in range(1, steps):
        joined_u = gather(f"out{step}_u", joined_u(), step)
    attn_in, qkv, heads_out, attn_out, mlp_in, d_mlp_out = line(
        lambda *a: attend(*a[:4], a[4:], capacity), live_count, routed, cot_routed, small, *attn_weights
    )
    pair_d = doubled(pieces_d, 1)
    for step in range(1, steps - 1):
        pair_d = gather(f"out{step}_d", pair_d, step)()
    joined_d = gather("last_d", pair_d, steps - 1)
    ups = whole("core_u", joined_u())
    pre, hidden, dn_kept, dn_sent = line(
        lambda *a: up_layer(*a[:2], a[2:]), mlp_in, d_mlp_out, *ups
    )
    joined_d = joined_d()

    joined_d, dn_kept, dn_sent = together(joined_d, dn_kept, dn_sent)
    dn_arrived = named("core_dn", moves.swap, once(dn_sent), moves.core)
    downs = whole("core_d", joined_d)
    dn = (wide_open(dn_kept), wide_open(dn_arrived))

    last = steps - 1
    dn_kept, dn_sent = split_step(dn, last, True)
    dn_sent, *rest = after((dn_sent, mlp_in, pre, hidden), downs)
    dn_sent, rest = together(dn_sent, rest)
    dn_arrived = named("back_dn", moves.swap_step, dn_sent, last)
    update, d_mlp_in, dot, up_kept, up_sent = down_layer(
        live_count, routed, cot_routed, small, turn, attn_out, rest[0], d_mlp_out, ups, downs, *rest[1:], capacity
    )
    dn = (*dn_kept, *dn_arrived)
    for step in reversed(range(1, last)):
        dn_kept, dn_sent = split_step(dn, step, False)
        dn = (*dn_kept, *named("back_dn", moves.swap_step, dn_sent, step))

    def halve_small(array, bit):
        mine = array.shape[1] // 2
        with jax.named_scope("small"):
            return array[:, :mine] + moves.swap(array[:, mine:], bit)

    def spread_small(array, bit):
        with jax.named_scope("small"):
            pairs = [(i, i ^ bit) for i in range(moves.tensor)]
            return array + lax.ppermute(array, "tensor", pairs)

    def from_behind(name, rows):
        pieces = [rows]
        with jax.named_scope("z_" + name):
            for _ in range(moves.tensor - 1 - ahead):
                pieces.append(moves.shift(pieces[-1], -1))
        return pieces[:0:-1]

    dn, update, d_mlp_in, dot, up_kept, up_sent = together(dn, update, d_mlp_in, dot, up_kept, up_sent)
    up_arrived = named("core_up", moves.swap, once(up_sent), moves.core)
    dn_kept, dn_sent = split_step(dn, 0, False)
    dn = (*dn_kept, *named("back0_dn", moves.swap_step, dn_sent, 0))
    with jax.named_scope("z_update"):
        next_update = moves.shift(update, 1)
    behind_update = from_behind("update", update)
    d_routed, d_attn_out, d_qkv, small_grads = attend_back(
        live_count, routed, cot_routed, small, turn, attn_out, d_mlp_in, dot, qkv, attn_weights, capacity
    )
    q_kept, q_sent = attend_grads(attn_in, d_attn_out, heads_out, d_qkv)

    up_kept, up_arrived, dn, update, next_update, behind_update, d_routed, small_grads, q_kept, q_sent = together(
        up_kept, up_arrived, dn, update, next_update, behind_update, d_routed, small_grads, q_kept, q_sent
    )
    up_kept, up_sent = split_step((wide_open(up_kept), wide_open(up_arrived)), last, True)
    up = (*up_kept, *named("back1_up", moves.swap_step, up_sent, last))
    q_arrived = named("core_q", moves.swap, once(q_sent), moves.core)
    updates = out_on("update", (update, next_update), behind_update)
    with jax.named_scope("z_routed"):
        next_routed = moves.shift(d_routed, 1)
    dn_pieces = to_pieces(dn[:2], dn[2:], 1, moves.tensor)
    small_grads = once(small_grads)
    for step in reversed(range(1, last)):
        up_kept, up_sent = split_step(up, step, False)
        up = (*up_kept, *named("back_up", moves.swap_step, up_sent, step))

    up, q_kept, q_arrived, updates, d_routed, next_routed, dn_pieces, small_grads = together(
        up, q_kept, q_arrived, updates, d_routed, next_routed, dn_pieces, small_grads
    )
    ends = axes_of(0)
    up_kept, q_kept, messages = split_both(
        up, (wide_open(q_kept), wide_open(q_arrived)), ends, axes_of(last)
    )
    with jax.named_scope("back_both"):
        messages = [moves.swap(part, moves.chips[axis]) for part, axis in zip(messages, ends)]
    up = (*up_kept, *messages)
    q = (*q_kept, *reversed(messages))
    d_routeds = out_on("routed", (d_routed, next_routed), ())
    output = place_all(end_to_end(updates), tokens)
    behind_routed = from_behind("routed", d_routed)
    back_dn = sum_back("dn", dn_pieces)
    for step in reversed(range(1, last)):
        q_kept, q_sent = split_step(q, step, False)
        q = (*q_kept, *named("back_q", moves.swap_step, q_sent, step))

    q, up, d_routeds, behind_routed, output, small_grads, dn_pieces, back_dn = together(
        q, up, d_routeds, behind_routed, output, small_grads, dn_pieces, back_dn
    )
    q_kept, q_sent = split_step(q, 0, False)
    q = (*q_kept, *named("back0_q", moves.swap_step, q_sent, 0))
    fore_dn = sum_ahead("dn", dn_pieces)
    last_dn = sum_on("dn", back_dn)
    up_pieces = to_pieces(up[:2], up[2:], 1, moves.tensor)
    back_up = sum_back("up", up_pieces)

    routed_rows = end_to_end(list(d_routeds) + list(behind_routed))
    small_grads = halve_small(small_grads, moves.core)

    q, fore_dn, last_dn, up_pieces, back_up, small_grads, routed_rows = together(
        q, fore_dn, last_dn, up_pieces, back_up, small_grads, routed_rows
    )
    q_pieces = to_pieces(q[:2], q[2:], 2, moves.tensor)
    both_q = sum_both("q", q_pieces)
    last_up = sum_on("up", back_up)
    fore_up = sum_ahead("up", up_pieces)
    grad_tokens = place_all(routed_rows, cotangent)
    for bit in moves.chips:
        small_grads = halve_small(small_grads, bit)
    small_grads = spread_small(small_grads, 1)

    both_q, last_up, fore_up, grad_tokens, small_grads = together(
        both_q, last_up, fore_up, grad_tokens, small_grads
    )
    last_q = sum_on("q", both_q[1])
    bit = 2
    while bit < moves.tensor:
        small_grads = spread_small(small_grads, bit)
        bit *= 2
    grad_d = total_of([dn_pieces[0], fore_dn, last_dn])
    grad_q = total_of([q_pieces[0], both_q[0], last_q])
    grad_u = total_of([up_pieces[0], fore_up, last_up])

    return (
        output,
        grad_tokens,
        grad_q[:, :wide].astype(FULL),
        grad_q[:, wide : 2 * wide].astype(FULL),
        grad_q[:, 2 * wide : 3 * wide].astype(FULL),
        grad_q[:, 3 * wide :].T.astype(FULL),
        grad_u.astype(FULL),
        grad_d.T.astype(FULL),
        small_grads[0],
        small_grads[1],
        small_grads[2],
    )


def solution(mesh):
    in_specs = (
        P("batch", None),
        P("batch"),
        P("batch", None),
        P("batch", "tensor"),
        P("batch", "tensor"),
        P("batch", "tensor"),
        P("tensor", "batch"),
        P("batch", "tensor"),
        P("tensor", "batch"),
        P("batch"),
        P("batch"),
        P("batch"),
        P("batch", None),
    )
    out_specs = (
        P("batch", None),
        P("batch", None),
        P("batch", "tensor"),
        P("batch", "tensor"),
        P("batch", "tensor"),
        P("tensor", "batch"),
        P("batch", "tensor"),
        P("tensor", "batch"),
        P("batch"),
        P("batch"),
        P("batch"),
    )
    return jax.shard_map(
        functools.partial(shards, mesh),
        mesh=mesh,
        in_specs=in_specs,
        out_specs=out_specs,
        check_vma=False,
    )
```
